128 devices in a mesh: img: 4 (over y_hi, core), gz: 32 (over x, y_lo, z).
Axes of the slice: x: 4, y: 4 (y_hi: 2, y_lo: 2; y = y_hi * 2 + y_lo), z: 4, core: 2. Of those that a mesh axis runs over, the one named last changes fastest.
Arguments:
- images: float32 [16, 5, 64, 128, 128], P('img', None, 'gz'), may hold values from -12 to 12
- centre: int32 [16], P('img'), may hold values from 1 to 14, as said below
- positions: float32 [16], P('img'), may hold values from 0 to 1
Outputs:
- path: float32 [16, 5, 64, 128, 128], P('img', None, 'gz')
The draws below stay inside these ranges and needn't reach their ends.
Inputs may be any that keep to these rules, and one draw needn't show every extreme that they name: `centre`: centre_m lies within m - 1 to m + 1, clipped to 1 to 14; at the first target of each aligned block of 4 it is m - 1 and at the last m + 1, before clipping.
All inputs are finite; a program needn't handle non-finite values.
Results may differ from the reference program's by a relative error of at most 0.0003.
Values sent between devices are 32-bit elements; how exact they have to be, the bound alone decides.
No kernel may reach another device: no remote copies, remote signals or barrier semaphores. Data moves between devices by JAX's collectives and lax.ppermute only.
A program may use at most 64 MiB of HBM per device.

```python
import math
import jax
import jax.numpy as jnp
from jax import lax

NX = 128
NY = 128
IMG_DEV = 4
IMAGES = 16
NZ = 64


def draw_images(key, part):
    shape = (IMAGES, 5, NZ, NX, NY)
    noise_key = jax.random.fold_in(key, 11)
    scale_key = jax.random.fold_in(key, 12)
    base = jnp.clip(jax.random.normal(noise_key, shape, jnp.float32), -5.0, 5.0)
    per_image = jax.random.uniform(scale_key, (IMAGES,), jnp.float32, 0.7, 1.3)
    planes = jnp.arange(NZ, dtype=jnp.int32).astype(jnp.float32)
    ramp = 1.0 + 0.75 * planes / (NZ - 1)
    field = base * per_image[:, None, None, None, None] * ramp[None, None, :, None, None]
    return field


def draw_centre(key, part):
    offsets = jax.random.randint(jax.random.fold_in(key, 21), (IMAGES,), -1, 2)
    index = jnp.arange(IMAGES, dtype=jnp.int32)
    local = index % IMG_DEV
    offsets = jnp.where(local == 0, -1, jnp.where(local == IMG_DEV - 1, 1, offsets))
    return jnp.clip(index + offsets, 1, IMAGES - 2).astype(jnp.int32)


def draw_positions(key, part):
    jitter = jax.random.uniform(jax.random.fold_in(key, 31), (IMAGES,), jnp.float32, -0.3, 0.3)
    index = jnp.arange(IMAGES, dtype=jnp.int32).astype(jnp.float32)
    return jnp.clip((index + jitter) / (IMAGES - 1), 0.0, 1.0)


def setup_inputs(seed: int = 0) -> dict:
    keys = jax.random.split(jax.random.key(seed), 4)
    images = draw_images(jax.random.fold_in(keys[3], 71), 0)
    centre = draw_centre(jax.random.fold_in(keys[3], 71), 0)
    positions = draw_positions(jax.random.fold_in(keys[3], 71), 0)
    return dict(images=images, centre=centre, positions=positions)


elastic = 1.0
chiral_weight = 0.5
bulk_linear = -0.2
bulk_cubic = 0.5
bulk_quartic = 0.1
step_size = 1.0
smoothing = 64.0
epsilon = 1e-06
slot_pairs = ((0, 0), (0, 1), (0, 2), (1, 1), (1, 2))
slot_index = {(0, 0): 0, (0, 1): 1, (0, 2): 2, (1, 1): 3, (1, 2): 4}

def levi(first, middle, last):
    return (first - middle) * (middle - last) * (last - first) // 2

def tensor_entry(fields, row, column):
    if row > column:
        row, column = (column, row)
    if row == 2:
        return -(fields[0] + fields[3])
    return fields[slot_index[row, column]]

def nonlinear_drive(padded):
    fields_pad = [padded[:, slot] for slot in range(5)]
    centre_fields = [field[:, 1:-1] for field in fields_pad]
    grad_x = [(jnp.roll(field, -1, 2) - jnp.roll(field, 1, 2)) * 0.5 for field in centre_fields]
    grad_y = [(jnp.roll(field, -1, 3) - jnp.roll(field, 1, 3)) * 0.5 for field in centre_fields]
    grad_z = [(field[:, 2:] - field[:, :-2]) * 0.5 for field in fields_pad]
    gradients = (grad_x, grad_y, grad_z)
    laplace = []
    for field, inner in zip(fields_pad, centre_fields):
        value = field[:, 2:] + field[:, :-2] + jnp.roll(inner, 1, 2) + jnp.roll(inner, -1, 2)
        value = value + jnp.roll(inner, 1, 3) + jnp.roll(inner, -1, 3) - 6.0 * inner
        laplace.append(value)

    def curl_entry(row, column):
        total = jnp.zeros_like(centre_fields[0])
        for middle in range(3):
            for last in range(3):
                sign = levi(row, middle, last)
                if sign != 0:
                    total = total + sign * tensor_entry(gradients[middle], last, column)
        return total

    def square_entry(row, column):
        total = jnp.zeros_like(centre_fields[0])
        for middle in range(3):
            total = total + tensor_entry(centre_fields, row, middle) * tensor_entry(centre_fields, middle, column)
        return total
    trace = square_entry(0, 0) + square_entry(1, 1) + square_entry(2, 2)
    results = []
    for slot, pair in enumerate(slot_pairs):
        row, column = pair
        value = centre_fields[slot]
        chiral = curl_entry(row, column) + curl_entry(column, row)
        square = square_entry(row, column)
        if row == column:
            square = square - trace / 3.0
        bulk = bulk_linear * value - bulk_cubic * square + bulk_quartic * trace * value
        results.append(elastic * laplace[slot] - chiral_weight * chiral - bulk)
    return jnp.stack(results, axis=1)

def symbol_line(wave, length):
    return 2.0 - 2.0 * jnp.cos(2.0 * math.pi / length * wave.astype(jnp.float32))

def interp_matrix(arc, centre, target, columns, offset):
    nodes_index = jnp.arange(arc.shape[0], dtype=jnp.int32)

    def pick(where_at):
        return lax.optimization_barrier(jnp.sum(arc[None, :] * (nodes_index[None, :] == where_at[:, None]).astype(jnp.float32), axis=1))
    before = pick(centre - 1)
    middle = pick(centre)
    after = pick(centre + 1)
    weight_before = (target - middle) * (target - after) / ((before - middle) * (before - after))
    weight_middle = (target - before) * (target - after) / ((middle - before) * (middle - after))
    weight_after = (target - before) * (target - middle) / ((after - before) * (after - middle))
    column_index = jnp.arange(columns, dtype=jnp.int32)
    matrix = jnp.zeros((centre.shape[0], columns), jnp.float32)
    for shift_by, weight in ((-1, weight_before), (0, weight_middle), (1, weight_after)):
        spot = centre + shift_by - offset
        matrix = matrix + weight[:, None] * (column_index[None, :] == spot[:, None]).astype(jnp.float32)
    return matrix

def reference(images, centre, positions):
    symbol = symbol_line(jnp.arange(NZ, dtype=jnp.int32), NZ)[:, None, None]
    symbol = symbol + symbol_line(jnp.arange(NX, dtype=jnp.int32), NX)[None, :, None]
    symbol = symbol + symbol_line(jnp.arange(NY, dtype=jnp.int32), NY)[None, None, :]
    multiplier = step_size / (1.0 + smoothing * symbol)

    def advance(image):
        padded = jnp.concatenate([image[:, -1:], image, image[:, :1]], axis=1)
        drive = nonlinear_drive(padded[None])[0]
        spectrum = jnp.fft.fftn(drive, axes=(1, 2, 3))
        return image + jnp.real(jnp.fft.ifftn(spectrum * multiplier, axes=(1, 2, 3)))
    stepped = lax.map(advance, images)

    def gap_sum(index):
        gap = stepped[index + 1] - stepped[index]
        return jnp.sum(gap * gap)
    squares = lax.map(gap_sum, jnp.arange(IMAGES - 1, dtype=jnp.int32))
    cells = 5.0 * NZ * NX * NY
    dist = jnp.concatenate([jnp.sqrt(squares / cells + epsilon), jnp.zeros((1,), jnp.float32)])
    arc = jnp.cumsum(dist) - dist
    target = positions * arc[-1]
    matrix = interp_matrix(arc, centre, target, IMAGES, jnp.zeros((), jnp.int32))
    return jnp.einsum('mr,rqzxy->mqzxy', matrix, stepped, precision=lax.Precision.HIGHEST)
```

```python
import functools

import jax
import jax.numpy as jnp
import numpy as np
from jax import lax
from jax.experimental import pallas as pl
from jax.experimental.pallas import tpu as pltpu
from jax.sharding import PartitionSpec as P

NX = 128
NY = 128
NZ = 64
GROUPS = 32
IMAGES = 16
LOCAL = 4
CELLS = 5.0 * NZ * NX * NY
SMOOTH = 64.0
EPS = 1e-6
KEEP = 1.0 - 1.0 / SMOOTH
F32 = jnp.float32
BF16 = jnp.bfloat16


def real_basis(length):
    k = np.arange(length)[:, None]
    x = np.arange(length)[None, :]
    angle = 2.0 * np.pi * ((k * x) % length) / length
    table = np.where(k <= length // 2, np.cos(angle), np.sin(angle)) * np.sqrt(2.0 / length)
    table[0] = 1.0 / np.sqrt(length)
    table[length // 2] = np.cos(np.pi * np.arange(length)) / np.sqrt(length)
    return table


def split_np(table):
    import ml_dtypes

    high = table.astype(ml_dtypes.bfloat16)
    low = (table - high.astype(np.float64)).astype(ml_dtypes.bfloat16)
    return high, low


def right_table(table):
    high, low = split_np(table)
    row = np.concatenate([high, low], axis=1)
    return np.concatenate([row, row], axis=0)


def left_table(table):
    high, low = split_np(table)
    return np.concatenate([high, high, low], axis=1)


@functools.cache
def tables():
    basis_x = real_basis(NX)
    basis_y = real_basis(NY)
    swap = np.arange(NX).reshape(-1, 2, 4)[:, ::-1].reshape(-1)
    forward_y = right_table(basis_y.T)
    inverse_y = right_table(basis_y)
    forward_x = np.stack([left_table(basis_x), left_table(basis_x[swap])])
    inverse_x = np.stack([left_table(basis_x.T), left_table(basis_x[swap].T)])
    device = np.arange(GROUPS)[:, None]
    row = np.arange(8)[None, :] % 4
    wave_x = 8 * (device % 16) + 4 * (device // 16) + row
    lam_x = 2.0 - 2.0 * np.cos(2.0 * np.pi * wave_x / NX)
    lam_y = 2.0 - 2.0 * np.cos(2.0 * np.pi * np.arange(NY) / NY)
    lam = lam_x[:, :, None] + lam_y[None, None, :]
    excess = 0.5 / SMOOTH + 0.5 * lam
    rho = 1.0 / (1.0 + excess + np.sqrt(excess * (excess + 2.0)))
    return forward_y, inverse_y, forward_x, inverse_x, rho.astype(np.float32)


def split(value):
    high = value.astype(BF16)
    low = (value - high.astype(F32)).astype(BF16)
    return high, low


def times_right(value, table):
    high, low = split(value)
    both = jnp.dot(jnp.concatenate([high, low], axis=1), table, preferred_element_type=F32)
    return both[:, :128] + both[:, 128:]


def drive_planes(q, dz):
    q1, q2, q3, q4, q5 = q
    z12, z11m22, z23, z13 = dz

    def dx(f):
        return (pltpu.roll(f, NX - 1, 0) - pltpu.roll(f, 1, 0)) * 0.5

    def dy(f):
        return (pltpu.roll(f, NY - 1, 1) - pltpu.roll(f, 1, 1)) * 0.5

    qz = -(q1 + q4)
    s11 = q1 * q1 + q2 * q2 + q3 * q3
    s12 = q1 * q2 + q2 * q4 + q3 * q5
    s13 = q1 * q3 + q2 * q5 + q3 * qz
    s22 = q2 * q2 + q4 * q4 + q5 * q5
    s23 = q2 * q3 + q4 * q5 + q5 * qz
    s33 = q3 * q3 + q5 * q5 + qz * qz
    trace = s11 + s22 + s33
    scale = (0.2 + 1.0 / SMOOTH) - 0.1 * trace
    third = trace * (1.0 / 3.0)
    f1 = scale * q1 + 0.5 * (s11 - third) - dy(q3) + z12
    f2 = scale * q2 + 0.5 * s12 - 0.5 * (dy(q5) - dx(q3) + z11m22)
    f3 = scale * q3 + 0.5 * s13 - 0.5 * (dx(q2) + dy(qz - q1) - z23)
    f4 = scale * q4 + 0.5 * (s22 - third) - z12 + dx(q5)
    f5 = scale * q5 + 0.5 * s23 - 0.5 * (z13 + dx(q4 - qz) - dy(q2))
    return f1, f2, f3, f4, f5


def forward_kernel(img, low, high, ty, tx, out, stack, spectrum):
    for i in range(2):
        for zz in range(2):
            q = [img[i, c, zz] for c in range(5)]
            o = [img[i, c, 1 - zz] for c in range(5)]
            own = (o[1], o[0] - o[3], o[4], o[2])
            if zz == 0:
                dz = [(own[r] - low[i, r]) * 0.5 for r in range(4)]
            else:
                dz = [(high[i, r] - own[r]) * 0.5 for r in range(4)]
            for c, f in enumerate(drive_planes(q, dz)):
                h, l = split(times_right(f, ty[...]))
                cols = slice(zz * 128, zz * 128 + 128)
                stack[c, 0:128, cols] = h
                stack[c, 128:256, cols] = l
                stack[c, 256:384, cols] = h
        for c in range(5):
            spectrum[i, c] = jnp.dot(tx[i], stack[c], preferred_element_type=F32)
    first = lax.broadcasted_iota(jnp.int32, (16, 8, 128), 1) < 4
    for c in range(5):
        for zz in range(2):
            cols = slice(zz * 128, zz * 128 + 128)
            a = spectrum[0, c, :, cols].reshape(16, 8, 128)
            b = spectrum[1, c, :, cols].reshape(16, 8, 128)
            out[0:16, zz, 0, c] = jnp.where(first, a, b)
            out[16:32, zz, 0, c] = jnp.where(first, b, a)


def solve_kernel(where, f, rho_ref, out0, out1, work):
    del where
    rho = rho_ref[0]
    power = rho
    for _ in range(6):
        power = power * power
    closing = 1.0 / (1.0 - power)
    shape = (2, 5, 8, 128)
    zero = jnp.zeros(shape, F32)
    rb = jnp.broadcast_to(rho, shape)
    cb = jnp.broadcast_to(closing, shape)

    def ends(s, carry):
        v, u = carry
        for zz in range(2):
            v = f[s, zz] + rb * v
            u = f[GROUPS - 1 - s, 1 - zz] + rb * u
        return v, u

    v, u = lax.fori_loop(0, GROUPS, ends, (zero, zero))

    def up(s, v):
        for zz in range(2):
            v = f[s, zz] + rb * v
            work[s, zz] = v
        return v

    lax.fori_loop(0, GROUPS, up, v * cb)
    gain = rho * (1.0 / SMOOTH) / (1.0 - rho * rho)
    gb = jnp.broadcast_to(gain, shape)

    def down(n, u):
        s = GROUPS - 1 - n
        for zz in (1, 0):
            value = rb * u
            u = f[s, zz] + value
            result = gb * (work[s, zz] + value)
            out0[s, zz] = result[0]
            out1[s, zz] = result[1]
        return u

    lax.fori_loop(0, GROUPS, down, u * cb)


def inverse_kernel(spec, img, ty, tx, out, stack):
    first = lax.broadcasted_iota(jnp.int32, (16, 8, 128), 1) < 4
    for i in range(2):
        for c in range(5):
            for zz in range(2):
                even = spec[0:16, zz, c]
                odd = spec[16:32, zz, c]
                mine = jnp.where(first, even, odd) if i == 0 else jnp.where(first, odd, even)
                h, l = split(mine.reshape(128, 128))
                cols = slice(zz * 128, zz * 128 + 128)
                stack[c, 0:128, cols] = h
                stack[c, 128:256, cols] = l
                stack[c, 256:384, cols] = h
            both = jnp.dot(tx[i], stack[c], preferred_element_type=F32)
            for zz in range(2):
                update = times_right(both[:, zz * 128 : zz * 128 + 128], ty[...])
                out[i, c, zz] = KEEP * img[i, c, zz] + update


def gap_kernel(lower, upper, beyond, out):
    @pl.when(pl.program_id(0) == 0)
    def _():
        out[...] = jnp.zeros_like(out)

    def total(a, b):
        d = a - b
        d = (d * d).reshape(2 * 16, 8, 128)
        return jnp.sum(d, axis=0)

    chain = [lower[0, 0], lower[1, 0], upper[0, 0], upper[1, 0], beyond[0, 0]]
    for g in range(4):
        out[g] += total(chain[g + 1], chain[g])


def final_kernel(centre, positions, where, sums, below, lower, upper, above, out, weights):
    @pl.when(pl.program_id(0) == 0)
    def _():
        arc = [jnp.zeros((8, 128), F32)]
        for k in range(LOCAL):
            block = jnp.sum(sums[k * GROUPS : (k + 1) * GROUPS], axis=0)
            dist = jnp.sqrt(block * (1.0 / CELLS) + EPS)
            for g in range(4):
                if k * 4 + g < IMAGES - 1:
                    row = jnp.broadcast_to(dist[g : g + 1], (8, 128))
                    arc.append(arc[-1] + row)
        base = where[0] * LOCAL - 2
        for m in range(LOCAL):
            c = centre[m]
            tau = positions[m] * arc[-1]

            def pick(index):
                value = arc[0]
                for j in range(1, IMAGES):
                    value = jnp.where(index == j, arc[j], value)
                return value

            a, b, d = pick(c - 1), pick(c), pick(c + 1)
            w = (
                (tau - b) * (tau - d) / ((a - b) * (a - d)),
                (tau - a) * (tau - d) / ((b - a) * (b - d)),
                (tau - a) * (tau - b) / ((d - a) * (d - b)),
            )
            for r in range(5):
                spot = base + m + r
                value = jnp.zeros((8, 128), F32)
                for n in range(3):
                    value = jnp.where(c - 1 + n == spot, w[n], value)
                weights[m, r] = value

    pieces = [below[0], below[1], lower[0], lower[1], upper[0], upper[1], above[0], above[1]]
    pieces = [p.reshape(32, 8, 128) for p in pieces]
    for m in range(LOCAL):
        acc = pieces[m] * weights[m, 0][None]
        for r in range(1, 5):
            acc = acc + pieces[m + r] * weights[m, r][None]
        out[m, 0] = acc.reshape(2, 128, 128)


def whole(shape):
    return pl.BlockSpec(shape, lambda *_: (0,) * len(shape))


SMEM = pl.BlockSpec(memory_space=pltpu.SMEM)


def params(mib):
    return pltpu.CompilerParams(
        dimension_semantics=("arbitrary",), vmem_limit_bytes=mib * 1024 * 1024
    )


def forward(images, low, high, ty, tx):
    return pl.pallas_call(
        forward_kernel,
        out_shape=jax.ShapeDtypeStruct((GROUPS, 2, 2, 5, 8, 128), F32),
        grid=(2,),
        in_specs=[
            pl.BlockSpec((2, 5, 2, 128, 128), lambda p: (p, 0, 0, 0, 0)),
            pl.BlockSpec((2, 4, 128, 128), lambda p: (p, 0, 0, 0)),
            pl.BlockSpec((2, 4, 128, 128), lambda p: (p, 0, 0, 0)),
            whole((256, 256)),
            whole((2, 128, 384)),
        ],
        out_specs=pl.BlockSpec((GROUPS, 2, 1, 5, 8, 128), lambda p: (0, 0, p, 0, 0, 0)),
        scratch_shapes=[
            pltpu.VMEM((5, 384, 256), BF16),
            pltpu.VMEM((2, 5, 128, 256), F32),
        ],
        compiler_params=params(32),
        name="forward",
    )(images, low, high, ty, tx)


def solve(f, rho):
    half = jax.ShapeDtypeStruct((GROUPS, 2, 5, 8, 128), F32)
    where = lax.axis_index("gz").astype(jnp.int32).reshape(1)
    return pl.pallas_call(
        solve_kernel,
        out_shape=(half, half),
        grid_spec=pltpu.PrefetchScalarGridSpec(
            num_scalar_prefetch=1,
            grid=(1,),
            in_specs=[
                whole((GROUPS, 2, 2, 5, 8, 128)),
                pl.BlockSpec((1, 8, 128), lambda i, w: (w[0], 0, 0)),
            ],
            out_specs=(whole((GROUPS, 2, 5, 8, 128)), whole((GROUPS, 2, 5, 8, 128))),
            scratch_shapes=[pltpu.VMEM((GROUPS, 2, 2, 5, 8, 128), F32)],
        ),
        compiler_params=params(32),
        name="solve",
    )(where, f, rho)


def inverse(spec, images, pair, ty, tx):
    return pl.pallas_call(
        inverse_kernel,
        out_shape=jax.ShapeDtypeStruct((2, 5, 2, 128, 128), F32),
        grid=(1,),
        in_specs=[
            whole((GROUPS, 2, 5, 8, 128)),
            pl.BlockSpec((2, 5, 2, 128, 128), lambda p: (pair, 0, 0, 0, 0)),
            whole((256, 256)),
            whole((2, 128, 384)),
        ],
        out_specs=whole((2, 5, 2, 128, 128)),
        scratch_shapes=[pltpu.VMEM((5, 384, 256), BF16)],
        compiler_params=params(32),
        name="inverse",
    )(spec, images, ty, tx)


def gaps(lower, upper, beyond):
    pair = pl.BlockSpec((2, 1, 2, 128, 128), lambda c: (0, c, 0, 0, 0))
    one = pl.BlockSpec((1, 1, 2, 128, 128), lambda c: (0, c, 0, 0, 0))
    return pl.pallas_call(
        gap_kernel,
        out_shape=jax.ShapeDtypeStruct((4, 8, 128), F32),
        grid=(5,),
        in_specs=[pair, pair, one],
        out_specs=whole((4, 8, 128)),
        compiler_params=params(16),
        name="gaps",
    )(lower, upper, beyond)


def final(centre, positions, sums, below, lower, upper, above):
    pair = pl.BlockSpec((2, 1, 2, 128, 128), lambda c: (0, c, 0, 0, 0))
    where = lax.axis_index("img").astype(jnp.int32).reshape(1)
    return pl.pallas_call(
        final_kernel,
        out_shape=jax.ShapeDtypeStruct((4, 5, 2, 128, 128), F32),
        grid=(5,),
        in_specs=[SMEM, SMEM, SMEM, whole((128, 8, 128)), pair, pair, pair, pair],
        out_specs=pl.BlockSpec((4, 1, 2, 128, 128), lambda c: (0, c, 0, 0, 0)),
        scratch_shapes=[pltpu.VMEM((4, 5, 8, 128), F32)],
        compiler_params=params(32),
        name="final",
    )(centre, positions, where, sums, below, lower, upper, above)


def local(images, centre, positions):
    forward_y, inverse_y, forward_x, inverse_x, rho = (jnp.asarray(t) for t in tables())
    ring = [(i, (i + 1) % GROUPS) for i in range(GROUPS)]
    back = [(b, a) for a, b in ring]
    rows = [(i, i + 1) for i in range(LOCAL - 1)]
    rows_back = [(b, a) for a, b in rows]

    def rotated(plane):
        q = images[:, :, plane]
        return jnp.stack([q[:, 1], q[:, 0] - q[:, 3], q[:, 4], q[:, 2]], axis=1)

    low = lax.ppermute(rotated(1), "gz", ring)
    high = lax.ppermute(rotated(0), "gz", back)
    f = forward(images, low, high, forward_y, forward_x)
    f = lax.all_to_all(f, "gz", 0, 0, tiled=True)
    u0, u1 = solve(f, rho)
    u0 = lax.all_to_all(u0, "gz", 0, 0, tiled=True)
    u1 = lax.all_to_all(u1, "gz", 0, 0, tiled=True)
    lower = inverse(u0, images, 0, inverse_y, inverse_x)
    above = lax.ppermute(lower, "img", rows_back)
    upper = inverse(u1, images, 1, inverse_y, inverse_x)
    below = lax.ppermute(upper, "img", rows)
    part = gaps(lower, upper, above)
    part = jnp.sum(part, axis=(1, 2))
    part = jnp.pad(part, (0, 4))
    part = jnp.broadcast_to(part[None, :, None], (128, 8, 128))
    sums = lax.all_to_all(part, ("img", "gz"), 0, 0, tiled=True)
    return final(centre, positions, sums, below, lower, upper, above)


def solution(mesh):
    in_specs = (P("img", None, "gz", None, None), P("img"), P("img"))
    out_specs = P("img", None, "gz", None, None)
    return jax.shard_map(local, mesh=mesh, in_specs=in_specs, out_specs=out_specs, check_vma=False)
```

```python
import functools

import jax
import jax.numpy as jnp
import numpy as np
from jax import lax
from jax.experimental import pallas as pl
from jax.experimental.pallas import tpu as pltpu
from jax.sharding import PartitionSpec as P

NX = 128
NY = 128
NZ = 64
GROUPS = 32
IMAGES = 16
LOCAL = 4
CELLS = 5.0 * NZ * NX * NY
SMOOTH = 64.0
EPS = 1e-6
KEEP = 1.0 - 1.0 / SMOOTH
F32 = jnp.float32
BF16 = jnp.bfloat16


def real_basis(length):
    k = np.arange(length)[:, None]
    x = np.arange(length)[None, :]
    angle = 2.0 * np.pi * ((k * x) % length) / length
    table = np.where(k <= length // 2, np.cos(angle), np.sin(angle)) * np.sqrt(2.0 / length)
    table[0] = 1.0 / np.sqrt(length)
    table[length // 2] = np.cos(np.pi * np.arange(length)) / np.sqrt(length)
    return table


def split_np(table):
    import ml_dtypes

    high = table.astype(ml_dtypes.bfloat16)
    low = (table - high.astype(np.float64)).astype(ml_dtypes.bfloat16)
    return high, low


def right_table(table):
    high, low = split_np(table)
    row = np.concatenate([high, low], axis=1)
    return np.concatenate([row, row], axis=0)


def left_table(table):
    high, low = split_np(table)
    return np.concatenate([high, high, low], axis=1)


@functools.cache
def tables():
    basis_x = real_basis(NX)
    basis_y = real_basis(NY)
    swap = np.arange(NX).reshape(-1, 2, 4)[:, ::-1].reshape(-1)
    forward_y = right_table(basis_y.T)
    inverse_y = right_table(basis_y)
    forward_x = np.stack([left_table(basis_x), left_table(basis_x[swap])])
    inverse_x = np.stack([left_table(basis_x.T), left_table(basis_x[swap].T)])
    device = np.arange(GROUPS)[:, None]
    row = np.arange(8)[None, :] % 4
    wave_x = 8 * (device % 16) + 4 * (device // 16) + row
    lam_x = 2.0 - 2.0 * np.cos(2.0 * np.pi * wave_x / NX)
    lam_y = 2.0 - 2.0 * np.cos(2.0 * np.pi * np.arange(NY) / NY)
    lam = lam_x[:, :, None] + lam_y[None, None, :]
    excess = 0.5 / SMOOTH + 0.5 * lam
    rho = 1.0 / (1.0 + excess + np.sqrt(excess * (excess + 2.0)))
    return forward_y, inverse_y, forward_x, inverse_x, rho.astype(np.float32)


def split(value):
    high = value.astype(BF16)
    low = (value - high.astype(F32)).astype(BF16)
    return high, low


def times_right(value, table):
    high, low = split(value)
    both = jnp.dot(jnp.concatenate([high, low], axis=1), table, preferred_element_type=F32)
    return both[:, :128] + both[:, 128:]


def dx(f):
    return (pltpu.roll(f, NX - 1, 0) - pltpu.roll(f, 1, 0)) * 0.5


def dy(f):
    return (pltpu.roll(f, NY - 1, 1) - pltpu.roll(f, 1, 1)) * 0.5


def local_drive(q):
    q1, q2, q3, q4, q5 = q
    qz = -(q1 + q4)
    s11 = q1 * q1 + q2 * q2 + q3 * q3
    s12 = q1 * q2 + q2 * q4 + q3 * q5
    s13 = q1 * q3 + q2 * q5 + q3 * qz
    s22 = q2 * q2 + q4 * q4 + q5 * q5
    s23 = q2 * q3 + q4 * q5 + q5 * qz
    s33 = q3 * q3 + q5 * q5 + qz * qz
    trace = s11 + s22 + s33
    scale = (0.2 + 1.0 / SMOOTH) - 0.1 * trace
    third = trace * (1.0 / 3.0)
    f1 = scale * q1 + 0.5 * (s11 - third) - dy(q3)
    f2 = scale * q2 + 0.5 * s12 - 0.5 * (dy(q5) - dx(q3))
    f3 = scale * q3 + 0.5 * s13 - 0.5 * (dx(q2) + dy(qz - q1))
    f4 = scale * q4 + 0.5 * (s22 - third) + dx(q5)
    f5 = scale * q5 + 0.5 * s23 - 0.5 * (dx(q4 - qz) - dy(q2))
    return f1, f2, f3, f4, f5


def mixed(q):
    return q[1], q[0] - q[3], q[4], q[2]


def spread(r):
    return 0.5 * r[0], -0.25 * r[1], 0.25 * r[2], -0.5 * r[0], -0.25 * r[3]


def along_plane(f):
    around = pltpu.roll(f, NX - 1, 0) + pltpu.roll(f, 1, 0)
    around = around + pltpu.roll(f, NY - 1, 1) + pltpu.roll(f, 1, 1)
    return (6.0 + 1.0 / SMOOTH) * f - around


def push(stack, slot, half, value):
    h, l = split(value)
    cols = slice(half * 128, half * 128 + 128)
    stack[slot, 0:128, cols] = h
    stack[slot, 128:256, cols] = l
    stack[slot, 256:384, cols] = h


def forward_kernel(img, ty, tx, rho_ref, out, keep, stack, spectrum):
    for i in range(2):
        qe = [img[i, c, 0] for c in range(5)]
        qo = [img[i, c, 1] for c in range(5)]
        re = mixed(qe)
        ro = mixed(qo)
        for c, (f, g) in enumerate(zip(local_drive(qe), spread(ro))):
            push(stack, c, 0, times_right(f + 2.0 * g, ty[...]))
        bo = spread([along_plane(r) for r in ro])
        for c, (f, g, b) in enumerate(zip(local_drive(qo), spread(re), bo)):
            push(stack, c, 1, times_right(f - g - b, ty[...]))
        for r in range(4):
            push(stack, 5 + r // 2, r % 2, times_right(re[r], ty[...]))
        for n in range(7):
            spectrum[i, n] = jnp.dot(tx[i], stack[n], preferred_element_type=F32)
    first = lax.broadcasted_iota(jnp.int32, (16, 8, 128), 1) < 4
    for part in range(2):
        rows = slice(part * 16, part * 16 + 16)
        rho = rho_ref[rows]
        beta = rho + 1.0 / rho
        back = (1.0 / SMOOTH) / beta

        def tile(n, half):
            cols = slice(half * 128, half * 128 + 128)
            a = spectrum[0, n, :, cols].reshape(16, 8, 128)
            b = spectrum[1, n, :, cols].reshape(16, 8, 128)
            return jnp.where(first, a, b) if part == 0 else jnp.where(first, b, a)

        g = spread([beta * tile(5 + r // 2, r % 2) for r in range(4)])
        for c in range(5):
            y = tile(c, 0)
            out[rows, 0, 0, c] = beta * tile(c, 1) + y
            out[rows, 1, 0, c] = y + g[c]
            keep[rows, 0, c] = back * y


def solve_kernel(where, f, rho_ref, out0, out1, right, work):
    del where
    rho = rho_ref[0]
    sigma = rho * rho
    power = sigma
    for _ in range(5):
        power = power * power
    closing = 1.0 / (1.0 - power)
    shape = (2, 5, 8, 128)
    zero = jnp.zeros(shape, F32)
    sb = jnp.broadcast_to(sigma, shape)
    cb = jnp.broadcast_to(closing, shape)

    def ends(s, carry):
        v, u, p = carry
        r = f[s, 0] + f[lax.rem(s + 1, GROUPS), 1]
        right[s] = r
        return r + sb * v, u + p[None, None] * r, p * sigma

    v, u, _ = lax.fori_loop(0, GROUPS, ends, (zero, zero, jnp.ones((8, 128), F32)))
    u_last = u * cb

    def up(s, v):
        v = right[s] + sb * v
        work[s] = v
        return v

    lax.fori_loop(0, GROUPS, up, v * cb)
    gain = jnp.broadcast_to(sigma / (1.0 - sigma * sigma), shape)
    back = jnp.broadcast_to((1.0 / SMOOTH) / (rho + 1.0 / rho), shape)

    def put(s, slot, value):
        out0[s, slot] = value[0]
        out1[s, slot] = value[1]

    def down(n, carry):
        u, after = carry
        s = GROUPS - 1 - n
        value = sb * u
        p = gain * (work[s] + value)
        put(s, 0, p)
        put(s + 1, 1, back * (p + after))
        return right[s] + value, p

    value = sb * u_last
    last = gain * (work[GROUPS - 1] + value)
    put(GROUPS - 1, 0, last)
    _, head = lax.fori_loop(1, GROUPS, down, (right[GROUPS - 1] + value, last))
    put(0, 1, back * (head + last))


def fold(value):
    return jnp.sum((value * value).reshape(16, 8, 128), axis=0)


def inverse_kernel(*refs, pair):
    if pair == 0:
        spec, keep, img, ty, tx, out, sums, stack = refs
    else:
        spec, keep, img, ty, tx, lower, out, sums, stack = refs
    first = lax.broadcasted_iota(jnp.int32, (16, 8, 128), 1) < 4
    inner = jnp.zeros((8, 128), F32)
    cross = jnp.zeros((8, 128), F32)
    for i in range(2):
        qo = [img[i, c, 1] for c in range(5)]
        go = spread(mixed(qo))
        for c in range(5):
            p_even, p_odd = spec[0:16, 0, c], spec[16:32, 0, c]
            w_even = spec[0:16, 1, c] + keep[0:16, 0, c]
            w_odd = spec[16:32, 1, c] + keep[16:32, 0, c]
            if i == 1:
                p_even, p_odd, w_even, w_odd = p_odd, p_even, w_odd, w_even
            push(stack, c, 0, jnp.where(first, w_even, w_odd).reshape(128, 128))
            push(stack, c, 1, jnp.where(first, p_even, p_odd).reshape(128, 128))
            both = jnp.dot(tx[i], stack[c], preferred_element_type=F32)
            even = KEEP * img[i, c, 0] + times_right(both[:, :128], ty[...])
            odd = times_right(both[:, 128:], ty[...])
            odd = KEEP * qo[c] + (odd + go[c]) * (1.0 / SMOOTH)
            out[i, c, 0] = even
            out[i, c, 1] = odd
            if i == 1:
                inner = inner + fold(even - out[0, c, 0]) + fold(odd - out[0, c, 1])
            elif pair == 1:
                cross = cross + fold(even - lower[0, c, 0]) + fold(odd - lower[0, c, 1])
    sums[0] = inner
    if pair == 1:
        sums[1] = cross


def edge_kernel(first_sums, second_sums, upper, above, out):
    edge = jnp.zeros((8, 128), F32)
    for c in range(5):
        for zz in range(2):
            edge = edge + fold(above[0, c, zz] - upper[0, c, zz])
    rows = [first_sums[0], second_sums[1], second_sums[0], edge]
    index = lax.broadcasted_iota(jnp.int32, (8, 128), 0)
    total = jnp.zeros((8, 128), F32)
    for g, row in enumerate(rows):
        total = jnp.where(index == g, jnp.sum(row), total)
    out[...] = jnp.broadcast_to(total, (128, 8, 128))


def final_kernel(centre, positions, where, sums, below, lower, upper, above, out, weights):
    @pl.when(pl.program_id(0) == 0)
    def _():
        arc = [jnp.zeros((8, 128), F32)]
        for k in range(LOCAL):
            block = jnp.sum(sums[k * GROUPS : (k + 1) * GROUPS], axis=0)
            dist = jnp.sqrt(block * (1.0 / CELLS) + EPS)
            for g in range(4):
                if k * 4 + g < IMAGES - 1:
                    row = jnp.broadcast_to(dist[g : g + 1], (8, 128))
                    arc.append(arc[-1] + row)
        base = where[0] * LOCAL - 2
        for m in range(LOCAL):
            c = centre[m]
            tau = positions[m] * arc[-1]

            def pick(index):
                value = arc[0]
                for j in range(1, IMAGES):
                    value = jnp.where(index == j, arc[j], value)
                return value

            a, b, d = pick(c - 1), pick(c), pick(c + 1)
            w = (
                (tau - b) * (tau - d) / ((a - b) * (a - d)),
                (tau - a) * (tau - d) / ((b - a) * (b - d)),
                (tau - a) * (tau - b) / ((d - a) * (d - b)),
            )
            for r in range(5):
                spot = base + m + r
                value = jnp.zeros((8, 128), F32)
                for n in range(3):
                    value = jnp.where(c - 1 + n == spot, w[n], value)
                weights[m, r] = value

    pieces = [below[0], below[1], lower[0], lower[1], upper[0], upper[1], above[0], above[1]]
    pieces = [p.reshape(32, 8, 128) for p in pieces]
    for m in range(LOCAL):
        acc = pieces[m] * weights[m, 0][None]
        for r in range(1, 5):
            acc = acc + pieces[m + r] * weights[m, r][None]
        out[m, 0] = acc.reshape(2, 128, 128)


def whole(shape):
    return pl.BlockSpec(shape, lambda *_: (0,) * len(shape))


SMEM = pl.BlockSpec(memory_space=pltpu.SMEM)


def params(mib):
    return pltpu.CompilerParams(
        dimension_semantics=("arbitrary",), vmem_limit_bytes=mib * 1024 * 1024
    )


def forward(images, ty, tx, rho):
    return pl.pallas_call(
        forward_kernel,
        out_shape=(
            jax.ShapeDtypeStruct((GROUPS, 2, 2, 5, 8, 128), F32),
            jax.ShapeDtypeStruct((GROUPS, 2, 5, 8, 128), F32),
        ),
        grid=(2,),
        in_specs=[
            pl.BlockSpec((2, 5, 2, 128, 128), lambda p: (p, 0, 0, 0, 0)),
            whole((256, 256)),
            whole((2, 128, 384)),
            whole((GROUPS, 8, 128)),
        ],
        out_specs=(
            pl.BlockSpec((GROUPS, 2, 1, 5, 8, 128), lambda p: (0, 0, p, 0, 0, 0)),
            pl.BlockSpec((GROUPS, 1, 5, 8, 128), lambda p: (0, p, 0, 0, 0)),
        ),
        scratch_shapes=[
            pltpu.VMEM((7, 384, 256), BF16),
            pltpu.VMEM((2, 7, 128, 256), F32),
        ],
        compiler_params=params(32),
        name="forward",
    )(images, ty, tx, rho)


def solve(f, rho):
    half = jax.ShapeDtypeStruct((GROUPS, 2, 5, 8, 128), F32)
    where = lax.axis_index("gz").astype(jnp.int32).reshape(1)
    return pl.pallas_call(
        solve_kernel,
        out_shape=(half, half),
        grid_spec=pltpu.PrefetchScalarGridSpec(
            num_scalar_prefetch=1,
            grid=(1,),
            in_specs=[
                whole((GROUPS, 2, 2, 5, 8, 128)),
                pl.BlockSpec((1, 8, 128), lambda i, w: (w[0], 0, 0)),
            ],
            out_specs=(whole((GROUPS, 2, 5, 8, 128)), whole((GROUPS, 2, 5, 8, 128))),
            scratch_shapes=[
                pltpu.VMEM((GROUPS, 2, 5, 8, 128), F32),
                pltpu.VMEM((GROUPS, 2, 5, 8, 128), F32),
            ],
        ),
        compiler_params=params(32),
        name="solve",
    )(where, f, rho)


def inverse(spec, keep, images, pair, ty, tx, *lower):
    specs = [
        whole((GROUPS, 2, 5, 8, 128)),
        pl.BlockSpec((GROUPS, 1, 5, 8, 128), lambda p: (0, pair, 0, 0, 0)),
        pl.BlockSpec((2, 5, 2, 128, 128), lambda p: (pair, 0, 0, 0, 0)),
        whole((256, 256)),
        whole((2, 128, 384)),
    ]
    if pair == 1:
        specs.append(pl.BlockSpec((1, 5, 2, 128, 128), lambda p: (1, 0, 0, 0, 0)))
    return pl.pallas_call(
        functools.partial(inverse_kernel, pair=pair),
        out_shape=(
            jax.ShapeDtypeStruct((2, 5, 2, 128, 128), F32),
            jax.ShapeDtypeStruct((2, 8, 128), F32),
        ),
        grid=(1,),
        in_specs=specs,
        out_specs=(whole((2, 5, 2, 128, 128)), whole((2, 8, 128))),
        scratch_shapes=[pltpu.VMEM((5, 384, 256), BF16)],
        compiler_params=params(32),
        name="inverse",
    )(spec, keep, images, ty, tx, *lower)


def edge(first_sums, second_sums, upper, above):
    return pl.pallas_call(
        edge_kernel,
        out_shape=jax.ShapeDtypeStruct((128, 8, 128), F32),
        grid=(1,),
        in_specs=[
            whole((2, 8, 128)),
            whole((2, 8, 128)),
            pl.BlockSpec((1, 5, 2, 128, 128), lambda p: (1, 0, 0, 0, 0)),
            pl.BlockSpec((1, 5, 2, 128, 128), lambda p: (0, 0, 0, 0, 0)),
        ],
        out_specs=whole((128, 8, 128)),
        compiler_params=params(16),
        name="edge",
    )(first_sums, second_sums, upper, above)


def final(centre, positions, sums, below, lower, upper, above):
    pair = pl.BlockSpec((2, 1, 2, 128, 128), lambda c: (0, c, 0, 0, 0))
    where = lax.axis_index("img").astype(jnp.int32).reshape(1)
    return pl.pallas_call(
        final_kernel,
        out_shape=jax.ShapeDtypeStruct((4, 5, 2, 128, 128), F32),
        grid=(5,),
        in_specs=[SMEM, SMEM, SMEM, whole((128, 8, 128)), pair, pair, pair, pair],
        out_specs=pl.BlockSpec((4, 1, 2, 128, 128), lambda c: (0, c, 0, 0, 0)),
        scratch_shapes=[pltpu.VMEM((4, 5, 8, 128), F32)],
        compiler_params=params(32),
        name="final",
    )(centre, positions, where, sums, below, lower, upper, above)


def local(images, centre, positions):
    forward_y, inverse_y, forward_x, inverse_x, rho = (jnp.asarray(t) for t in tables())
    rows = [(i, i + 1) for i in range(LOCAL - 1)]
    rows_back = [(b, a) for a, b in rows]
    f, keep = forward(images, forward_y, forward_x, rho)
    f = lax.all_to_all(f, "gz", 0, 0, tiled=True)
    u0, u1 = solve(f, rho)
    u0 = lax.all_to_all(u0, "gz", 0, 0, tiled=True)
    u1 = lax.all_to_all(u1, "gz", 0, 0, tiled=True)
    lower, first_sums = inverse(u0, keep, images, 0, inverse_y, inverse_x)
    above = lax.ppermute(lower, "img", rows_back)
    upper, second_sums = inverse(u1, keep, images, 1, inverse_y, inverse_x, lower)
    below = lax.ppermute(upper, "img", rows)
    part = edge(first_sums, second_sums, upper, above)
    sums = lax.all_to_all(part, ("img", "gz"), 0, 0, tiled=True)
    return final(centre, positions, sums, below, lower, upper, above)


def solution(mesh):
    in_specs = (P("img", None, "gz", None, None), P("img"), P("img"))
    out_specs = P("img", None, "gz", None, None)
    return jax.shard_map(local, mesh=mesh, in_specs=in_specs, out_specs=out_specs, check_vma=False)
```

```python
import functools

import jax
import jax.numpy as jnp
import numpy as np
from jax import lax
from jax.experimental import pallas as pl
from jax.experimental.pallas import tpu as pltpu
from jax.sharding import PartitionSpec as P

NX = 128
NY = 128
NZ = 64
GROUPS = 32
IMAGES = 16
LOCAL = 4
CELLS = 5.0 * NZ * NX * NY
SMOOTH = 64.0
EPS = 1e-6
KEEP = 1.0 - 1.0 / SMOOTH
FORWARD_MIB = 60
SOLVE_MIB = 32
INVERSE_MIB = 64
EDGE_MIB = 64
FINAL_MIB = 64
F32 = jnp.float32
BF16 = jnp.bfloat16


def real_basis(length):
    k = np.arange(length)[:, None]
    x = np.arange(length)[None, :]
    angle = 2.0 * np.pi * ((k * x) % length) / length
    table = np.where(k <= length // 2, np.cos(angle), np.sin(angle)) * np.sqrt(2.0 / length)
    table[0] = 1.0 / np.sqrt(length)
    table[length // 2] = np.cos(np.pi * np.arange(length)) / np.sqrt(length)
    return table


def split_np(table):
    import ml_dtypes

    high = table.astype(ml_dtypes.bfloat16)
    low = (table - high.astype(np.float64)).astype(ml_dtypes.bfloat16)
    return high, low


def right_table(table):
    high, low = split_np(table)
    row = np.concatenate([high, low], axis=1)
    return np.concatenate([row, row], axis=0)


def left_table(table):
    high, low = split_np(table)
    return np.concatenate([high, high, low], axis=1)


@functools.cache
def tables():
    basis_x = real_basis(NX)
    basis_y = real_basis(NY)
    swap = np.arange(NX).reshape(-1, 2, 4)[:, ::-1].reshape(-1)
    forward_y = right_table(basis_y.T)
    inverse_y = right_table(basis_y)
    forward_x = np.stack([left_table(basis_x), left_table(basis_x[swap])])
    inverse_x = np.stack([left_table(basis_x.T), left_table(basis_x[swap].T)])
    device = np.arange(GROUPS)[:, None]
    row = np.arange(8)[None, :] % 4
    wave_x = 8 * (device % 16) + 4 * (device // 16) + row
    lam_x = 2.0 - 2.0 * np.cos(2.0 * np.pi * wave_x / NX)
    lam_y = 2.0 - 2.0 * np.cos(2.0 * np.pi * np.arange(NY) / NY)
    lam = lam_x[:, :, None] + lam_y[None, None, :]
    excess = 0.5 / SMOOTH + 0.5 * lam
    rho = 1.0 / (1.0 + excess + np.sqrt(excess * (excess + 2.0)))
    return forward_y, inverse_y, forward_x, inverse_x, rho.astype(np.float32)


def split(value):
    high = value.astype(BF16)
    low = (value - high.astype(F32)).astype(BF16)
    return high, low


def times_right(value, table):
    high, low = split(value)
    both = jnp.dot(jnp.concatenate([high, low], axis=1), table, preferred_element_type=F32)
    return both[:, :128] + both[:, 128:]


def dx(f):
    return (pltpu.roll(f, NX - 1, 0) - pltpu.roll(f, 1, 0)) * 0.5


def dy(f):
    return (pltpu.roll(f, NY - 1, 1) - pltpu.roll(f, 1, 1)) * 0.5


def local_drive(q):
    q1, q2, q3, q4, q5 = q
    qz = -(q1 + q4)
    s11 = q1 * q1 + q2 * q2 + q3 * q3
    s12 = q1 * q2 + q2 * q4 + q3 * q5
    s13 = q1 * q3 + q2 * q5 + q3 * qz
    s22 = q2 * q2 + q4 * q4 + q5 * q5
    s23 = q2 * q3 + q4 * q5 + q5 * qz
    s33 = q3 * q3 + q5 * q5 + qz * qz
    trace = s11 + s22 + s33
    scale = (0.2 + 1.0 / SMOOTH) - 0.1 * trace
    third = trace * (1.0 / 3.0)
    f1 = scale * q1 + 0.5 * (s11 - third) - dy(q3)
    f2 = scale * q2 + 0.5 * s12 - 0.5 * (dy(q5) - dx(q3))
    f3 = scale * q3 + 0.5 * s13 - 0.5 * (dx(q2) + dy(qz - q1))
    f4 = scale * q4 + 0.5 * (s22 - third) + dx(q5)
    f5 = scale * q5 + 0.5 * s23 - 0.5 * (dx(q4 - qz) - dy(q2))
    return f1, f2, f3, f4, f5


def mixed(q):
    return q[1], q[0] - q[3], q[4], q[2]


def spread(r):
    return 0.5 * r[0], -0.25 * r[1], 0.25 * r[2], -0.5 * r[0], -0.25 * r[3]


def along_plane(f):
    around = pltpu.roll(f, NX - 1, 0) + pltpu.roll(f, 1, 0)
    around = around + pltpu.roll(f, NY - 1, 1) + pltpu.roll(f, 1, 1)
    return (6.0 + 1.0 / SMOOTH) * f - around


def push(stack, slot, half, value):
    h, l = split(value)
    cols = slice(half * 128, half * 128 + 128)
    stack[slot, 0:128, cols] = h
    stack[slot, 128:256, cols] = l
    stack[slot, 256:384, cols] = h


def forward_kernel(img, ty, tx, rho_ref, out, keep, stack, spectrum):
    for i in range(2):
        qe = [img[i, c, 0] for c in range(5)]
        qo = [img[i, c, 1] for c in range(5)]
        re = mixed(qe)
        ro = mixed(qo)
        for c, (f, g) in enumerate(zip(local_drive(qe), spread(ro))):
            push(stack, c, 0, times_right(f + 2.0 * g, ty[...]))
        bo = spread([along_plane(r) for r in ro])
        for c, (f, g, b) in enumerate(zip(local_drive(qo), spread(re), bo)):
            push(stack, c, 1, times_right(f - g - b, ty[...]))
        for r in range(4):
            push(stack, 5 + r // 2, r % 2, times_right(re[r], ty[...]))
        for n in range(7):
            spectrum[i, n] = jnp.dot(tx[i], stack[n], preferred_element_type=F32)
    first = lax.broadcasted_iota(jnp.int32, (16, 8, 128), 1) < 4
    for part in range(2):
        rows = slice(part * 16, part * 16 + 16)
        rho = rho_ref[rows]
        beta = rho + 1.0 / rho
        back = (1.0 / SMOOTH) / beta

        def tile(n, half):
            cols = slice(half * 128, half * 128 + 128)
            a = spectrum[0, n, :, cols].reshape(16, 8, 128)
            b = spectrum[1, n, :, cols].reshape(16, 8, 128)
            return jnp.where(first, a, b) if part == 0 else jnp.where(first, b, a)

        g = spread([beta * tile(5 + r // 2, r % 2) for r in range(4)])
        for c in range(5):
            y = tile(c, 0)
            out[rows, 0, 0, c] = beta * tile(c, 1) + y
            out[rows, 1, 0, c] = y + g[c]
            keep[rows, 0, c] = back * y


def solve_kernel(where, f, rho_ref, out, right, work):
    del where
    rho = rho_ref[0]
    sigma = rho * rho
    power = sigma
    for _ in range(5):
        power = power * power
    closing = 1.0 / (1.0 - power)
    shape = (2, 5, 8, 128)
    zero = jnp.zeros(shape, F32)
    sb = jnp.broadcast_to(sigma, shape)
    cb = jnp.broadcast_to(closing, shape)

    def ends(s, carry):
        v, u, p = carry
        r = f[s, 0] + f[lax.rem(s + 1, GROUPS), 1]
        right[s] = r
        return r + sb * v, u + p[None, None] * r, p * sigma

    v, u, _ = lax.fori_loop(0, GROUPS, ends, (zero, zero, jnp.ones((8, 128), F32)))
    u_last = u * cb

    def up(s, v):
        v = right[s] + sb * v
        work[s] = v
        return v

    lax.fori_loop(0, GROUPS, up, v * cb)
    gain = jnp.broadcast_to(sigma / (1.0 - sigma * sigma), shape)
    back = jnp.broadcast_to((1.0 / SMOOTH) / (rho + 1.0 / rho), shape)

    def put(s, slot, value):
        out[s, slot] = value

    def down(n, carry):
        u, after = carry
        s = GROUPS - 1 - n
        value = sb * u
        p = gain * (work[s] + value)
        put(s, 0, p)
        put(s + 1, 1, back * (p + after))
        return right[s] + value, p

    value = sb * u_last
    last = gain * (work[GROUPS - 1] + value)
    put(GROUPS - 1, 0, last)
    _, head = lax.fori_loop(1, GROUPS, down, (right[GROUPS - 1] + value, last))
    put(0, 1, back * (head + last))


def fold(value):
    return jnp.sum((value * value).reshape(16, 8, 128), axis=0)


def inverse_kernel(*refs, pair):
    spec, keep, img, mix, minus, ty, tx = refs[:7]
    stack = refs[-1]
    if pair == 0:
        out, sums = refs[7:9], refs[9]
    else:
        lower, upper, sums = refs[7:10]
        out = [upper.at[0], upper.at[1]]
    c = pl.program_id(0)
    weight = jnp.where(c == 0, 0.5, jnp.where(c == 3, -0.5, jnp.where(c == 2, 0.25, -0.25)))
    weight = weight * (1.0 / SMOOTH)
    other = jnp.where(c == 1, 0.25 / SMOOTH, 0.0)
    first = lax.broadcasted_iota(jnp.int32, (16, 8, 128), 1) < 4

    @pl.when(c == 0)
    def _():
        sums[...] = jnp.zeros_like(sums)

    planes = []
    for i in range(2):
        p_even, p_odd = spec[0:16, 0, 0, 0], spec[16:32, 0, 0, 0]
        w_even = spec[0:16, 1, 0, 0] + keep[0:16, 0, 0]
        w_odd = spec[16:32, 1, 0, 0] + keep[16:32, 0, 0]
        if i == 1:
            p_even, p_odd, w_even, w_odd = p_odd, p_even, w_odd, w_even
        push(stack, i, 0, jnp.where(first, w_even, w_odd).reshape(128, 128))
        push(stack, i, 1, jnp.where(first, p_even, p_odd).reshape(128, 128))
        both = jnp.dot(tx[i], stack[i], preferred_element_type=F32)
        even = KEEP * img[i, 0, 0] + times_right(both[:, :128], ty[...])
        odd = times_right(both[:, 128:], ty[...])
        odd = KEEP * img[i, 0, 1] + odd * (1.0 / SMOOTH)
        odd = odd + (weight * mix[i, 0, 0] + other * minus[i, 0, 0])
        out[i][0, 0] = even
        out[i][0, 1] = odd
        planes.append((even, odd))
    sums[0] += fold(planes[1][0] - planes[0][0]) + fold(planes[1][1] - planes[0][1])
    if pair == 1:
        sums[1] += fold(planes[0][0] - lower[0, 0]) + fold(planes[0][1] - lower[0, 1])


def edge_kernel(first_sums, second_sums, upper, above, out):
    edge = jnp.zeros((8, 128), F32)
    for c in range(5):
        for zz in range(2):
            edge = edge + fold(above[c, zz] - upper[0, c, zz])
    rows = [first_sums[0], second_sums[1], second_sums[0], edge]
    index = lax.broadcasted_iota(jnp.int32, (1, 128), 1)
    total = jnp.zeros((1, 128), F32)
    for g, row in enumerate(rows):
        total = jnp.where(index == g, jnp.sum(row), total)
    out[...] = jnp.broadcast_to(total, (128, 1, 128))


def final_kernel(
    centre, positions, where, sums, below, s0, s1, upper, a0, a1, out, weights
):
    @pl.when(pl.program_id(0) == 0)
    def _():
        arc = [jnp.zeros((8, 128), F32)]
        lane = lax.broadcasted_iota(jnp.int32, (1, 128), 1)
        for k in range(LOCAL):
            block = jnp.sum(sums[k * GROUPS : (k + 1) * GROUPS], axis=0)
            dist = jnp.sqrt(block * (1.0 / CELLS) + EPS)
            for g in range(4):
                if k * 4 + g < IMAGES - 1:
                    value = jnp.sum(jnp.where(lane == g, dist, 0.0), axis=1, keepdims=True)
                    arc.append(arc[-1] + jnp.broadcast_to(value, (8, 128)))
        base = where[0] * LOCAL - 2
        for m in range(LOCAL):
            c = centre[m]
            tau = positions[m] * arc[-1]

            def pick(index):
                value = arc[0]
                for j in range(1, IMAGES):
                    value = jnp.where(index == j, arc[j], value)
                return value

            a, b, d = pick(c - 1), pick(c), pick(c + 1)
            w = (
                (tau - b) * (tau - d) / ((a - b) * (a - d)),
                (tau - a) * (tau - d) / ((b - a) * (b - d)),
                (tau - a) * (tau - b) / ((d - a) * (d - b)),
            )
            for r in range(5):
                spot = base + m + r
                value = jnp.zeros((8, 128), F32)
                for n in range(3):
                    value = jnp.where(c - 1 + n == spot, w[n], value)
                weights[m, r] = value

    pieces = [below[0], below[1], s0, s1, upper[0], upper[1], a0, a1]
    pieces = [p[...].reshape(32, 8, 128) for p in pieces]
    for m in range(LOCAL):
        acc = pieces[m] * weights[m, 0][None]
        for r in range(1, 5):
            acc = acc + pieces[m + r] * weights[m, r][None]
        out[m, 0] = acc.reshape(2, 128, 128)


def whole(shape):
    return pl.BlockSpec(shape, lambda *_: (0,) * len(shape))


SMEM = pl.BlockSpec(memory_space=pltpu.SMEM)


def params(mib):
    return pltpu.CompilerParams(
        dimension_semantics=("arbitrary",), vmem_limit_bytes=min(int(mib * 1024 * 1024), 67_043_328)
    )


def cost(flops, moved):
    return pl.CostEstimate(flops=flops, bytes_accessed=moved, transcendentals=0)


def forward(images, ty, tx, rho):
    return pl.pallas_call(
        forward_kernel,
        out_shape=(
            jax.ShapeDtypeStruct((GROUPS, 2, 2, 5, 8, 128), F32),
            jax.ShapeDtypeStruct((GROUPS, 2, 5, 8, 128), F32),
        ),
        grid=(2,),
        in_specs=[
            pl.BlockSpec((2, 5, 2, 128, 128), lambda p: (p, 0, 0, 0, 0)),
            whole((256, 256)),
            whole((2, 128, 384)),
            whole((GROUPS, 8, 128)),
        ],
        out_specs=(
            pl.BlockSpec((GROUPS, 2, 1, 5, 8, 128), lambda p: (0, 0, p, 0, 0, 0)),
            pl.BlockSpec((GROUPS, 1, 5, 8, 128), lambda p: (0, p, 0, 0, 0)),
        ),
        scratch_shapes=[
            pltpu.VMEM((7, 384, 256), BF16),
            pltpu.VMEM((2, 7, 128, 256), F32),
        ],
        compiler_params=params(FORWARD_MIB),
        cost_estimate=cost(3000000000, 9000000),
        name="forward",
    )(images, ty, tx, rho)


def solve(f, rho):
    where = lax.axis_index("gz").astype(jnp.int32).reshape(1)
    shape = (GROUPS, 2, 2, 5, 8, 128)
    return pl.pallas_call(
        solve_kernel,
        out_shape=jax.ShapeDtypeStruct(shape, F32),
        grid_spec=pltpu.PrefetchScalarGridSpec(
            num_scalar_prefetch=1,
            grid=(1,),
            in_specs=[
                whole(shape),
                pl.BlockSpec((1, 8, 128), lambda i, w: (w[0], 0, 0)),
            ],
            out_specs=whole(shape),
            scratch_shapes=[
                pltpu.VMEM((GROUPS, 2, 5, 8, 128), F32),
                pltpu.VMEM((GROUPS, 2, 5, 8, 128), F32),
            ],
        ),
        compiler_params=params(SOLVE_MIB),
        cost_estimate=cost(20000000, 6000000),
        name="solve",
    )(where, f, rho)


def mix_index(pair):
    def index(c):
        source = jnp.where(c == 1, 0, jnp.where(c == 2, 4, jnp.where(c == 4, 2, 1)))
        return pair, source, 1, 0, 0

    return index


def inverse(spec, keep, images, pair, ty, tx, *lower):
    single = pl.BlockSpec((None, 2, 128, 128), lambda c: (c, 0, 0, 0))
    flat = jax.ShapeDtypeStruct((5, 2, 128, 128), F32)
    specs = [
        pl.BlockSpec((GROUPS, 2, 1, 1, 8, 128), lambda c: (0, 0, pair, c, 0, 0)),
        pl.BlockSpec((GROUPS, 1, 1, 8, 128), lambda c: (0, pair, c, 0, 0)),
        pl.BlockSpec((2, 1, 2, 128, 128), lambda c: (pair, c, 0, 0, 0)),
        pl.BlockSpec((2, 1, 1, 128, 128), mix_index(pair)),
        pl.BlockSpec((2, 1, 1, 128, 128), lambda c: (pair, 3, 1, 0, 0)),
        whole((256, 256)),
        whole((2, 128, 384)),
    ]
    if pair == 1:
        specs.append(pl.BlockSpec((1, 2, 128, 128), lambda c: (c, 0, 0, 0)))
        out_shape = (jax.ShapeDtypeStruct((2, 5, 2, 128, 128), F32),)
        out_specs = (pl.BlockSpec((2, 1, 2, 128, 128), lambda c: (0, c, 0, 0, 0)),)
    else:
        out_shape = (flat, flat)
        out_specs = (pl.BlockSpec((1, 2, 128, 128), lambda c: (c, 0, 0, 0)),) * 2
    return pl.pallas_call(
        functools.partial(inverse_kernel, pair=pair),
        out_shape=(*out_shape, jax.ShapeDtypeStruct((2, 8, 128), F32)),
        grid=(5,),
        in_specs=specs,
        out_specs=(*out_specs, whole((2, 8, 128))),
        scratch_shapes=[pltpu.VMEM((2, 384, 256), BF16)],
        compiler_params=params(INVERSE_MIB),
        cost_estimate=cost(2000000000, 6000000),
        name="inverse",
    )(spec, keep, images, images, images, ty, tx, *lower)


def edge(first_sums, second_sums, upper, above):
    return pl.pallas_call(
        edge_kernel,
        out_shape=jax.ShapeDtypeStruct((128, 1, 128), F32),
        grid=(1,),
        in_specs=[
            whole((2, 8, 128)),
            whole((2, 8, 128)),
            pl.BlockSpec((1, 5, 2, 128, 128), lambda p: (1, 0, 0, 0, 0)),
            whole((5, 2, 128, 128)),
        ],
        out_specs=whole((128, 1, 128)),
        compiler_params=params(EDGE_MIB),
        cost_estimate=cost(2000000, 1300000),
        name="edge",
    )(first_sums, second_sums, upper, above)


def final(centre, positions, sums, below, s0, s1, upper, a0, a1):
    pair = pl.BlockSpec((2, 1, 2, 128, 128), lambda c: (0, c, 0, 0, 0))
    one = pl.BlockSpec((1, 2, 128, 128), lambda c: (c, 0, 0, 0))
    where = lax.axis_index("img").astype(jnp.int32).reshape(1)
    return pl.pallas_call(
        final_kernel,
        out_shape=jax.ShapeDtypeStruct((4, 5, 2, 128, 128), F32),
        grid=(5,),
        in_specs=[SMEM, SMEM, SMEM, whole((128, 1, 128)), pair, one, one, pair, one, one],
        out_specs=pl.BlockSpec((4, 1, 2, 128, 128), lambda c: (0, c, 0, 0, 0)),
        scratch_shapes=[pltpu.VMEM((4, 5, 8, 128), F32)],
        compiler_params=params(FINAL_MIB),
        cost_estimate=cost(30000000, 8000000),
        name="final",
    )(centre, positions, where, sums, below, s0, s1, upper, a0, a1)


def local(images, centre, positions):
    forward_y, inverse_y, forward_x, inverse_x, rho = (jnp.asarray(t) for t in tables())
    rows = [(i, i + 1) for i in range(LOCAL - 1)]
    rows_back = [(b, a) for a, b in rows]
    f, keep = forward(images, forward_y, forward_x, rho)
    f = lax.all_to_all(f, "gz", 0, 0, tiled=True)
    u = solve(f, rho)
    u = lax.all_to_all(u, "gz", 0, 0, tiled=True)
    s0, s1, first_sums = inverse(u, keep, images, 0, inverse_y, inverse_x)
    a0 = lax.ppermute(s0, "img", rows_back)
    a1 = lax.ppermute(s1, "img", rows_back)
    upper, second_sums = inverse(u, keep, images, 1, inverse_y, inverse_x, s1)
    below = lax.ppermute(upper, "img", rows)
    part = edge(first_sums, second_sums, upper, a0)
    sums = lax.all_to_all(part, ("img", "gz"), 0, 0, tiled=True)
    return final(centre, positions, sums, below, s0, s1, upper, a0, a1)


def solution(mesh):
    in_specs = (P("img", None, "gz", None, None), P("img"), P("img"))
    out_specs = P("img", None, "gz", None, None)
    return jax.shard_map(
        local, mesh=mesh, in_specs=in_specs, out_specs=out_specs, check_vma=False
    )
```

```python
import functools

import jax
import jax.numpy as jnp
import numpy as np
from jax import lax
from jax.experimental import pallas as pl
from jax.experimental.pallas import tpu as pltpu
from jax.sharding import PartitionSpec as P

NX = 128
NY = 128
NZ = 64
GROUPS = 32
IMAGES = 16
LOCAL = 4
CELLS = 5.0 * NZ * NX * NY
SMOOTH = 64.0
EPS = 1e-6
KEEP = 1.0 - 1.0 / SMOOTH
FORWARD_MIB = 60
SOLVE_MIB = 16
INVERSE_MIB = 8
EDGE_MIB = 4
FINAL_MIB = 16
F32 = jnp.float32
BF16 = jnp.bfloat16


def real_basis(length):
    k = np.arange(length)[:, None]
    x = np.arange(length)[None, :]
    angle = 2.0 * np.pi * ((k * x) % length) / length
    table = np.where(k <= length // 2, np.cos(angle), np.sin(angle)) * np.sqrt(2.0 / length)
    table[0] = 1.0 / np.sqrt(length)
    table[length // 2] = np.cos(np.pi * np.arange(length)) / np.sqrt(length)
    return table


def split_np(table):
    import ml_dtypes

    high = table.astype(ml_dtypes.bfloat16)
    low = (table - high.astype(np.float64)).astype(ml_dtypes.bfloat16)
    return high, low


def right_table(table):
    high, low = split_np(table)
    row = np.concatenate([high, low], axis=1)
    return np.concatenate([row, row], axis=0)


def left_table(table):
    high, low = split_np(table)
    return np.concatenate([high, high, low], axis=1)


@functools.cache
def tables():
    basis_x = real_basis(NX)
    basis_y = real_basis(NY)
    swap = np.arange(NX).reshape(-1, 2, 4)[:, ::-1].reshape(-1)
    forward_y = right_table(basis_y.T)
    inverse_y = right_table(basis_y)
    forward_x = np.stack([left_table(basis_x), left_table(basis_x[swap])])
    inverse_x = np.stack([left_table(basis_x.T), left_table(basis_x[swap].T)])
    device = np.arange(GROUPS)[:, None]
    row = np.arange(8)[None, :] % 4
    wave_x = 8 * (device % 16) + 4 * (device // 16) + row
    lam_x = 2.0 - 2.0 * np.cos(2.0 * np.pi * wave_x / NX)
    lam_y = 2.0 - 2.0 * np.cos(2.0 * np.pi * np.arange(NY) / NY)
    lam = lam_x[:, :, None] + lam_y[None, None, :]
    excess = 0.5 / SMOOTH + 0.5 * lam
    rho = 1.0 / (1.0 + excess + np.sqrt(excess * (excess + 2.0)))
    return forward_y, inverse_y, forward_x, inverse_x, rho.astype(np.float32)


def split(value):
    high = value.astype(BF16)
    low = (value - high.astype(F32)).astype(BF16)
    return high, low


def times_right(value, table):
    high, low = split(value)
    both = jnp.dot(jnp.concatenate([high, low], axis=1), table, preferred_element_type=F32)
    return both[:, :128] + both[:, 128:]


def dx(f):
    return (pltpu.roll(f, NX - 1, 0) - pltpu.roll(f, 1, 0)) * 0.5


def dy(f):
    return (pltpu.roll(f, NY - 1, 1) - pltpu.roll(f, 1, 1)) * 0.5


def local_drive(q):
    q1, q2, q3, q4, q5 = q
    qz = -(q1 + q4)
    s11 = q1 * q1 + q2 * q2 + q3 * q3
    s12 = q1 * q2 + q2 * q4 + q3 * q5
    s13 = q1 * q3 + q2 * q5 + q3 * qz
    s22 = q2 * q2 + q4 * q4 + q5 * q5
    s23 = q2 * q3 + q4 * q5 + q5 * qz
    s33 = q3 * q3 + q5 * q5 + qz * qz
    trace = s11 + s22 + s33
    scale = (0.2 + 1.0 / SMOOTH) - 0.1 * trace
    third = trace * (1.0 / 3.0)
    f1 = scale * q1 + 0.5 * (s11 - third) - dy(q3)
    f2 = scale * q2 + 0.5 * s12 - 0.5 * (dy(q5) - dx(q3))
    f3 = scale * q3 + 0.5 * s13 - 0.5 * (dx(q2) + dy(qz - q1))
    f4 = scale * q4 + 0.5 * (s22 - third) + dx(q5)
    f5 = scale * q5 + 0.5 * s23 - 0.5 * (dx(q4 - qz) - dy(q2))
    return f1, f2, f3, f4, f5


def mixed(q):
    return q[1], q[0] - q[3], q[4], q[2]


def spread(r):
    return 0.5 * r[0], -0.25 * r[1], 0.25 * r[2], -0.5 * r[0], -0.25 * r[3]


def along_plane(f):
    around = pltpu.roll(f, NX - 1, 0) + pltpu.roll(f, 1, 0)
    around = around + pltpu.roll(f, NY - 1, 1) + pltpu.roll(f, 1, 1)
    return (6.0 + 1.0 / SMOOTH) * f - around


def push(stack, slot, half, value):
    h, l = split(value)
    cols = slice(half * 128, half * 128 + 128)
    stack[slot, 0:128, cols] = h
    stack[slot, 128:256, cols] = l
    stack[slot, 256:384, cols] = h


def forward_kernel(img, ty, tx, rho_ref, out, keep, stack, spectrum):
    for i in range(2):
        qe = [img[i, c, 0] for c in range(5)]
        qo = [img[i, c, 1] for c in range(5)]
        re = mixed(qe)
        ro = mixed(qo)
        for c, (f, g) in enumerate(zip(local_drive(qe), spread(ro))):
            push(stack, c, 0, times_right(f + 2.0 * g, ty[...]))
        bo = spread([along_plane(r) for r in ro])
        for c, (f, g, b) in enumerate(zip(local_drive(qo), spread(re), bo)):
            push(stack, c, 1, times_right(f - g - b, ty[...]))
        for r in range(4):
            push(stack, 5 + r // 2, r % 2, times_right(re[r], ty[...]))
        for n in range(7):
            spectrum[i, n] = jnp.dot(tx[i], stack[n], preferred_element_type=F32)
    first = lax.broadcasted_iota(jnp.int32, (16, 8, 128), 1) < 4
    for part in range(2):
        rows = slice(part * 16, part * 16 + 16)
        rho = rho_ref[rows]
        beta = rho + 1.0 / rho
        back = (1.0 / SMOOTH) / beta

        def tile(n, half):
            cols = slice(half * 128, half * 128 + 128)
            a = spectrum[0, n, :, cols].reshape(16, 8, 128)
            b = spectrum[1, n, :, cols].reshape(16, 8, 128)
            return jnp.where(first, a, b) if part == 0 else jnp.where(first, b, a)

        g = spread([beta * tile(5 + r // 2, r % 2) for r in range(4)])
        for c in range(5):
            y = tile(c, 0)
            out[rows, 0, 0, c] = beta * tile(c, 1) + y
            out[rows, 1, 0, c] = y + g[c]
            keep[0, c, rows] = back * y


def solve_kernel(where, f, rho_ref, out, right, work):
    del where
    rho = rho_ref[0]
    sigma = rho * rho
    power = sigma
    for _ in range(5):
        power = power * power
    closing = 1.0 / (1.0 - power)
    shape = (2, 5, 8, 128)
    zero = jnp.zeros(shape, F32)
    sb = jnp.broadcast_to(sigma, shape)
    cb = jnp.broadcast_to(closing, shape)

    def ends(s, carry):
        v, u, p = carry
        r = f[s, 0] + f[lax.rem(s + 1, GROUPS), 1]
        right[s] = r
        return r + sb * v, u + p[None, None] * r, p * sigma

    v, u, _ = lax.fori_loop(0, GROUPS, ends, (zero, zero, jnp.ones((8, 128), F32)))
    u_last = u * cb

    def up(s, v):
        v = right[s] + sb * v
        work[s] = v
        return v

    lax.fori_loop(0, GROUPS, up, v * cb)
    gain = jnp.broadcast_to(sigma / (1.0 - sigma * sigma), shape)
    back = jnp.broadcast_to((1.0 / SMOOTH) / (rho + 1.0 / rho), shape)

    def put(s, slot, value):
        out[s, :, :, slot] = value

    def down(n, carry):
        u, after = carry
        s = GROUPS - 1 - n
        value = sb * u
        p = gain * (work[s] + value)
        put(s, 0, p)
        put(s + 1, 1, back * (p + after))
        return right[s] + value, p

    value = sb * u_last
    last = gain * (work[GROUPS - 1] + value)
    put(GROUPS - 1, 0, last)
    _, head = lax.fori_loop(1, GROUPS, down, (right[GROUPS - 1] + value, last))
    put(0, 1, back * (head + last))


def fold(value):
    return jnp.sum((value * value).reshape(16, 8, 128), axis=0)


def inverse_kernel(*refs, pair):
    spec, keep, img, ty, tx = refs[:5]
    stack = refs[-1]
    if pair == 0:
        out, sums = refs[5:7], refs[7]
    else:
        lower, upper, sums = refs[5:8]
        out = [upper.at[0], upper.at[1]]
    first = lax.broadcasted_iota(jnp.int32, (16, 8, 128), 1) < 4
    sums[...] = jnp.zeros_like(sums)

    @pl.loop(0, 5)
    def _(c):
        weight = jnp.where(c == 0, 0.5, jnp.where(c == 3, -0.5, jnp.where(c == 2, 0.25, -0.25)))
        weight = weight * (1.0 / SMOOTH)
        other = jnp.where(c == 1, 0.25 / SMOOTH, 0.0)
        source = jnp.where(c == 1, 0, jnp.where(c == 2, 4, jnp.where(c == 4, 2, 1)))
        planes = []
        for i in range(2):
            image = 2 * pair + i
            p_even, p_odd = spec[0:16, pair, c, 0], spec[16:32, pair, c, 0]
            w_even = spec[0:16, pair, c, 1] + keep[pair, c, 0:16]
            w_odd = spec[16:32, pair, c, 1] + keep[pair, c, 16:32]
            if i == 1:
                p_even, p_odd, w_even, w_odd = p_odd, p_even, w_odd, w_even
            push(stack, i, 0, jnp.where(first, w_even, w_odd).reshape(128, 128))
            push(stack, i, 1, jnp.where(first, p_even, p_odd).reshape(128, 128))
            both = jnp.dot(tx[i], stack[i], preferred_element_type=F32)
            even = KEEP * img[image, c, 0] + times_right(both[:, :128], ty[...])
            odd = times_right(both[:, 128:], ty[...])
            odd = KEEP * img[image, c, 1] + odd * (1.0 / SMOOTH)
            odd = odd + (weight * img[image, source, 1] + other * img[image, 3, 1])
            out[i][c, 0] = even
            out[i][c, 1] = odd
            planes.append((even, odd))
        sums[0] += fold(planes[1][0] - planes[0][0]) + fold(planes[1][1] - planes[0][1])
        if pair == 1:
            sums[1] += fold(planes[0][0] - lower[c, 0]) + fold(planes[0][1] - lower[c, 1])


def edge_kernel(first_sums, second_sums, upper, above, out):
    edge = jnp.zeros((8, 128), F32)
    for c in range(5):
        for zz in range(2):
            edge = edge + fold(above[c, zz] - upper[1, c, zz])
    rows = [first_sums[0], second_sums[1], second_sums[0], edge]
    index = lax.broadcasted_iota(jnp.int32, (1, 128), 1)
    total = jnp.zeros((1, 128), F32)
    for g, row in enumerate(rows):
        total = jnp.where(index == g, jnp.sum(row), total)
    out[...] = jnp.broadcast_to(total, (128, 1, 128))


def final_kernel(
    centre, positions, where, sums, below, s0, s1, upper, a0, a1, out, weights
):
    @pl.when(pl.program_id(0) == 0)
    def _():
        arc = [jnp.zeros((8, 128), F32)]
        lane = lax.broadcasted_iota(jnp.int32, (1, 128), 1)
        for k in range(LOCAL):
            block = jnp.sum(sums[k * GROUPS : (k + 1) * GROUPS], axis=0)
            dist = jnp.sqrt(block * (1.0 / CELLS) + EPS)
            for g in range(4):
                if k * 4 + g < IMAGES - 1:
                    value = jnp.sum(jnp.where(lane == g, dist, 0.0), axis=1, keepdims=True)
                    arc.append(arc[-1] + jnp.broadcast_to(value, (8, 128)))
        base = where[0] * LOCAL - 2
        for m in range(LOCAL):
            c = centre[m]
            tau = positions[m] * arc[-1]

            def pick(index):
                value = arc[0]
                for j in range(1, IMAGES):
                    value = jnp.where(index == j, arc[j], value)
                return value

            a, b, d = pick(c - 1), pick(c), pick(c + 1)
            w = (
                (tau - b) * (tau - d) / ((a - b) * (a - d)),
                (tau - a) * (tau - d) / ((b - a) * (b - d)),
                (tau - a) * (tau - b) / ((d - a) * (d - b)),
            )
            for r in range(5):
                spot = base + m + r
                value = jnp.zeros((8, 128), F32)
                for n in range(3):
                    value = jnp.where(c - 1 + n == spot, w[n], value)
                weights[m, r] = value

    c = pl.program_id(0)
    pieces = [below[0, 0], below[1, 0], s0[c], s1[c], upper[0, c], upper[1, c], a0[c], a1[0]]
    pieces = [p.reshape(32, 8, 128) for p in pieces]
    for m in range(LOCAL):
        acc = pieces[m] * weights[m, 0][None]
        for r in range(1, 5):
            acc = acc + pieces[m + r] * weights[m, r][None]
        out[m, 0] = acc.reshape(2, 128, 128)


def whole(shape):
    return pl.BlockSpec(shape, lambda *_: (0,) * len(shape))


SMEM = pl.BlockSpec(memory_space=pltpu.SMEM)
VMEM = pl.BlockSpec(memory_space=pltpu.VMEM)


def plain(mib):
    return pltpu.CompilerParams(vmem_limit_bytes=mib * 1024 * 1024)


def params(mib):
    return pltpu.CompilerParams(
        dimension_semantics=("arbitrary",), vmem_limit_bytes=min(int(mib * 1024 * 1024), 67_043_328)
    )


def cost(flops, moved):
    return pl.CostEstimate(flops=flops, bytes_accessed=moved, transcendentals=0)


def forward(images, ty, tx, rho):
    return pl.pallas_call(
        forward_kernel,
        out_shape=(
            jax.ShapeDtypeStruct((GROUPS, 2, 2, 5, 8, 128), F32),
            jax.ShapeDtypeStruct((2, 5, GROUPS, 8, 128), F32),
        ),
        grid=(2,),
        in_specs=[
            pl.BlockSpec((2, 5, 2, 128, 128), lambda p: (p, 0, 0, 0, 0)),
            whole((256, 256)),
            whole((2, 128, 384)),
            whole((GROUPS, 8, 128)),
        ],
        out_specs=(
            pl.BlockSpec((GROUPS, 2, 1, 5, 8, 128), lambda p: (0, 0, p, 0, 0, 0)),
            pl.BlockSpec((1, 5, GROUPS, 8, 128), lambda p: (p, 0, 0, 0, 0)),
        ),
        scratch_shapes=[
            pltpu.VMEM((7, 384, 256), BF16),
            pltpu.VMEM((2, 7, 128, 256), F32),
        ],
        compiler_params=params(FORWARD_MIB),
        cost_estimate=cost(3000000000, 9000000),
        name="forward",
    )(images, ty, tx, rho)


def solve(f, rho):
    where = lax.axis_index("gz").astype(jnp.int32).reshape(1)
    result = (GROUPS, 2, 5, 2, 8, 128)
    return pl.pallas_call(
        solve_kernel,
        out_shape=pltpu.VMEM(result, F32),
        grid_spec=pltpu.PrefetchScalarGridSpec(
            num_scalar_prefetch=1,
            grid=(1,),
            in_specs=[
                VMEM,
                pl.BlockSpec((1, 8, 128), lambda i, w: (w[0], 0, 0)),
            ],
            out_specs=VMEM,
            scratch_shapes=[
                pltpu.VMEM((GROUPS, 2, 5, 8, 128), F32),
                pltpu.VMEM((GROUPS, 2, 5, 8, 128), F32),
            ],
        ),
        compiler_params=params(SOLVE_MIB),
        cost_estimate=cost(20000000, 6000000),
        name="solve",
    )(where, f, rho)


def inverse(spec, keep, images, pair, ty, tx, *lower):
    if pair == 1:
        out_shape = (pltpu.VMEM((2, 5, 2, 128, 128), F32),)
    else:
        out_shape = (pltpu.VMEM((5, 2, 128, 128), F32),) * 2
    out_shape = (*out_shape, pltpu.VMEM((2, 8, 128), F32))
    args = (spec, keep, images, ty, tx, *lower)
    return pl.pallas_call(
        functools.partial(inverse_kernel, pair=pair),
        out_shape=out_shape,
        in_specs=[VMEM] * len(args),
        out_specs=(VMEM,) * len(out_shape),
        scratch_shapes=[pltpu.VMEM((2, 384, 256), BF16)],
        compiler_params=plain(INVERSE_MIB),
        cost_estimate=cost(2_000_000_000, 6_000_000),
        name="inverse",
    )(*args)


def edge(first_sums, second_sums, upper, above):
    return pl.pallas_call(
        edge_kernel,
        out_shape=jax.ShapeDtypeStruct((128, 1, 128), F32),
        in_specs=[VMEM] * 4,
        out_specs=VMEM,
        compiler_params=plain(EDGE_MIB),
        cost_estimate=cost(2_000_000, 1_300_000),
        name="edge",
    )(first_sums, second_sums, upper, above)


def final(centre, positions, sums, below, s0, s1, upper, a0, a1):
    pair = pl.BlockSpec((2, 1, 2, 128, 128), lambda c: (0, c, 0, 0, 0))
    one = pl.BlockSpec((1, 2, 128, 128), lambda c: (c, 0, 0, 0))
    where = lax.axis_index("img").astype(jnp.int32).reshape(1)
    return pl.pallas_call(
        final_kernel,
        out_shape=jax.ShapeDtypeStruct((4, 5, 2, 128, 128), F32),
        grid=(5,),
        in_specs=[SMEM, SMEM, SMEM, VMEM, pair, VMEM, VMEM, VMEM, VMEM, one],
        out_specs=pl.BlockSpec((4, 1, 2, 128, 128), lambda c: (0, c, 0, 0, 0)),
        scratch_shapes=[pltpu.VMEM((4, 5, 8, 128), F32)],
        compiler_params=params(FINAL_MIB),
        cost_estimate=cost(30000000, 8000000),
        name="final",
    )(centre, positions, where, sums, below, s0, s1, upper, a0, a1)


def local(images, centre, positions):
    forward_y, inverse_y, forward_x, inverse_x, rho = (jnp.asarray(t) for t in tables())
    rows = [(i, i + 1) for i in range(LOCAL - 1)]
    rows_back = [(b, a) for a, b in rows]
    f, keep = forward(images, forward_y, forward_x, rho)
    f = lax.all_to_all(f, "gz", 0, 0, tiled=True)
    u = solve(f, rho)
    u = lax.all_to_all(u, "gz", 0, 0, tiled=True)
    s0, s1, first_sums = inverse(u, keep, images, 0, inverse_y, inverse_x)
    a0 = lax.ppermute(s0, "img", rows_back)
    a1 = lax.ppermute(s1, "img", rows_back)
    upper, second_sums = inverse(u, keep, images, 1, inverse_y, inverse_x, s1)
    below = lax.ppermute(upper, "img", rows)
    part = edge(first_sums, second_sums, upper, a0)
    sums = lax.all_to_all(part, ("img", "gz"), 0, 0, tiled=True)
    return final(centre, positions, sums, below, s0, s1, upper, a0, a1)


def solution(mesh):
    in_specs = (P("img", None, "gz", None, None), P("img"), P("img"))
    out_specs = P("img", None, "gz", None, None)
    return jax.shard_map(
        local, mesh=mesh, in_specs=in_specs, out_specs=out_specs, check_vma=False
    )
```

```python
import functools

import jax
import jax.numpy as jnp
import numpy as np
from jax import lax
from jax.experimental import pallas as pl
from jax.experimental.pallas import tpu as pltpu
from jax.sharding import PartitionSpec as P

NX = 128
NY = 128
NZ = 64
GROUPS = 32
IMAGES = 16
LOCAL = 4
CELLS = 5.0 * NZ * NX * NY
SMOOTH = 64.0
EPS = 1e-6
KEEP = 1.0 - 1.0 / SMOOTH
FORWARD_MIB = 60
SOLVE_MIB = 16
INVERSE_MIB = 8
EDGE_MIB = 4
FINAL_MIB = 16
F32 = jnp.float32
BF16 = jnp.bfloat16


def real_basis(length):
    k = np.arange(length)[:, None]
    x = np.arange(length)[None, :]
    angle = 2.0 * np.pi * ((k * x) % length) / length
    table = np.where(k <= length // 2, np.cos(angle), np.sin(angle)) * np.sqrt(2.0 / length)
    table[0] = 1.0 / np.sqrt(length)
    table[length // 2] = np.cos(np.pi * np.arange(length)) / np.sqrt(length)
    return table


def split_np(table):
    import ml_dtypes

    high = table.astype(ml_dtypes.bfloat16)
    low = (table - high.astype(np.float64)).astype(ml_dtypes.bfloat16)
    return high, low


def right_table(table):
    high, low = split_np(table)
    row = np.concatenate([high, low], axis=1)
    return np.concatenate([row, row], axis=0)


def left_table(table):
    high, low = split_np(table)
    return np.concatenate([high, high, low], axis=1)


@functools.cache
def tables():
    basis_x = real_basis(NX)
    basis_y = real_basis(NY)
    swap = np.arange(NX).reshape(-1, 2, 4)[:, ::-1].reshape(-1)
    forward_y = right_table(basis_y.T)
    inverse_y = right_table(basis_y)
    forward_x = np.stack([left_table(basis_x), left_table(basis_x[swap])])
    inverse_x = np.stack([left_table(basis_x.T), left_table(basis_x[swap].T)])
    device = np.arange(GROUPS)[:, None]
    row = np.arange(8)[None, :] % 4
    wave_x = 8 * (device % 16) + 4 * (device // 16) + row
    lam_x = 2.0 - 2.0 * np.cos(2.0 * np.pi * wave_x / NX)
    lam_y = 2.0 - 2.0 * np.cos(2.0 * np.pi * np.arange(NY) / NY)
    lam = lam_x[:, :, None] + lam_y[None, None, :]
    excess = 0.5 / SMOOTH + 0.5 * lam
    rho = 1.0 / (1.0 + excess + np.sqrt(excess * (excess + 2.0)))
    return forward_y, inverse_y, forward_x, inverse_x, rho.astype(np.float32)


def split(value):
    high = value.astype(BF16)
    low = (value - high.astype(F32)).astype(BF16)
    return high, low


def times_right(value, table):
    high, low = split(value)
    both = jnp.dot(jnp.concatenate([high, low], axis=1), table, preferred_element_type=F32)
    return both[:, :128] + both[:, 128:]


def shifts(f, axis):
    size = NX if axis == 0 else NY
    return pltpu.roll(f, size - 1, axis), pltpu.roll(f, 1, axis)


def local_drive(q):
    q1, q2, q3, q4, q5 = q
    both = q1 + q4
    s11 = q1 * q1 + (q2 * q2 + q3 * q3)
    d = q2 * q2
    s22 = q4 * q4 + (d + q5 * q5)
    half_trace = (s11 + s22) + (q1 * q4 - d)
    scale = (0.2 + 1.0 / SMOOTH) - 0.2 * half_trace
    third = half_trace * (1.0 / 3.0)
    h2, h3 = 0.5 * q2, 0.5 * q3
    rolled = {}
    for name, f in (("2", q2), ("3", q3), ("5", q5)):
        for axis in range(2):
            rolled[name, axis] = shifts(f, axis)

    def step(name, axis):
        after, before = rolled[name, axis]
        return after - before

    after, before = shifts(both + q1, 1)
    step_y = after - before
    after, before = shifts(both + q4, 0)
    step_x = after - before
    f1 = scale * q1 + (0.5 * (s11 - step("3", 1)) - third)
    f2 = q2 * (scale + 0.5 * both) + h3 * q5 + 0.25 * (step("3", 0) - step("5", 1))
    f3 = q3 * (scale - 0.5 * q4) + h2 * q5 + 0.25 * (step_y - step("2", 0))
    f4 = scale * q4 + (0.5 * (s22 + step("5", 0)) - third)
    f5 = q5 * (scale - 0.5 * q1) + h2 * q3 + 0.25 * (step("2", 1) - step_x)
    return (f1, f2, f3, f4, f5), rolled


def mixed(q):
    return q[1], q[0] - q[3], q[4], q[2]


def add_spread(f, r, factor):
    half = (0.5 * factor) * r[0]
    return (
        f[0] + half,
        f[1] - (0.25 * factor) * r[1],
        f[2] + (0.25 * factor) * r[2],
        f[3] - half,
        f[4] - (0.25 * factor) * r[3],
    )


def along_plane(f, x, y):
    return (6.0 + 1.0 / SMOOTH) * f - ((x[0] + x[1]) + (y[0] + y[1]))


def push(stack, slot, half, value):
    h, l = split(value)
    cols = slice(half * 128, half * 128 + 128)
    stack[slot, 0:128, cols] = h
    stack[slot, 128:256, cols] = l
    stack[slot, 256:384, cols] = h


def forward_kernel(img, ty, tx, rho_ref, out, keep, stack, spectrum):
    for i in range(2):
        qe = [img[i, c, 0] for c in range(5)]
        qo = [img[i, c, 1] for c in range(5)]
        re = mixed(qe)
        ro = mixed(qo)
        f, _ = local_drive(qe)
        for c, value in enumerate(add_spread(f, ro, 2.0)):
            push(stack, c, 0, times_right(value, ty[...]))
        f, rolled = local_drive(qo)
        total = [re[1] + along_plane(ro[1], shifts(ro[1], 0), shifts(ro[1], 1))]
        for r, name in ((0, "2"), (2, "5"), (3, "3")):
            total.append(re[r] + along_plane(ro[r], rolled[name, 0], rolled[name, 1]))
        total = (total[1], total[0], total[2], total[3])
        for c, value in enumerate(add_spread(f, total, -1.0)):
            push(stack, c, 1, times_right(value, ty[...]))
        for r in range(4):
            push(stack, 5 + r // 2, r % 2, times_right(re[r], ty[...]))
        for n in range(7):
            spectrum[i, n] = jnp.dot(tx[i], stack[n], preferred_element_type=F32)
    first = lax.broadcasted_iota(jnp.int32, (16, 8, 128), 1) < 4
    for part in range(2):
        rows = slice(part * 16, part * 16 + 16)
        rho = rho_ref[rows]
        beta = rho + 1.0 / rho
        back = (1.0 / SMOOTH) / beta

        def tile(n, half):
            cols = slice(half * 128, half * 128 + 128)
            a = spectrum[0, n, :, cols].reshape(16, 8, 128)
            b = spectrum[1, n, :, cols].reshape(16, 8, 128)
            return jnp.where(first, a, b) if part == 0 else jnp.where(first, b, a)

        g = [beta * tile(5 + r // 2, r % 2) for r in range(4)]
        ys = [tile(c, 0) for c in range(5)]
        ks = add_spread(ys, g, 1.0)
        for c in range(5):
            y = ys[c]
            out[rows, 0, 0, c] = beta * tile(c, 1) + y
            out[rows, 1, 0, c] = ks[c]
            keep[0, c, rows] = back * y


def solve_kernel(where, f, rho_ref, out, right, work):
    del where
    rho = rho_ref[0]
    sigma = rho * rho
    power = sigma
    for _ in range(5):
        power = power * power
    closing = 1.0 / (1.0 - power)
    shape = (2, 5, 8, 128)
    zero = jnp.zeros(shape, F32)
    sb = jnp.broadcast_to(sigma, shape)
    cb = jnp.broadcast_to(closing, shape)

    def ends(s, carry):
        v, u, p = carry
        r = f[s, 0] + f[lax.rem(s + 1, GROUPS), 1]
        right[s] = r
        return r + sb * v, u + p[None, None] * r, p * sigma

    v, u, _ = lax.fori_loop(0, GROUPS, ends, (zero, zero, jnp.ones((8, 128), F32)))
    u_last = u * cb

    def up(s, v):
        v = right[s] + sb * v
        work[s] = v
        return v

    lax.fori_loop(0, GROUPS, up, v * cb)
    gain = jnp.broadcast_to(sigma / (1.0 - sigma * sigma), shape)
    back = jnp.broadcast_to((1.0 / SMOOTH) / (rho + 1.0 / rho), shape)

    def put(s, slot, value):
        out[s, :, :, slot] = value

    def down(n, carry):
        u, after = carry
        s = GROUPS - 1 - n
        value = sb * u
        p = gain * (work[s] + value)
        put(s, 0, p)
        put(s + 1, 1, back * (p + after))
        return right[s] + value, p

    value = sb * u_last
    last = gain * (work[GROUPS - 1] + value)
    put(GROUPS - 1, 0, last)
    _, head = lax.fori_loop(1, GROUPS, down, (right[GROUPS - 1] + value, last))
    put(0, 1, back * (head + last))


def fold(value):
    return jnp.sum((value * value).reshape(16, 8, 128), axis=0)


def inverse_kernel(*refs, chosen):
    spec, keep, img, ty, tx = refs[:5]
    stack = refs[-1]
    if chosen[0] == 0:
        out = [refs[5]]
        start = None
    else:
        start, second, upper, sums = refs[5:9]
        out = [second, upper.at[0], upper.at[1]]
        sums[...] = jnp.zeros_like(sums)
    first = lax.broadcasted_iota(jnp.int32, (16, 8, 128), 1) < 4

    @pl.loop(0, 5)
    def _(c):
        weight = jnp.where(c == 0, 0.5, jnp.where(c == 3, -0.5, jnp.where(c == 2, 0.25, -0.25)))
        weight = weight * (1.0 / SMOOTH)
        other = jnp.where(c == 1, 0.25 / SMOOTH, 0.0)
        source = jnp.where(c == 1, 0, jnp.where(c == 2, 4, jnp.where(c == 4, 2, 1)))
        if start is not None:
            last = (start[c, 0], start[c, 1])
        for n, image in enumerate(chosen):
            pair, i = image // 2, image % 2
            p_even, p_odd = spec[0:16, pair, c, 0], spec[16:32, pair, c, 0]
            w_even = spec[0:16, pair, c, 1] + keep[pair, c, 0:16]
            w_odd = spec[16:32, pair, c, 1] + keep[pair, c, 16:32]
            if i == 1:
                p_even, p_odd, w_even, w_odd = p_odd, p_even, w_odd, w_even
            push(stack, n, 0, jnp.where(first, w_even, w_odd).reshape(128, 128))
            push(stack, n, 1, jnp.where(first, p_even, p_odd).reshape(128, 128))
            both = jnp.dot(tx[i], stack[n], preferred_element_type=F32)
            even = KEEP * img[image, c, 0] + times_right(both[:, :128], ty[...])
            odd = times_right(both[:, 128:], ty[...])
            odd = KEEP * img[image, c, 1] + odd * (1.0 / SMOOTH)
            odd = odd + (weight * img[image, source, 1] + other * img[image, 3, 1])
            out[n][c, 0] = even
            out[n][c, 1] = odd
            if start is not None:
                sums[n] += fold(even - last[0]) + fold(odd - last[1])
                last = (even, odd)


def edge_kernel(sums, upper, above, out):
    edge = jnp.zeros((8, 128), F32)
    for c in range(5):
        for zz in range(2):
            edge = edge + fold(above[c, zz] - upper[1, c, zz])
    rows = [sums[0], sums[1], sums[2], edge]
    index = lax.broadcasted_iota(jnp.int32, (1, 128), 1)
    total = jnp.zeros((1, 128), F32)
    for g, row in enumerate(rows):
        total = jnp.where(index == g, jnp.sum(row), total)
    out[...] = jnp.broadcast_to(total, (128, 1, 128))


def final_kernel(
    centre, positions, where, sums, below, s0, s1, upper, a0, a1, out, weights
):
    @pl.when(pl.program_id(0) == 0)
    def _():
        arc = [jnp.zeros((8, 128), F32)]
        lane = lax.broadcasted_iota(jnp.int32, (1, 128), 1)
        for k in range(LOCAL):
            block = jnp.sum(sums[k * GROUPS : (k + 1) * GROUPS], axis=0)
            dist = jnp.sqrt(block * (1.0 / CELLS) + EPS)
            for g in range(4):
                if k * 4 + g < IMAGES - 1:
                    value = jnp.sum(jnp.where(lane == g, dist, 0.0), axis=1, keepdims=True)
                    arc.append(arc[-1] + jnp.broadcast_to(value, (8, 128)))
        base = where[0] * LOCAL - 2
        for m in range(LOCAL):
            c = centre[m]
            tau = positions[m] * arc[-1]

            def pick(index):
                value = arc[0]
                for j in range(1, IMAGES):
                    value = jnp.where(index == j, arc[j], value)
                return value

            a, b, d = pick(c - 1), pick(c), pick(c + 1)
            w = (
                (tau - b) * (tau - d) / ((a - b) * (a - d)),
                (tau - a) * (tau - d) / ((b - a) * (b - d)),
                (tau - a) * (tau - b) / ((d - a) * (d - b)),
            )
            for r in range(5):
                spot = base + m + r
                value = jnp.zeros((8, 128), F32)
                for n in range(3):
                    value = jnp.where(c - 1 + n == spot, w[n], value)
                weights[m, r] = value

    c = pl.program_id(0)
    pieces = [below[0, 0], below[1, 0], s0[c], s1[c], upper[0, c], upper[1, c], a0[c], a1[0]]
    pieces = [p.reshape(32, 8, 128) for p in pieces]
    for m in range(LOCAL):
        acc = pieces[m] * weights[m, 0][None]
        for r in range(1, 5):
            acc = acc + pieces[m + r] * weights[m, r][None]
        out[m, 0] = acc.reshape(2, 128, 128)


def whole(shape):
    return pl.BlockSpec(shape, lambda *_: (0,) * len(shape))


SMEM = pl.BlockSpec(memory_space=pltpu.SMEM)
VMEM = pl.BlockSpec(memory_space=pltpu.VMEM)


def plain(mib):
    return pltpu.CompilerParams(vmem_limit_bytes=mib * 1024 * 1024)


def params(mib):
    return pltpu.CompilerParams(
        dimension_semantics=("arbitrary",), vmem_limit_bytes=min(int(mib * 1024 * 1024), 67_043_328)
    )


def cost(flops, moved):
    return pl.CostEstimate(flops=flops, bytes_accessed=moved, transcendentals=0)


def forward(images, ty, tx, rho):
    return pl.pallas_call(
        forward_kernel,
        out_shape=(
            jax.ShapeDtypeStruct((GROUPS, 2, 2, 5, 8, 128), F32),
            jax.ShapeDtypeStruct((2, 5, GROUPS, 8, 128), F32),
        ),
        grid=(2,),
        in_specs=[
            pl.BlockSpec((2, 5, 2, 128, 128), lambda p: (p, 0, 0, 0, 0)),
            whole((256, 256)),
            whole((2, 128, 384)),
            whole((GROUPS, 8, 128)),
        ],
        out_specs=(
            pl.BlockSpec((GROUPS, 2, 1, 5, 8, 128), lambda p: (0, 0, p, 0, 0, 0)),
            pl.BlockSpec((1, 5, GROUPS, 8, 128), lambda p: (p, 0, 0, 0, 0)),
        ),
        scratch_shapes=[
            pltpu.VMEM((7, 384, 256), BF16),
            pltpu.VMEM((2, 7, 128, 256), F32),
        ],
        compiler_params=params(FORWARD_MIB),
        cost_estimate=cost(3000000000, 9000000),
        name="forward",
    )(images, ty, tx, rho)


def solve(f, rho):
    where = lax.axis_index("gz").astype(jnp.int32).reshape(1)
    result = (GROUPS, 2, 5, 2, 8, 128)
    return pl.pallas_call(
        solve_kernel,
        out_shape=pltpu.VMEM(result, F32),
        grid_spec=pltpu.PrefetchScalarGridSpec(
            num_scalar_prefetch=1,
            grid=(1,),
            in_specs=[
                VMEM,
                pl.BlockSpec((1, 8, 128), lambda i, w: (w[0], 0, 0)),
            ],
            out_specs=VMEM,
            scratch_shapes=[
                pltpu.VMEM((GROUPS, 2, 5, 8, 128), F32),
                pltpu.VMEM((GROUPS, 2, 5, 8, 128), F32),
            ],
        ),
        compiler_params=params(SOLVE_MIB),
        cost_estimate=cost(20000000, 6000000),
        name="solve",
    )(where, f, rho)


def inverse(chosen, spec, keep, images, ty, tx, *start):
    one = pltpu.VMEM((5, 2, 128, 128), F32)
    if start:
        out_shape = (one, pltpu.VMEM((2, 5, 2, 128, 128), F32), pltpu.VMEM((3, 8, 128), F32))
    else:
        out_shape = (one,)
    args = (spec, keep, images, ty, tx, *start)
    count = len(chosen)
    return pl.pallas_call(
        functools.partial(inverse_kernel, chosen=chosen),
        out_shape=out_shape,
        in_specs=[VMEM] * len(args),
        out_specs=(VMEM,) * len(out_shape),
        scratch_shapes=[pltpu.VMEM((count, 384, 256), BF16)],
        compiler_params=plain(INVERSE_MIB),
        cost_estimate=cost(1_000_000_000 * count, 3_000_000 * count),
        name="inverse",
    )(*args)


def edge(sums, upper, above):
    return pl.pallas_call(
        edge_kernel,
        out_shape=jax.ShapeDtypeStruct((128, 1, 128), F32),
        in_specs=[VMEM] * 3,
        out_specs=VMEM,
        compiler_params=plain(EDGE_MIB),
        cost_estimate=cost(2_000_000, 1_300_000),
        name="edge",
    )(sums, upper, above)


def final(centre, positions, sums, below, s0, s1, upper, a0, a1):
    pair = pl.BlockSpec((2, 1, 2, 128, 128), lambda c: (0, c, 0, 0, 0))
    one = pl.BlockSpec((1, 2, 128, 128), lambda c: (c, 0, 0, 0))
    where = lax.axis_index("img").astype(jnp.int32).reshape(1)
    return pl.pallas_call(
        final_kernel,
        out_shape=jax.ShapeDtypeStruct((4, 5, 2, 128, 128), F32),
        grid=(5,),
        in_specs=[SMEM, SMEM, SMEM, VMEM, pair, VMEM, VMEM, VMEM, VMEM, one],
        out_specs=pl.BlockSpec((4, 1, 2, 128, 128), lambda c: (0, c, 0, 0, 0)),
        scratch_shapes=[pltpu.VMEM((4, 5, 8, 128), F32)],
        compiler_params=params(FINAL_MIB),
        cost_estimate=cost(30000000, 8000000),
        name="final",
    )(centre, positions, where, sums, below, s0, s1, upper, a0, a1)


def local(images, centre, positions):
    forward_y, inverse_y, forward_x, inverse_x, rho = (jnp.asarray(t) for t in tables())
    rows = [(i, i + 1) for i in range(LOCAL - 1)]
    rows_back = [(b, a) for a, b in rows]
    f, keep = forward(images, forward_y, forward_x, rho)
    f = lax.all_to_all(f, "gz", 0, 0, tiled=True)
    u = solve(f, rho)
    u = lax.all_to_all(u, "gz", 0, 0, tiled=True)
    (s0,) = inverse((0,), u, keep, images, inverse_y, inverse_x)
    a0 = lax.ppermute(s0, "img", rows_back)
    s1, upper, sums = inverse((1, 2, 3), u, keep, images, inverse_y, inverse_x, s0)
    a1 = lax.ppermute(s1, "img", rows_back)
    below = lax.ppermute(upper, "img", rows)
    part = edge(sums, upper, a0)
    sums = lax.all_to_all(part, ("img", "gz"), 0, 0, tiled=True)
    return final(centre, positions, sums, below, s0, s1, upper, a0, a1)


def solution(mesh):
    in_specs = (P("img", None, "gz", None, None), P("img"), P("img"))
    out_specs = P("img", None, "gz", None, None)
    return jax.shard_map(
        local, mesh=mesh, in_specs=in_specs, out_specs=out_specs, check_vma=False
    )
```

```python
import functools

import jax
import jax.numpy as jnp
import numpy as np
from jax import lax
from jax.experimental import pallas as pl
from jax.experimental.pallas import tpu as pltpu
from jax.sharding import PartitionSpec as P

NX = 128
NY = 128
NZ = 64
GROUPS = 32
IMAGES = 16
LOCAL = 4
CELLS = 5.0 * NZ * NX * NY
SMOOTH = 64.0
EPS = 1e-6
KEEP = 1.0 - 1.0 / SMOOTH
FORWARD_MIB = 60
SOLVE_MIB = 16
INVERSE_MIB = 62.3
EDGE_MIB = 4
FINAL_MIB = 16
F32 = jnp.float32
BF16 = jnp.bfloat16


def real_basis(length):
    k = np.arange(length)[:, None]
    x = np.arange(length)[None, :]
    angle = 2.0 * np.pi * ((k * x) % length) / length
    table = np.where(k <= length // 2, np.cos(angle), np.sin(angle)) * np.sqrt(2.0 / length)
    table[0] = 1.0 / np.sqrt(length)
    table[length // 2] = np.cos(np.pi * np.arange(length)) / np.sqrt(length)
    return table


def split_np(table):
    import ml_dtypes

    high = table.astype(ml_dtypes.bfloat16)
    low = (table - high.astype(np.float64)).astype(ml_dtypes.bfloat16)
    return high, low


def right_table(table):
    high, low = split_np(table)
    row = np.concatenate([high, low], axis=1)
    return np.concatenate([row, row], axis=0)


def left_table(table):
    high, low = split_np(table)
    return np.concatenate([high, high, low], axis=1)


@functools.cache
def tables():
    basis_x = real_basis(NX)
    basis_y = real_basis(NY)
    swap = np.arange(NX).reshape(-1, 2, 4)[:, ::-1].reshape(-1)
    forward_y = right_table(basis_y.T)
    inverse_y = right_table(basis_y)
    forward_x = np.stack([left_table(basis_x), left_table(basis_x[swap])])
    inverse_x = np.stack([left_table(basis_x.T), left_table(basis_x[swap].T)])
    device = np.arange(GROUPS)[:, None]
    row = np.arange(8)[None, :] % 4
    wave_x = 8 * (device % 16) + 4 * (device // 16) + row
    lam_x = 2.0 - 2.0 * np.cos(2.0 * np.pi * wave_x / NX)
    lam_y = 2.0 - 2.0 * np.cos(2.0 * np.pi * np.arange(NY) / NY)
    lam = lam_x[:, :, None] + lam_y[None, None, :]
    excess = 0.5 / SMOOTH + 0.5 * lam
    rho = 1.0 / (1.0 + excess + np.sqrt(excess * (excess + 2.0)))
    return forward_y, inverse_y, forward_x, inverse_x, rho.astype(np.float32)


def split(value):
    high = value.astype(BF16)
    low = (value - high.astype(F32)).astype(BF16)
    return high, low


def times_right(value, table):
    high, low = split(value)
    both = jnp.dot(jnp.concatenate([high, low], axis=1), table, preferred_element_type=F32)
    return both[:, :128] + both[:, 128:]


def shifts(f, axis):
    size = NX if axis == 0 else NY
    return pltpu.roll(f, size - 1, axis), pltpu.roll(f, 1, axis)


def local_drive(q):
    q1, q2, q3, q4, q5 = q
    both = q1 + q4
    s11 = q1 * q1 + (q2 * q2 + q3 * q3)
    d = q2 * q2
    s22 = q4 * q4 + (d + q5 * q5)
    half_trace = (s11 + s22) + (q1 * q4 - d)
    scale = (0.2 + 1.0 / SMOOTH) - 0.2 * half_trace
    third = half_trace * (1.0 / 3.0)
    h2, h3 = 0.5 * q2, 0.5 * q3
    rolled = {}
    for name, f in (("2", q2), ("3", q3), ("5", q5)):
        for axis in range(2):
            rolled[name, axis] = shifts(f, axis)

    def step(name, axis):
        after, before = rolled[name, axis]
        return after - before

    after, before = shifts(both + q1, 1)
    step_y = after - before
    after, before = shifts(both + q4, 0)
    step_x = after - before
    f1 = scale * q1 + (0.5 * (s11 - step("3", 1)) - third)
    f2 = q2 * (scale + 0.5 * both) + h3 * q5 + 0.25 * (step("3", 0) - step("5", 1))
    f3 = q3 * (scale - 0.5 * q4) + h2 * q5 + 0.25 * (step_y - step("2", 0))
    f4 = scale * q4 + (0.5 * (s22 + step("5", 0)) - third)
    f5 = q5 * (scale - 0.5 * q1) + h2 * q3 + 0.25 * (step("2", 1) - step_x)
    return (f1, f2, f3, f4, f5), rolled


def mixed(q):
    return q[1], q[0] - q[3], q[4], q[2]


def add_spread(f, r, factor):
    half = (0.5 * factor) * r[0]
    return (
        f[0] + half,
        f[1] - (0.25 * factor) * r[1],
        f[2] + (0.25 * factor) * r[2],
        f[3] - half,
        f[4] - (0.25 * factor) * r[3],
    )


def along_plane(f, x, y):
    return (6.0 + 1.0 / SMOOTH) * f - ((x[0] + x[1]) + (y[0] + y[1]))


def push(stack, slot, half, value):
    h, l = split(value)
    cols = slice(half * 128, half * 128 + 128)
    stack[slot, 0:128, cols] = h
    stack[slot, 128:256, cols] = l
    stack[slot, 256:384, cols] = h


def forward_kernel(img, ty, tx, rho_ref, out, keep, stack, spectrum):
    for i in range(2):
        qe = [img[i, c, 0] for c in range(5)]
        qo = [img[i, c, 1] for c in range(5)]
        re = mixed(qe)
        ro = mixed(qo)
        f, _ = local_drive(qe)
        for c, value in enumerate(add_spread(f, ro, 2.0)):
            push(stack, c, 0, times_right(value, ty[...]))
        f, rolled = local_drive(qo)
        total = [re[1] + along_plane(ro[1], shifts(ro[1], 0), shifts(ro[1], 1))]
        for r, name in ((0, "2"), (2, "5"), (3, "3")):
            total.append(re[r] + along_plane(ro[r], rolled[name, 0], rolled[name, 1]))
        total = (total[1], total[0], total[2], total[3])
        for c, value in enumerate(add_spread(f, total, -1.0)):
            push(stack, c, 1, times_right(value, ty[...]))
        for r in range(4):
            push(stack, 5 + r // 2, r % 2, times_right(re[r], ty[...]))
        for n in range(7):
            spectrum[i, n] = jnp.dot(tx[i], stack[n], preferred_element_type=F32)
    first = lax.broadcasted_iota(jnp.int32, (16, 8, 128), 1) < 4
    for part in range(2):
        rows = slice(part * 16, part * 16 + 16)
        rho = rho_ref[rows]
        beta = rho + 1.0 / rho
        back = (1.0 / SMOOTH) / beta

        def tile(n, half):
            cols = slice(half * 128, half * 128 + 128)
            a = spectrum[0, n, :, cols].reshape(16, 8, 128)
            b = spectrum[1, n, :, cols].reshape(16, 8, 128)
            return jnp.where(first, a, b) if part == 0 else jnp.where(first, b, a)

        g = [beta * tile(5 + r // 2, r % 2) for r in range(4)]
        ys = [tile(c, 0) for c in range(5)]
        ks = add_spread(ys, g, 1.0)
        for c in range(5):
            y = ys[c]
            out[rows, 0, 0, c] = beta * tile(c, 1) + y
            out[rows, 1, 0, c] = ks[c]
            keep[0, c, rows] = back * y


def solve_kernel(where, f, rho_ref, out0, out1, right, work):
    del where
    rho = rho_ref[0]
    sigma = rho * rho
    power = sigma
    for _ in range(5):
        power = power * power
    closing = 1.0 / (1.0 - power)
    shape = (2, 5, 8, 128)
    zero = jnp.zeros(shape, F32)
    sb = jnp.broadcast_to(sigma, shape)
    cb = jnp.broadcast_to(closing, shape)

    def ends(s, carry):
        v, u, p = carry
        r = f[s, 0] + f[lax.rem(s + 1, GROUPS), 1]
        right[s] = r
        return r + sb * v, u + p[None, None] * r, p * sigma

    v, u, _ = lax.fori_loop(0, GROUPS, ends, (zero, zero, jnp.ones((8, 128), F32)))
    u_last = u * cb

    def up(s, v):
        v = right[s] + sb * v
        work[s] = v
        return v

    lax.fori_loop(0, GROUPS, up, v * cb)
    gain = jnp.broadcast_to(sigma / (1.0 - sigma * sigma), shape)
    back = jnp.broadcast_to((1.0 / SMOOTH) / (rho + 1.0 / rho), shape)

    def put(s, slot, value):
        out0[s, :, slot] = value[0]
        out1[s, :, slot] = value[1]

    def down(n, carry):
        u, after = carry
        s = GROUPS - 1 - n
        value = sb * u
        p = gain * (work[s] + value)
        put(s, 0, p)
        put(s + 1, 1, back * (p + after))
        return right[s] + value, p

    value = sb * u_last
    last = gain * (work[GROUPS - 1] + value)
    put(GROUPS - 1, 0, last)
    _, head = lax.fori_loop(1, GROUPS, down, (right[GROUPS - 1] + value, last))
    put(0, 1, back * (head + last))


def fold(value):
    return jnp.sum((value * value).reshape(16, 8, 128), axis=0)


def inverse_kernel(*refs, pair):
    spec_hbm, keep_hbm, img_hbm, ty, tx = refs[:5]
    spec, img, keep, spec_sem, img_sem, keep_sem, stack = refs[-7:]
    if pair == 0:
        out, sums = refs[5:7], refs[7]
        start = None
    else:
        start, upper, sums = refs[5:8]
        out = [upper.at[0], upper.at[1]]

    def fetch_keep(c):
        return pltpu.make_async_copy(keep_hbm.at[pair, c], keep.at[c], keep_sem.at[c])

    def fetch_spec(c):
        return pltpu.make_async_copy(spec_hbm.at[:, c], spec.at[c], spec_sem.at[c])

    images = pltpu.make_async_copy(img_hbm.at[pl.ds(2 * pair, 2)], img, img_sem)
    images.start()
    for c in range(5):
        fetch_spec(c).start()
        fetch_keep(c).start()
    sums[...] = jnp.zeros_like(sums)
    first = lax.broadcasted_iota(jnp.int32, (16, 8, 128), 1) < 4
    images.wait()

    @pl.loop(0, 5)
    def _(c):
        fetch_spec(c).wait()
        fetch_keep(c).wait()
        weight = jnp.where(c == 0, 0.5, jnp.where(c == 3, -0.5, jnp.where(c == 2, 0.25, -0.25)))
        weight = weight * (1.0 / SMOOTH)
        other = jnp.where(c == 1, 0.25 / SMOOTH, 0.0)
        source = jnp.where(c == 1, 0, jnp.where(c == 2, 4, jnp.where(c == 4, 2, 1)))
        last = None if start is None else (start[c, 0], start[c, 1])
        for i in range(2):
            p_even, p_odd = spec[c, 0:16, 0], spec[c, 16:32, 0]
            w_even = spec[c, 0:16, 1] + keep[c, 0:16]
            w_odd = spec[c, 16:32, 1] + keep[c, 16:32]
            if i == 1:
                p_even, p_odd, w_even, w_odd = p_odd, p_even, w_odd, w_even
            push(stack, i, 0, jnp.where(first, w_even, w_odd).reshape(128, 128))
            push(stack, i, 1, jnp.where(first, p_even, p_odd).reshape(128, 128))
            both = jnp.dot(tx[i], stack[i], preferred_element_type=F32)
            even = KEEP * img[i, c, 0] + times_right(both[:, :128], ty[...])
            odd = times_right(both[:, 128:], ty[...])
            odd = KEEP * img[i, c, 1] + odd * (1.0 / SMOOTH)
            odd = odd + (weight * img[i, source, 1] + other * img[i, 3, 1])
            out[i][c, 0] = even
            out[i][c, 1] = odd
            if last is not None:
                sums[i] += fold(even - last[0]) + fold(odd - last[1])
            last = (even, odd)


def edge_kernel(first_sums, second_sums, upper, above, out):
    edge = jnp.zeros((8, 128), F32)
    for c in range(5):
        for zz in range(2):
            edge = edge + fold(above[c, zz] - upper[1, c, zz])
    rows = [first_sums[1], second_sums[0], second_sums[1], edge]
    index = lax.broadcasted_iota(jnp.int32, (1, 128), 1)
    total = jnp.zeros((1, 128), F32)
    for g, row in enumerate(rows):
        total = jnp.where(index == g, jnp.sum(row), total)
    out[...] = jnp.broadcast_to(total, (128, 1, 128))


def final_kernel(
    centre, positions, where, sums, below, s0, s1, upper, a0, a1, out, weights
):
    @pl.when(pl.program_id(0) == 0)
    def _():
        arc = [jnp.zeros((8, 128), F32)]
        lane = lax.broadcasted_iota(jnp.int32, (1, 128), 1)
        for k in range(LOCAL):
            block = jnp.sum(sums[k * GROUPS : (k + 1) * GROUPS], axis=0)
            dist = jnp.sqrt(block * (1.0 / CELLS) + EPS)
            for g in range(4):
                if k * 4 + g < IMAGES - 1:
                    value = jnp.sum(jnp.where(lane == g, dist, 0.0), axis=1, keepdims=True)
                    arc.append(arc[-1] + jnp.broadcast_to(value, (8, 128)))
        base = where[0] * LOCAL - 2
        for m in range(LOCAL):
            c = centre[m]
            tau = positions[m] * arc[-1]

            def pick(index):
                value = arc[0]
                for j in range(1, IMAGES):
                    value = jnp.where(index == j, arc[j], value)
                return value

            a, b, d = pick(c - 1), pick(c), pick(c + 1)
            w = (
                (tau - b) * (tau - d) / ((a - b) * (a - d)),
                (tau - a) * (tau - d) / ((b - a) * (b - d)),
                (tau - a) * (tau - b) / ((d - a) * (d - b)),
            )
            for r in range(5):
                spot = base + m + r
                value = jnp.zeros((8, 128), F32)
                for n in range(3):
                    value = jnp.where(c - 1 + n == spot, w[n], value)
                weights[m, r] = value

    pieces = [below[0, 0], below[1, 0], s0[0], s1[0], upper[0, 0], upper[1, 0], a0[0], a1[0]]
    pieces = [p.reshape(32, 8, 128) for p in pieces]
    for m in range(LOCAL):
        acc = pieces[m] * weights[m, 0][None]
        for r in range(1, 5):
            acc = acc + pieces[m + r] * weights[m, r][None]
        out[m, 0] = acc.reshape(2, 128, 128)


def whole(shape):
    return pl.BlockSpec(shape, lambda *_: (0,) * len(shape))


SMEM = pl.BlockSpec(memory_space=pltpu.SMEM)
VMEM = pl.BlockSpec(memory_space=pltpu.VMEM)
HBM = pl.BlockSpec(memory_space=pltpu.HBM)


def plain(mib):
    return pltpu.CompilerParams(vmem_limit_bytes=min(int(mib * 1024 * 1024), 67_043_328))


def params(mib):
    return pltpu.CompilerParams(
        dimension_semantics=("arbitrary",), vmem_limit_bytes=min(int(mib * 1024 * 1024), 67_043_328)
    )


def cost(flops, moved):
    return pl.CostEstimate(flops=flops, bytes_accessed=moved, transcendentals=0)


def forward(images, ty, tx, rho):
    return pl.pallas_call(
        forward_kernel,
        out_shape=(
            jax.ShapeDtypeStruct((GROUPS, 2, 2, 5, 8, 128), F32),
            jax.ShapeDtypeStruct((2, 5, GROUPS, 8, 128), F32),
        ),
        grid=(2,),
        in_specs=[
            pl.BlockSpec((2, 5, 2, 128, 128), lambda p: (p, 0, 0, 0, 0)),
            whole((256, 256)),
            whole((2, 128, 384)),
            whole((GROUPS, 8, 128)),
        ],
        out_specs=(
            pl.BlockSpec((GROUPS, 2, 1, 5, 8, 128), lambda p: (0, 0, p, 0, 0, 0)),
            pl.BlockSpec((1, 5, GROUPS, 8, 128), lambda p: (p, 0, 0, 0, 0)),
        ),
        scratch_shapes=[
            pltpu.VMEM((7, 384, 256), BF16),
            pltpu.VMEM((2, 7, 128, 256), F32),
        ],
        compiler_params=params(FORWARD_MIB),
        cost_estimate=cost(3000000000, 9000000),
        name="forward",
    )(images, ty, tx, rho)


def solve(f, rho):
    where = lax.axis_index("gz").astype(jnp.int32).reshape(1)
    half = pltpu.VMEM((GROUPS, 5, 2, 8, 128), F32)
    return pl.pallas_call(
        solve_kernel,
        out_shape=(half, half),
        grid_spec=pltpu.PrefetchScalarGridSpec(
            num_scalar_prefetch=1,
            grid=(1,),
            in_specs=[
                VMEM,
                pl.BlockSpec((1, 8, 128), lambda i, w: (w[0], 0, 0)),
            ],
            out_specs=(VMEM, VMEM),
            scratch_shapes=[
                pltpu.VMEM((GROUPS, 2, 5, 8, 128), F32),
                pltpu.VMEM((GROUPS, 2, 5, 8, 128), F32),
            ],
        ),
        compiler_params=params(SOLVE_MIB),
        cost_estimate=cost(20000000, 6000000),
        name="solve",
    )(where, f, rho)


def inverse(pair, spec, keep, images, ty, tx, *start):
    if pair == 0:
        out_shape = (pltpu.VMEM((5, 2, 128, 128), F32),) * 2
    else:
        out_shape = (pltpu.VMEM((2, 5, 2, 128, 128), F32),)
    out_shape = (*out_shape, pltpu.VMEM((2, 8, 128), F32))
    args = (spec, keep, images, ty, tx, *start)
    return pl.pallas_call(
        functools.partial(inverse_kernel, pair=pair),
        out_shape=out_shape,
        in_specs=[HBM, HBM, HBM, VMEM, VMEM] + [VMEM] * len(start),
        out_specs=(VMEM,) * len(out_shape),
        scratch_shapes=[
            pltpu.VMEM((5, GROUPS, 2, 8, 128), F32),
            pltpu.VMEM((2, 5, 2, 128, 128), F32),
            pltpu.VMEM((5, GROUPS, 8, 128), F32),
            pltpu.SemaphoreType.DMA((5,)),
            pltpu.SemaphoreType.DMA,
            pltpu.SemaphoreType.DMA((5,)),
            pltpu.VMEM((2, 384, 256), BF16),
        ],
        compiler_params=plain(INVERSE_MIB),
        cost_estimate=cost(2_000_000_000, 6_000_000),
        name="inverse",
    )(*args)


def edge(first_sums, second_sums, upper, above):
    return pl.pallas_call(
        edge_kernel,
        out_shape=jax.ShapeDtypeStruct((128, 1, 128), F32),
        in_specs=[VMEM] * 4,
        out_specs=VMEM,
        compiler_params=plain(EDGE_MIB),
        cost_estimate=cost(2_000_000, 1_300_000),
        name="edge",
    )(first_sums, second_sums, upper, above)


def final(centre, positions, sums, below, s0, s1, upper, a0, a1):
    pair = pl.BlockSpec((2, 1, 2, 128, 128), lambda c: (0, c, 0, 0, 0))
    one = pl.BlockSpec((1, 2, 128, 128), lambda c: (c, 0, 0, 0))
    where = lax.axis_index("img").astype(jnp.int32).reshape(1)
    return pl.pallas_call(
        final_kernel,
        out_shape=jax.ShapeDtypeStruct((4, 5, 2, 128, 128), F32),
        grid=(5,),
        in_specs=[SMEM, SMEM, SMEM, VMEM, pair, one, one, pair, one, one],
        out_specs=pl.BlockSpec((4, 1, 2, 128, 128), lambda c: (0, c, 0, 0, 0)),
        scratch_shapes=[pltpu.VMEM((4, 5, 8, 128), F32)],
        compiler_params=params(FINAL_MIB),
        cost_estimate=cost(30000000, 8000000),
        name="final",
    )(centre, positions, where, sums, below, s0, s1, upper, a0, a1)


def local(images, centre, positions):
    forward_y, inverse_y, forward_x, inverse_x, rho = (jnp.asarray(t) for t in tables())
    rows = [(i, i + 1) for i in range(LOCAL - 1)]
    rows_back = [(b, a) for a, b in rows]
    f, keep = forward(images, forward_y, forward_x, rho)
    f = lax.all_to_all(f, "gz", 0, 0, tiled=True)
    u0, u1 = solve(f, rho)
    u0 = lax.all_to_all(u0, "gz", 0, 0, tiled=True)
    u1 = lax.all_to_all(u1, "gz", 0, 0, tiled=True)
    s0, s1, first_sums = inverse(0, u0, keep, images, inverse_y, inverse_x)
    a0 = lax.ppermute(s0, "img", rows_back)
    upper, second_sums = inverse(1, u1, keep, images, inverse_y, inverse_x, s1)
    a1 = lax.ppermute(s1, "img", rows_back)
    below = lax.ppermute(upper, "img", rows)
    part = edge(first_sums, second_sums, upper, a0)
    sums = lax.all_to_all(part, ("img", "gz"), 0, 0, tiled=True)
    return final(centre, positions, sums, below, s0, s1, upper, a0, a1)


def solution(mesh):
    in_specs = (P("img", None, "gz", None, None), P("img"), P("img"))
    out_specs = P("img", None, "gz", None, None)
    return jax.shard_map(
        local, mesh=mesh, in_specs=in_specs, out_specs=out_specs, check_vma=False
    )
```

```python
import functools

import jax
import jax.numpy as jnp
import numpy as np
from jax import lax
from jax.experimental import pallas as pl
from jax.experimental.pallas import tpu as pltpu
from jax.sharding import PartitionSpec as P

NX = 128
NY = 128
NZ = 64
GROUPS = 32
IMAGES = 16
LOCAL = 4
CELLS = 5.0 * NZ * NX * NY
SMOOTH = 64.0
EPS = 1e-6
KEEP = 1.0 - 1.0 / SMOOTH
SLOTS = 5
FORWARD_MIB = 60
SOLVE_MIB = 16
INVERSE_MIB = 8
EDGE_MIB = 4
FINAL_MIB = 16
F32 = jnp.float32
BF16 = jnp.bfloat16


def real_basis(length):
    k = np.arange(length)[:, None]
    x = np.arange(length)[None, :]
    angle = 2.0 * np.pi * ((k * x) % length) / length
    table = np.where(k <= length // 2, np.cos(angle), np.sin(angle)) * np.sqrt(2.0 / length)
    table[0] = 1.0 / np.sqrt(length)
    table[length // 2] = np.cos(np.pi * np.arange(length)) / np.sqrt(length)
    return table


def split_np(table):
    import ml_dtypes

    high = table.astype(ml_dtypes.bfloat16)
    low = (table - high.astype(np.float64)).astype(ml_dtypes.bfloat16)
    return high, low


def right_table(table):
    high, low = split_np(table)
    row = np.concatenate([high, low], axis=1)
    return np.concatenate([row, row], axis=0)


def left_table(table):
    high, low = split_np(table)
    return np.concatenate([high, high, low], axis=1)


@functools.cache
def tables():
    basis_x = real_basis(NX)
    basis_y = real_basis(NY)
    swap = np.arange(NX).reshape(-1, 2, 4)[:, ::-1].reshape(-1)
    forward_y = right_table(basis_y.T)
    inverse_y = right_table(basis_y)
    forward_x = np.stack([left_table(basis_x), left_table(basis_x[swap])])
    inverse_x = np.stack([left_table(basis_x.T), left_table(basis_x[swap].T)])
    device = np.arange(GROUPS)[:, None]
    row = np.arange(8)[None, :] % 4
    wave_x = 8 * (device % 16) + 4 * (device // 16) + row
    lam_x = 2.0 - 2.0 * np.cos(2.0 * np.pi * wave_x / NX)
    lam_y = 2.0 - 2.0 * np.cos(2.0 * np.pi * np.arange(NY) / NY)
    lam = lam_x[:, :, None] + lam_y[None, None, :]
    excess = 0.5 / SMOOTH + 0.5 * lam
    rho = 1.0 / (1.0 + excess + np.sqrt(excess * (excess + 2.0)))
    return forward_y, inverse_y, forward_x, inverse_x, rho.astype(np.float32)


def split(value):
    high = value.astype(BF16)
    low = (value - high.astype(F32)).astype(BF16)
    return high, low


def times_right(value, table):
    high, low = split(value)
    both = jnp.dot(jnp.concatenate([high, low], axis=1), table, preferred_element_type=F32)
    return both[:, :128] + both[:, 128:]


def shifts(f, axis):
    size = NX if axis == 0 else NY
    return pltpu.roll(f, size - 1, axis), pltpu.roll(f, 1, axis)


def local_drive(q):
    q1, q2, q3, q4, q5 = q
    both = q1 + q4
    s11 = q1 * q1 + (q2 * q2 + q3 * q3)
    d = q2 * q2
    s22 = q4 * q4 + (d + q5 * q5)
    half_trace = (s11 + s22) + (q1 * q4 - d)
    scale = (0.2 + 1.0 / SMOOTH) - 0.2 * half_trace
    third = half_trace * (1.0 / 3.0)
    h2, h3 = 0.5 * q2, 0.5 * q3
    rolled = {}
    for name, f in (("2", q2), ("3", q3), ("5", q5)):
        for axis in range(2):
            rolled[name, axis] = shifts(f, axis)

    def step(name, axis):
        after, before = rolled[name, axis]
        return after - before

    after, before = shifts(both + q1, 1)
    step_y = after - before
    after, before = shifts(both + q4, 0)
    step_x = after - before
    f1 = scale * q1 + (0.5 * (s11 - step("3", 1)) - third)
    f2 = q2 * (scale + 0.5 * both) + h3 * q5 + 0.25 * (step("3", 0) - step("5", 1))
    f3 = q3 * (scale - 0.5 * q4) + h2 * q5 + 0.25 * (step_y - step("2", 0))
    f4 = scale * q4 + (0.5 * (s22 + step("5", 0)) - third)
    f5 = q5 * (scale - 0.5 * q1) + h2 * q3 + 0.25 * (step("2", 1) - step_x)
    return (f1, f2, f3, f4, f5), rolled


def mixed(q):
    return q[1], q[0] - q[3], q[4], q[2]


def add_spread(f, r, factor):
    half = (0.5 * factor) * r[0]
    return (
        f[0] + half,
        f[1] - (0.25 * factor) * r[1],
        f[2] + (0.25 * factor) * r[2],
        f[3] - half,
        f[4] - (0.25 * factor) * r[3],
    )


def along_plane(f, x, y):
    return (6.0 + 1.0 / SMOOTH) * f - ((x[0] + x[1]) + (y[0] + y[1]))


def push(stack, slot, half, value):
    h, l = split(value)
    cols = slice(half * 128, half * 128 + 128)
    stack[slot, 0:128, cols] = h
    stack[slot, 128:256, cols] = l
    stack[slot, 256:384, cols] = h


def forward_kernel(img, ty, tx, rho_ref, out, keep, stack, spectrum):
    for i in range(2):
        qe = [img[i, c, 0] for c in range(5)]
        qo = [img[i, c, 1] for c in range(5)]
        re = mixed(qe)
        ro = mixed(qo)
        f, _ = local_drive(qe)
        for c, value in enumerate(add_spread(f, ro, 2.0)):
            push(stack, c, 0, times_right(value, ty[...]))
        f, rolled = local_drive(qo)
        total = [re[1] + along_plane(ro[1], shifts(ro[1], 0), shifts(ro[1], 1))]
        for r, name in ((0, "2"), (2, "5"), (3, "3")):
            total.append(re[r] + along_plane(ro[r], rolled[name, 0], rolled[name, 1]))
        total = (total[1], total[0], total[2], total[3])
        for c, value in enumerate(add_spread(f, total, -1.0)):
            push(stack, c, 1, times_right(value, ty[...]))
        for r in range(4):
            push(stack, 5 + r // 2, r % 2, times_right(re[r], ty[...]))
        for n in range(7):
            spectrum[i, n] = jnp.dot(tx[i], stack[n], preferred_element_type=F32)
    first = lax.broadcasted_iota(jnp.int32, (16, 8, 128), 1) < 4
    for part in range(2):
        rows = slice(part * 16, part * 16 + 16)
        rho = rho_ref[rows]
        beta = rho + 1.0 / rho
        back = (1.0 / SMOOTH) / beta

        def tile(n, half):
            cols = slice(half * 128, half * 128 + 128)
            a = spectrum[0, n, :, cols].reshape(16, 8, 128)
            b = spectrum[1, n, :, cols].reshape(16, 8, 128)
            return jnp.where(first, a, b) if part == 0 else jnp.where(first, b, a)

        g = [beta * tile(5 + r // 2, r % 2) for r in range(4)]
        ys = [tile(c, 0) for c in range(5)]
        ks = add_spread(ys, g, 1.0)
        for c in range(5):
            y = ys[c]
            out[rows, 0, 0, c] = beta * tile(c, 1) + y
            out[rows, 1, 0, c] = ks[c]
            keep[0, c, rows] = back * y


def solve_kernel(where, f, rho_ref, out, right, work):
    del where
    rho = rho_ref[0]
    sigma = rho * rho
    power = sigma
    for _ in range(5):
        power = power * power
    closing = 1.0 / (1.0 - power)
    shape = (2, 5, 8, 128)
    zero = jnp.zeros(shape, F32)
    sb = jnp.broadcast_to(sigma, shape)
    cb = jnp.broadcast_to(closing, shape)

    def ends(s, carry):
        v, u, p = carry
        r = f[s, 0] + f[lax.rem(s + 1, GROUPS), 1]
        right[s] = r
        return r + sb * v, u + p[None, None] * r, p * sigma

    v, u, _ = lax.fori_loop(0, GROUPS, ends, (zero, zero, jnp.ones((8, 128), F32)))
    u_last = u * cb

    def up(s, v):
        v = right[s] + sb * v
        work[s] = v
        return v

    lax.fori_loop(0, GROUPS, up, v * cb)
    gain = jnp.broadcast_to(sigma / (1.0 - sigma * sigma), shape)
    back = jnp.broadcast_to((1.0 / SMOOTH) / (rho + 1.0 / rho), shape)

    def put(s, slot, value):
        out[s, :, :, slot] = value

    def down(n, carry):
        u, after = carry
        s = GROUPS - 1 - n
        value = sb * u
        p = gain * (work[s] + value)
        put(s, 0, p)
        put(s + 1, 1, back * (p + after))
        return right[s] + value, p

    value = sb * u_last
    last = gain * (work[GROUPS - 1] + value)
    put(GROUPS - 1, 0, last)
    _, head = lax.fori_loop(1, GROUPS, down, (right[GROUPS - 1] + value, last))
    put(0, 1, back * (head + last))


def fold(value):
    return jnp.sum((value * value).reshape(16, 8, 128), axis=0)


def inverse_kernel(*refs, chosen):
    spec, keep, img, ty, tx = refs[:5]
    stack = refs[-1]
    if chosen[0] == 0:
        out = [refs[5]]
        start = None
    else:
        start, second, upper, sums = refs[5:9]
        out = [second, upper.at[0], upper.at[1]]
        sums[...] = jnp.zeros_like(sums)
    first = lax.broadcasted_iota(jnp.int32, (16, 8, 128), 1) < 4

    mixes = ((1, 0.5), (0, -0.25), (4, 0.25), (1, -0.5), (2, -0.25))
    for c in range(5):
        source, weight = mixes[c]
        weight = weight / SMOOTH
        if start is not None:
            last = (start[c, 0], start[c, 1])
        for n, image in enumerate(chosen):
            pair, i = image // 2, image % 2
            p_even, p_odd = spec[0:16, pair, c, 0], spec[16:32, pair, c, 0]
            w_even = spec[0:16, pair, c, 1] + keep[pair, c, 0:16]
            w_odd = spec[16:32, pair, c, 1] + keep[pair, c, 16:32]
            if i == 1:
                p_even, p_odd, w_even, w_odd = p_odd, p_even, w_odd, w_even
            slot = (c * len(chosen) + n) % SLOTS
            push(stack, slot, 0, jnp.where(first, w_even, w_odd).reshape(128, 128))
            push(stack, slot, 1, jnp.where(first, p_even, p_odd).reshape(128, 128))
            both = jnp.dot(tx[i], stack[slot], preferred_element_type=F32)
            even = KEEP * img[image, c, 0] + times_right(both[:, :128], ty[...])
            odd = times_right(both[:, 128:], ty[...])
            mix = img[image, source, 1]
            if c == 1:
                mix = mix - img[image, 3, 1]
            odd = KEEP * img[image, c, 1] + odd * (1.0 / SMOOTH) + weight * mix
            out[n][c, 0] = even
            out[n][c, 1] = odd
            if start is not None:
                sums[n] += fold(even - last[0]) + fold(odd - last[1])
                last = (even, odd)


def edge_kernel(sums, upper, above, out):
    edge = jnp.zeros((8, 128), F32)
    for c in range(5):
        for zz in range(2):
            edge = edge + fold(above[c, zz] - upper[1, c, zz])
    rows = [sums[0], sums[1], sums[2], edge]
    index = lax.broadcasted_iota(jnp.int32, (1, 128), 1)
    total = jnp.zeros((1, 128), F32)
    for g, row in enumerate(rows):
        total = jnp.where(index == g, jnp.sum(row), total)
    out[...] = jnp.broadcast_to(total, (128, 1, 128))


def final_kernel(
    centre,
    positions,
    where,
    sums,
    below_hbm,
    s0,
    s1,
    upper,
    a0,
    a1_hbm,
    out_hbm,
    below,
    a1,
    out,
    below_sem,
    a1_sem,
    out_sem,
):
    def fetch_below(c):
        return pltpu.make_async_copy(below_hbm.at[:, c], below.at[c], below_sem.at[c])

    def fetch_a1(c):
        return pltpu.make_async_copy(a1_hbm.at[c], a1.at[c], a1_sem.at[c])

    def store(c):
        return pltpu.make_async_copy(out.at[c], out_hbm.at[:, c], out_sem.at[c])

    for c in range(5):
        fetch_below(c).start()
        fetch_a1(c).start()
    arc = [jnp.zeros((8, 128), F32)]
    lane = lax.broadcasted_iota(jnp.int32, (1, 128), 1)
    for k in range(LOCAL):
        block = jnp.sum(sums[k * GROUPS : (k + 1) * GROUPS], axis=0)
        dist = jnp.sqrt(block * (1.0 / CELLS) + EPS)
        for g in range(4):
            if k * 4 + g < IMAGES - 1:
                value = jnp.sum(jnp.where(lane == g, dist, 0.0), axis=1, keepdims=True)
                arc.append(arc[-1] + jnp.broadcast_to(value, (8, 128)))
    base = where[0] * LOCAL - 2
    weights = {}
    for m in range(LOCAL):
        c = centre[m]
        tau = positions[m] * arc[-1]

        def pick(index):
            value = arc[0]
            for j in range(1, IMAGES):
                value = jnp.where(index == j, arc[j], value)
            return value

        a, b, d = pick(c - 1), pick(c), pick(c + 1)
        w = (
            (tau - b) * (tau - d) / ((a - b) * (a - d)),
            (tau - a) * (tau - d) / ((b - a) * (b - d)),
            (tau - a) * (tau - b) / ((d - a) * (d - b)),
        )
        for r in range(5):
            spot = base + m + r
            value = jnp.zeros((8, 128), F32)
            for n in range(3):
                value = jnp.where(c - 1 + n == spot, w[n], value)
            weights[m, r] = value

    for c in range(5):
        fetch_below(c).wait()
        fetch_a1(c).wait()
        lines = [below.at[c, 0], below.at[c, 1], s0.at[c], s1.at[c]]
        lines += [upper.at[0, c], upper.at[1, c], a0.at[c], a1.at[c]]
        for zz in range(2):
            for n in range(16):
                rows = slice(8 * n, 8 * n + 8)
                pieces = [line[zz, rows] for line in lines]
                for m in range(LOCAL):
                    acc = pieces[m] * weights[m, 0]
                    for r in range(1, 5):
                        acc = acc + pieces[m + r] * weights[m, r]
                    out[c, m, zz, rows] = acc
        store(c).start()
    for c in range(5):
        store(c).wait()


def whole(shape):
    return pl.BlockSpec(shape, lambda *_: (0,) * len(shape))


SMEM = pl.BlockSpec(memory_space=pltpu.SMEM)
VMEM = pl.BlockSpec(memory_space=pltpu.VMEM)
HBM = pl.BlockSpec(memory_space=pltpu.HBM)


def plain(mib):
    return pltpu.CompilerParams(vmem_limit_bytes=mib * 1024 * 1024)


def params(mib):
    return pltpu.CompilerParams(
        dimension_semantics=("arbitrary",), vmem_limit_bytes=min(int(mib * 1024 * 1024), 67_043_328)
    )


def cost(flops, moved):
    return pl.CostEstimate(flops=flops, bytes_accessed=moved, transcendentals=0)


def forward(images, ty, tx, rho):
    return pl.pallas_call(
        forward_kernel,
        out_shape=(
            jax.ShapeDtypeStruct((GROUPS, 2, 2, 5, 8, 128), F32),
            jax.ShapeDtypeStruct((2, 5, GROUPS, 8, 128), F32),
        ),
        grid=(2,),
        in_specs=[
            pl.BlockSpec((2, 5, 2, 128, 128), lambda p: (p, 0, 0, 0, 0)),
            whole((256, 256)),
            whole((2, 128, 384)),
            whole((GROUPS, 8, 128)),
        ],
        out_specs=(
            pl.BlockSpec((GROUPS, 2, 1, 5, 8, 128), lambda p: (0, 0, p, 0, 0, 0)),
            pl.BlockSpec((1, 5, GROUPS, 8, 128), lambda p: (p, 0, 0, 0, 0)),
        ),
        scratch_shapes=[
            pltpu.VMEM((7, 384, 256), BF16),
            pltpu.VMEM((2, 7, 128, 256), F32),
        ],
        compiler_params=params(FORWARD_MIB),
        cost_estimate=cost(3000000000, 9000000),
        name="forward",
    )(images, ty, tx, rho)


def solve(f, rho):
    where = lax.axis_index("gz").astype(jnp.int32).reshape(1)
    result = (GROUPS, 2, 5, 2, 8, 128)
    return pl.pallas_call(
        solve_kernel,
        out_shape=pltpu.VMEM(result, F32),
        grid_spec=pltpu.PrefetchScalarGridSpec(
            num_scalar_prefetch=1,
            grid=(1,),
            in_specs=[
                VMEM,
                pl.BlockSpec((1, 8, 128), lambda i, w: (w[0], 0, 0)),
            ],
            out_specs=VMEM,
            scratch_shapes=[
                pltpu.VMEM((GROUPS, 2, 5, 8, 128), F32),
                pltpu.VMEM((GROUPS, 2, 5, 8, 128), F32),
            ],
        ),
        compiler_params=params(SOLVE_MIB),
        cost_estimate=cost(20000000, 6000000),
        name="solve",
    )(where, f, rho)


def inverse(chosen, spec, keep, images, ty, tx, *start):
    one = pltpu.VMEM((5, 2, 128, 128), F32)
    if start:
        out_shape = (one, pltpu.VMEM((2, 5, 2, 128, 128), F32), pltpu.VMEM((3, 8, 128), F32))
    else:
        out_shape = (one,)
    args = (spec, keep, images, ty, tx, *start)
    count = len(chosen)
    return pl.pallas_call(
        functools.partial(inverse_kernel, chosen=chosen),
        out_shape=out_shape,
        in_specs=[VMEM] * len(args),
        out_specs=(VMEM,) * len(out_shape),
        scratch_shapes=[pltpu.VMEM((SLOTS, 384, 256), BF16)],
        compiler_params=plain(INVERSE_MIB),
        cost_estimate=cost(1_000_000_000 * count, 3_000_000 * count),
        name="inverse",
    )(*args)


def edge(sums, upper, above):
    return pl.pallas_call(
        edge_kernel,
        out_shape=jax.ShapeDtypeStruct((128, 1, 128), F32),
        in_specs=[VMEM] * 3,
        out_specs=VMEM,
        compiler_params=plain(EDGE_MIB),
        cost_estimate=cost(2_000_000, 1_300_000),
        name="edge",
    )(sums, upper, above)


def final(centre, positions, sums, below, s0, s1, upper, a0, a1):
    where = lax.axis_index("img").astype(jnp.int32).reshape(1)
    return pl.pallas_call(
        final_kernel,
        out_shape=jax.ShapeDtypeStruct((4, 5, 2, 128, 128), F32),
        in_specs=[SMEM, SMEM, SMEM, VMEM, HBM, VMEM, VMEM, VMEM, VMEM, HBM],
        out_specs=HBM,
        scratch_shapes=[
            pltpu.VMEM((5, 2, 2, 128, 128), F32),
            pltpu.VMEM((5, 2, 128, 128), F32),
            pltpu.VMEM((5, 4, 2, 128, 128), F32),
            pltpu.SemaphoreType.DMA((5,)),
            pltpu.SemaphoreType.DMA((5,)),
            pltpu.SemaphoreType.DMA((5,)),
        ],
        compiler_params=plain(FINAL_MIB),
        cost_estimate=cost(30_000_000, 8_000_000),
        name="final",
    )(centre, positions, where, sums, below, s0, s1, upper, a0, a1)


def local(images, centre, positions):
    forward_y, inverse_y, forward_x, inverse_x, rho = (jnp.asarray(t) for t in tables())
    rows = [(i, i + 1) for i in range(LOCAL - 1)]
    rows_back = [(b, a) for a, b in rows]
    f, keep = forward(images, forward_y, forward_x, rho)
    f = lax.all_to_all(f, "gz", 0, 0, tiled=True)
    u = solve(f, rho)
    u = lax.all_to_all(u, "gz", 0, 0, tiled=True)
    (s0,) = inverse((0,), u, keep, images, inverse_y, inverse_x)
    a0 = lax.ppermute(s0, "img", rows_back)
    s1, upper, sums = inverse((1, 2, 3), u, keep, images, inverse_y, inverse_x, s0)
    a1 = lax.ppermute(s1, "img", rows_back)
    below = lax.ppermute(upper, "img", rows)
    part = edge(sums, upper, a0)
    sums = lax.all_to_all(part, ("img", "gz"), 0, 0, tiled=True)
    return final(centre, positions, sums, below, s0, s1, upper, a0, a1)


def solution(mesh):
    in_specs = (P("img", None, "gz", None, None), P("img"), P("img"))
    out_specs = P("img", None, "gz", None, None)
    return jax.shard_map(
        local, mesh=mesh, in_specs=in_specs, out_specs=out_specs, check_vma=False
    )
```

```python
import functools

import jax
import jax.numpy as jnp
import numpy as np
from jax import lax
from jax.experimental import pallas as pl
from jax.experimental.pallas import tpu as pltpu
from jax.sharding import PartitionSpec as P

NX = 128
NY = 128
NZ = 64
GROUPS = 32
IMAGES = 16
LOCAL = 4
CELLS = 5.0 * NZ * NX * NY
SMOOTH = 64.0
EPS = 1e-6
KEEP = 1.0 - 1.0 / SMOOTH
SLOTS = 5
FORWARD_MIB = 56
SOLVE_MIB = 16
INVERSE_MIB = 8
EDGE_MIB = 4
FINAL_MIB = 16
F32 = jnp.float32
BF16 = jnp.bfloat16


def real_basis(length):
    k = np.arange(length)[:, None]
    x = np.arange(length)[None, :]
    angle = 2.0 * np.pi * ((k * x) % length) / length
    table = np.where(k <= length // 2, np.cos(angle), np.sin(angle)) * np.sqrt(2.0 / length)
    table[0] = 1.0 / np.sqrt(length)
    table[length // 2] = np.cos(np.pi * np.arange(length)) / np.sqrt(length)
    return table


def split_np(table):
    import ml_dtypes

    high = table.astype(ml_dtypes.bfloat16)
    low = (table - high.astype(np.float64)).astype(ml_dtypes.bfloat16)
    return high, low


def right_table(table):
    high, low = split_np(table)
    row = np.concatenate([high, low], axis=1)
    return np.concatenate([row, row], axis=0)


def left_table(table):
    high, low = split_np(table)
    return np.concatenate([high, high, low], axis=1)


@functools.cache
def tables():
    basis_x = real_basis(NX)
    basis_y = real_basis(NY)
    swap = np.arange(NX).reshape(-1, 2, 4)[:, ::-1].reshape(-1)
    forward_y = right_table(basis_y.T)
    inverse_y = right_table(basis_y)
    forward_x = np.stack([left_table(basis_x), left_table(basis_x[swap])])
    inverse_x = np.stack([left_table(basis_x.T), left_table(basis_x[swap].T)])
    device = np.arange(GROUPS)[:, None]
    row = np.arange(8)[None, :] % 4
    wave_x = 8 * (device % 16) + 4 * (device // 16) + row
    lam_x = 2.0 - 2.0 * np.cos(2.0 * np.pi * wave_x / NX)
    lam_y = 2.0 - 2.0 * np.cos(2.0 * np.pi * np.arange(NY) / NY)
    lam = lam_x[:, :, None] + lam_y[None, None, :]
    excess = 0.5 / SMOOTH + 0.5 * lam
    rho = 1.0 / (1.0 + excess + np.sqrt(excess * (excess + 2.0)))
    return forward_y, inverse_y, forward_x, inverse_x, rho.astype(np.float32)


def split(value):
    high = value.astype(BF16)
    low = (value - high.astype(F32)).astype(BF16)
    return high, low


def times_right(value, table):
    high, low = split(value)
    both = jnp.dot(jnp.concatenate([high, low], axis=1), table, preferred_element_type=F32)
    return both[:, :128] + both[:, 128:]


def shifts(f, axis):
    size = NX if axis == 0 else NY
    return pltpu.roll(f, size - 1, axis), pltpu.roll(f, 1, axis)


def local_drive(q):
    q1, q2, q3, q4, q5 = q
    both = q1 + q4
    s11 = q1 * q1 + (q2 * q2 + q3 * q3)
    d = q2 * q2
    s22 = q4 * q4 + (d + q5 * q5)
    half_trace = (s11 + s22) + (q1 * q4 - d)
    scale = (0.2 + 1.0 / SMOOTH) - 0.2 * half_trace
    third = half_trace * (1.0 / 3.0)
    h2, h3 = 0.5 * q2, 0.5 * q3
    rolled = {}
    for name, f in (("2", q2), ("3", q3), ("5", q5)):
        for axis in range(2):
            rolled[name, axis] = shifts(f, axis)

    def step(name, axis):
        after, before = rolled[name, axis]
        return after - before

    after, before = shifts(both + q1, 1)
    step_y = after - before
    after, before = shifts(both + q4, 0)
    step_x = after - before
    f1 = scale * q1 + (0.5 * (s11 - step("3", 1)) - third)
    f2 = q2 * (scale + 0.5 * both) + h3 * q5 + 0.25 * (step("3", 0) - step("5", 1))
    f3 = q3 * (scale - 0.5 * q4) + h2 * q5 + 0.25 * (step_y - step("2", 0))
    f4 = scale * q4 + (0.5 * (s22 + step("5", 0)) - third)
    f5 = q5 * (scale - 0.5 * q1) + h2 * q3 + 0.25 * (step("2", 1) - step_x)
    return (f1, f2, f3, f4, f5), rolled


def mixed(q):
    return q[1], q[0] - q[3], q[4], q[2]


def add_spread(f, r, factor):
    half = (0.5 * factor) * r[0]
    return (
        f[0] + half,
        f[1] - (0.25 * factor) * r[1],
        f[2] + (0.25 * factor) * r[2],
        f[3] - half,
        f[4] - (0.25 * factor) * r[3],
    )


def along_plane(f, x, y):
    return (6.0 + 1.0 / SMOOTH) * f - ((x[0] + x[1]) + (y[0] + y[1]))


def push(stack, slot, half, value):
    h, l = split(value)
    cols = slice(half * 128, half * 128 + 128)
    stack[slot, 0:128, cols] = h
    stack[slot, 128:256, cols] = l
    stack[slot, 256:384, cols] = h


def forward_kernel(where, img, ty, tx, rho_ref, out, keep, mine, stack, spectrum):
    pair = pl.program_id(0)
    mine[...] = rho_ref[where[0]]
    for i in range(2):
        qe = [img[i, c, 0] for c in range(5)]
        qo = [img[i, c, 1] for c in range(5)]
        re = mixed(qe)
        ro = mixed(qo)
        f, _ = local_drive(qe)
        for c, value in enumerate(add_spread(f, ro, 2.0)):
            push(stack, c, 0, times_right(value, ty[...]))
        f, rolled = local_drive(qo)
        total = [re[1] + along_plane(ro[1], shifts(ro[1], 0), shifts(ro[1], 1))]
        for r, name in ((0, "2"), (2, "5"), (3, "3")):
            total.append(re[r] + along_plane(ro[r], rolled[name, 0], rolled[name, 1]))
        total = (total[1], total[0], total[2], total[3])
        for c, value in enumerate(add_spread(f, total, -1.0)):
            push(stack, c, 1, times_right(value, ty[...]))
        for r in range(4):
            push(stack, 5 + r // 2, r % 2, times_right(re[r], ty[...]))
        for n in range(7):
            spectrum[i, n] = jnp.dot(tx[i], stack[n], preferred_element_type=F32)
    first = lax.broadcasted_iota(jnp.int32, (16, 8, 128), 1) < 4
    for part in range(2):
        rows = slice(part * 16, part * 16 + 16)
        rho = rho_ref[rows]
        beta = rho + 1.0 / rho
        back = (1.0 / SMOOTH) / beta

        def tile(n, half):
            cols = slice(half * 128, half * 128 + 128)
            a = spectrum[0, n, :, cols].reshape(16, 8, 128)
            b = spectrum[1, n, :, cols].reshape(16, 8, 128)
            return jnp.where(first, a, b) if part == 0 else jnp.where(first, b, a)

        g = [beta * tile(5 + r // 2, r % 2) for r in range(4)]
        ys = [tile(c, 0) for c in range(5)]
        ks = add_spread(ys, g, 1.0)
        for c in range(5):
            y = ys[c]
            out[rows, 0, pair, c] = beta * tile(c, 1) + y
            out[rows, 1, pair, c] = ks[c]
            keep[0, c, rows] = back * y


def solve_kernel(f, rho_ref, out, right, work):
    rho = rho_ref[...]
    sigma = rho * rho
    power = sigma
    for _ in range(5):
        power = power * power
    closing = 1.0 / (1.0 - power)
    shape = (2, 5, 8, 128)
    zero = jnp.zeros(shape, F32)
    sb = jnp.broadcast_to(sigma, shape)
    cb = jnp.broadcast_to(closing, shape)

    def ends(s, carry):
        v, u, p = carry
        r = f[s, 0] + f[lax.rem(s + 1, GROUPS), 1]
        right[s] = r
        return r + sb * v, u + p[None, None] * r, p * sigma

    v, u, _ = lax.fori_loop(0, GROUPS, ends, (zero, zero, jnp.ones((8, 128), F32)))
    u_last = u * cb

    def up(s, v):
        v = right[s] + sb * v
        work[s] = v
        return v

    lax.fori_loop(0, GROUPS, up, v * cb)
    gain = jnp.broadcast_to(sigma / (1.0 - sigma * sigma), shape)
    back = jnp.broadcast_to((1.0 / SMOOTH) / (rho + 1.0 / rho), shape)

    def put(s, slot, value):
        out[s, :, :, slot] = value

    def down(n, carry):
        u, after = carry
        s = GROUPS - 1 - n
        value = sb * u
        p = gain * (work[s] + value)
        put(s, 0, p)
        put(s + 1, 1, back * (p + after))
        return right[s] + value, p

    value = sb * u_last
    last = gain * (work[GROUPS - 1] + value)
    put(GROUPS - 1, 0, last)
    _, head = lax.fori_loop(1, GROUPS, down, (right[GROUPS - 1] + value, last))
    put(0, 1, back * (head + last))


def fold(value):
    return jnp.sum((value * value).reshape(16, 8, 128), axis=0)


def inverse_kernel(*refs, chosen):
    spec, keep, img, ty, tx = refs[:5]
    stack = refs[-1]
    if chosen[0] == 0:
        out = [refs[5]]
        start = None
    else:
        start, second, upper, sums = refs[5:9]
        out = [second, upper.at[0], upper.at[1]]
        sums[...] = jnp.zeros_like(sums)
    first = lax.broadcasted_iota(jnp.int32, (16, 8, 128), 1) < 4

    mixes = ((1, 0.5), (0, -0.25), (4, 0.25), (1, -0.5), (2, -0.25))
    for c in range(5):
        source, weight = mixes[c]
        weight = weight / SMOOTH
        if start is not None:
            last = (start[c, 0], start[c, 1])
        for n, image in enumerate(chosen):
            pair, i = image // 2, image % 2
            p_even, p_odd = spec[0:16, pair, c, 0], spec[16:32, pair, c, 0]
            w_even = spec[0:16, pair, c, 1] + keep[pair, c, 0:16]
            w_odd = spec[16:32, pair, c, 1] + keep[pair, c, 16:32]
            if i == 1:
                p_even, p_odd, w_even, w_odd = p_odd, p_even, w_odd, w_even
            slot = (c * len(chosen) + n) % SLOTS
            push(stack, slot, 0, jnp.where(first, w_even, w_odd).reshape(128, 128))
            push(stack, slot, 1, jnp.where(first, p_even, p_odd).reshape(128, 128))
            both = jnp.dot(tx[i], stack[slot], preferred_element_type=F32)
            even = KEEP * img[image, c, 0] + times_right(both[:, :128], ty[...])
            odd = times_right(both[:, 128:], ty[...])
            mix = img[image, source, 1]
            if c == 1:
                mix = mix - img[image, 3, 1]
            odd = KEEP * img[image, c, 1] + odd * (1.0 / SMOOTH) + weight * mix
            out[n][c, 0] = even
            out[n][c, 1] = odd
            if start is not None:
                sums[n] += fold(even - last[0]) + fold(odd - last[1])
                last = (even, odd)


def edge_kernel(sums, upper, above, out):
    edge = jnp.zeros((8, 128), F32)
    for c in range(5):
        for zz in range(2):
            edge = edge + fold(above[c, zz] - upper[1, c, zz])
    rows = [sums[0], sums[1], sums[2], edge]
    index = lax.broadcasted_iota(jnp.int32, (1, 128), 1)
    total = jnp.zeros((1, 128), F32)
    for g, row in enumerate(rows):
        total = jnp.where(index == g, jnp.sum(row), total)
    out[...] = jnp.broadcast_to(total, (128, 1, 128))


def final_kernel(
    centre,
    positions,
    where,
    sums,
    below_hbm,
    s0,
    s1,
    upper,
    a0,
    a1_hbm,
    out_hbm,
    below,
    a1,
    out,
    below_sem,
    a1_sem,
    out_sem,
):
    def fetch_below(c):
        return pltpu.make_async_copy(below_hbm.at[:, c], below.at[c], below_sem.at[c])

    def fetch_a1(c):
        return pltpu.make_async_copy(a1_hbm.at[c], a1.at[c], a1_sem.at[c])

    def store(c):
        return pltpu.make_async_copy(out.at[c], out_hbm.at[:, c], out_sem.at[c])

    for c in range(5):
        fetch_below(c).start()
        fetch_a1(c).start()
    arc = [jnp.zeros((8, 128), F32)]
    lane = lax.broadcasted_iota(jnp.int32, (1, 128), 1)
    for k in range(LOCAL):
        block = jnp.sum(sums[k * GROUPS : (k + 1) * GROUPS], axis=0)
        dist = jnp.sqrt(block * (1.0 / CELLS) + EPS)
        for g in range(4):
            if k * 4 + g < IMAGES - 1:
                value = jnp.sum(jnp.where(lane == g, dist, 0.0), axis=1, keepdims=True)
                arc.append(arc[-1] + jnp.broadcast_to(value, (8, 128)))
    base = where[0] * LOCAL - 2
    weights = {}
    for m in range(LOCAL):
        c = centre[m]
        tau = positions[m] * arc[-1]

        def pick(index):
            value = arc[0]
            for j in range(1, IMAGES):
                value = jnp.where(index == j, arc[j], value)
            return value

        a, b, d = pick(c - 1), pick(c), pick(c + 1)
        w = (
            (tau - b) * (tau - d) / ((a - b) * (a - d)),
            (tau - a) * (tau - d) / ((b - a) * (b - d)),
            (tau - a) * (tau - b) / ((d - a) * (d - b)),
        )
        for r in range(5):
            spot = base + m + r
            value = jnp.zeros((8, 128), F32)
            for n in range(3):
                value = jnp.where(c - 1 + n == spot, w[n], value)
            weights[m, r] = value

    for c in range(5):
        fetch_below(c).wait()
        fetch_a1(c).wait()
        lines = [below.at[c, 0], below.at[c, 1], s0.at[c], s1.at[c]]
        lines += [upper.at[0, c], upper.at[1, c], a0.at[c], a1.at[c]]
        for zz in range(2):
            for n in range(16):
                rows = slice(8 * n, 8 * n + 8)
                pieces = [line[zz, rows] for line in lines]
                for m in range(LOCAL):
                    acc = pieces[m] * weights[m, 0]
                    for r in range(1, 5):
                        acc = acc + pieces[m + r] * weights[m, r]
                    out[c, m, zz, rows] = acc
        store(c).start()
    for c in range(5):
        store(c).wait()


def whole(shape):
    return pl.BlockSpec(shape, lambda *_: (0,) * len(shape))


SMEM = pl.BlockSpec(memory_space=pltpu.SMEM)
VMEM = pl.BlockSpec(memory_space=pltpu.VMEM)
HBM = pl.BlockSpec(memory_space=pltpu.HBM)


def plain(mib):
    return pltpu.CompilerParams(vmem_limit_bytes=mib * 1024 * 1024)


def params(mib):
    return pltpu.CompilerParams(
        dimension_semantics=("arbitrary",), vmem_limit_bytes=min(int(mib * 1024 * 1024), 67_043_328)
    )


def cost(flops, moved):
    return pl.CostEstimate(flops=flops, bytes_accessed=moved, transcendentals=0)


def forward(images, ty, tx, rho):
    where = lax.axis_index("gz").astype(jnp.int32).reshape(1)
    return pl.pallas_call(
        forward_kernel,
        out_shape=(
            pltpu.VMEM((GROUPS, 2, 2, 5, 8, 128), F32),
            jax.ShapeDtypeStruct((2, 5, GROUPS, 8, 128), F32),
            pltpu.VMEM((8, 128), F32),
        ),
        grid=(2,),
        in_specs=[
            SMEM,
            pl.BlockSpec((2, 5, 2, 128, 128), lambda p: (p, 0, 0, 0, 0)),
            whole((256, 256)),
            whole((2, 128, 384)),
            whole((GROUPS, 8, 128)),
        ],
        out_specs=(
            VMEM,
            pl.BlockSpec((1, 5, GROUPS, 8, 128), lambda p: (p, 0, 0, 0, 0)),
            VMEM,
        ),
        scratch_shapes=[
            pltpu.VMEM((7, 384, 256), BF16),
            pltpu.VMEM((2, 7, 128, 256), F32),
        ],
        compiler_params=params(FORWARD_MIB),
        cost_estimate=cost(3000000000, 9000000),
        name="forward",
    )(where, images, ty, tx, rho)


def solve(f, rho):
    return pl.pallas_call(
        solve_kernel,
        out_shape=pltpu.VMEM((GROUPS, 2, 5, 2, 8, 128), F32),
        in_specs=[VMEM, VMEM],
        out_specs=VMEM,
        scratch_shapes=[
            pltpu.VMEM((GROUPS, 2, 5, 8, 128), F32),
            pltpu.VMEM((GROUPS, 2, 5, 8, 128), F32),
        ],
        compiler_params=plain(SOLVE_MIB),
        cost_estimate=cost(20_000_000, 6_000_000),
        name="solve",
    )(f, rho)


def inverse(chosen, spec, keep, images, ty, tx, *start):
    one = pltpu.VMEM((5, 2, 128, 128), F32)
    if start:
        out_shape = (one, pltpu.VMEM((2, 5, 2, 128, 128), F32), pltpu.VMEM((3, 8, 128), F32))
    else:
        out_shape = (one,)
    args = (spec, keep, images, ty, tx, *start)
    count = len(chosen)
    return pl.pallas_call(
        functools.partial(inverse_kernel, chosen=chosen),
        out_shape=out_shape,
        in_specs=[VMEM] * len(args),
        out_specs=(VMEM,) * len(out_shape),
        scratch_shapes=[pltpu.VMEM((SLOTS, 384, 256), BF16)],
        compiler_params=plain(INVERSE_MIB),
        cost_estimate=cost(1_000_000_000 * count, 3_000_000 * count),
        name="inverse",
    )(*args)


def edge(sums, upper, above):
    return pl.pallas_call(
        edge_kernel,
        out_shape=pltpu.VMEM((128, 1, 128), F32),
        in_specs=[VMEM] * 3,
        out_specs=VMEM,
        compiler_params=plain(EDGE_MIB),
        cost_estimate=cost(2_000_000, 1_300_000),
        name="edge",
    )(sums, upper, above)


def final(centre, positions, sums, below, s0, s1, upper, a0, a1):
    where = lax.axis_index("img").astype(jnp.int32).reshape(1)
    return pl.pallas_call(
        final_kernel,
        out_shape=jax.ShapeDtypeStruct((4, 5, 2, 128, 128), F32),
        in_specs=[SMEM, SMEM, SMEM, VMEM, HBM, VMEM, VMEM, VMEM, VMEM, HBM],
        out_specs=HBM,
        scratch_shapes=[
            pltpu.VMEM((5, 2, 2, 128, 128), F32),
            pltpu.VMEM((5, 2, 128, 128), F32),
            pltpu.VMEM((5, 4, 2, 128, 128), F32),
            pltpu.SemaphoreType.DMA((5,)),
            pltpu.SemaphoreType.DMA((5,)),
            pltpu.SemaphoreType.DMA((5,)),
        ],
        compiler_params=plain(FINAL_MIB),
        cost_estimate=cost(30_000_000, 8_000_000),
        name="final",
    )(centre, positions, where, sums, below, s0, s1, upper, a0, a1)


def local(images, centre, positions):
    forward_y, inverse_y, forward_x, inverse_x, rho = (jnp.asarray(t) for t in tables())
    rows = [(i, i + 1) for i in range(LOCAL - 1)]
    rows_back = [(b, a) for a, b in rows]
    f, keep, mine = forward(images, forward_y, forward_x, rho)
    f = lax.all_to_all(f, "gz", 0, 0, tiled=True)
    u = solve(f, mine)
    u = lax.all_to_all(u, "gz", 0, 0, tiled=True)
    (s0,) = inverse((0,), u, keep, images, inverse_y, inverse_x)
    a0 = lax.ppermute(s0, "img", rows_back)
    s1, upper, sums = inverse((1, 2, 3), u, keep, images, inverse_y, inverse_x, s0)
    a1 = lax.ppermute(s1, "img", rows_back)
    below = lax.ppermute(upper, "img", rows)
    part = edge(sums, upper, a0)
    sums = lax.all_to_all(part, ("img", "gz"), 0, 0, tiled=True)
    return final(centre, positions, sums, below, s0, s1, upper, a0, a1)


def solution(mesh):
    in_specs = (P("img", None, "gz", None, None), P("img"), P("img"))
    out_specs = P("img", None, "gz", None, None)
    return jax.shard_map(
        local, mesh=mesh, in_specs=in_specs, out_specs=out_specs, check_vma=False
    )
```

```python
import functools

import jax
import jax.numpy as jnp
import numpy as np
from jax import lax
from jax.experimental import pallas as pl
from jax.experimental.pallas import tpu as pltpu
from jax.sharding import PartitionSpec as P

NX = 128
NY = 128
NZ = 64
GROUPS = 32
IMAGES = 16
LOCAL = 4
CELLS = 5.0 * NZ * NX * NY
SMOOTH = 64.0
EPS = 1e-6
KEEP = 1.0 - 1.0 / SMOOTH
SLOTS = 5
FORWARD_MIB = 56
SOLVE_MIB = 16
INVERSE_MIB = 8
EDGE_MIB = 4
FINAL_MIB = 16
F32 = jnp.float32
BF16 = jnp.bfloat16


def real_basis(length):
    k = np.arange(length)[:, None]
    x = np.arange(length)[None, :]
    angle = 2.0 * np.pi * ((k * x) % length) / length
    table = np.where(k <= length // 2, np.cos(angle), np.sin(angle)) * np.sqrt(2.0 / length)
    table[0] = 1.0 / np.sqrt(length)
    table[length // 2] = np.cos(np.pi * np.arange(length)) / np.sqrt(length)
    return table


def split_np(table):
    import ml_dtypes

    high = table.astype(ml_dtypes.bfloat16)
    low = (table - high.astype(np.float64)).astype(ml_dtypes.bfloat16)
    return high, low


def right_table(table):
    high, low = split_np(table)
    row = np.concatenate([high, low], axis=1)
    return np.concatenate([row, row], axis=0)


def left_table(table):
    high, low = split_np(table)
    return np.concatenate([high, high, low], axis=1)


@functools.cache
def tables():
    basis_x = real_basis(NX)
    basis_y = real_basis(NY)
    swap = np.arange(NX).reshape(-1, 2, 4)[:, ::-1].reshape(-1)
    forward_y = right_table(0.25 * basis_y.T)
    inverse_y = right_table(basis_y)
    forward_x = np.stack([left_table(basis_x), left_table(basis_x[swap])])
    inverse_x = np.stack([left_table(basis_x.T), left_table(basis_x[swap].T)])
    device = np.arange(GROUPS)[:, None]
    row = np.arange(8)[None, :] % 4
    wave_x = 8 * (device % 16) + 4 * (device // 16) + row
    lam_x = 2.0 - 2.0 * np.cos(2.0 * np.pi * wave_x / NX)
    lam_y = 2.0 - 2.0 * np.cos(2.0 * np.pi * np.arange(NY) / NY)
    lam = lam_x[:, :, None] + lam_y[None, None, :]
    excess = 0.5 / SMOOTH + 0.5 * lam
    rho = 1.0 / (1.0 + excess + np.sqrt(excess * (excess + 2.0)))
    return forward_y, inverse_y, forward_x, inverse_x, rho.astype(np.float32)


def split(value):
    high = value.astype(BF16)
    low = (value - high.astype(F32)).astype(BF16)
    return high, low


def times_right(value, table):
    high, low = split(value)
    both = jnp.dot(jnp.concatenate([high, low], axis=1), table, preferred_element_type=F32)
    return both[:, :128] + both[:, 128:]


def shifts(f, axis):
    size = NX if axis == 0 else NY
    return pltpu.roll(f, size - 1, axis), pltpu.roll(f, 1, axis)


def local_drive(q):
    q1, q2, q3, q4, q5 = q
    d1, d2, d3, d4, d5 = (f + f for f in q)
    square = d2 * q2
    s11 = d1 * q1 + (square + d3 * q3)
    s22 = d4 * q4 + (square + d5 * q5)
    trace = (s11 + s22) + (d1 * q4 - square)
    scale = 4.0 * (0.2 + 1.0 / SMOOTH) - 0.4 * trace
    third = trace * (2.0 / 3.0)
    rolled = {}
    for name, f in (("2", q2), ("3", q3), ("5", q5)):
        for axis in range(2):
            rolled[name, axis] = shifts(f, axis)

    def step(name, axis):
        after, before = rolled[name, axis]
        return after - before

    after, before = shifts(d1 + q4, 1)
    step_y = after - before
    after, before = shifts(q1 + d4, 0)
    step_x = after - before
    f1 = scale * q1 + ((s11 - third) - 2.0 * step("3", 1))
    f2 = q2 * (scale + (d1 + d4)) + (d3 * q5 + (step("3", 0) - step("5", 1)))
    f3 = q3 * (scale - d4) + (d2 * q5 + (step_y - step("2", 0)))
    f4 = scale * q4 + ((s22 - third) + 2.0 * step("5", 0))
    f5 = q5 * (scale - d1) + (d2 * q3 + (step("2", 1) - step_x))
    return (f1, f2, f3, f4, f5), rolled


def mixed(q):
    return q[1], q[0] - q[3], q[4], q[2]


def add_spread(f, r, factor):
    whole_part = [value if factor in (1, -1) else abs(factor) * value for value in r]
    twice = (2.0 * abs(factor)) * r[0]
    if factor < 0:
        return (
            f[0] - twice,
            f[1] + whole_part[1],
            f[2] - whole_part[2],
            f[3] + twice,
            f[4] + whole_part[3],
        )
    return (
        f[0] + twice,
        f[1] - whole_part[1],
        f[2] + whole_part[2],
        f[3] - twice,
        f[4] - whole_part[3],
    )


def along_plane(f, x, y):
    return (6.0 + 1.0 / SMOOTH) * f - ((x[0] + x[1]) + (y[0] + y[1]))


def push(stack, slot, half, value):
    h, l = split(value)
    cols = slice(half * 128, half * 128 + 128)
    stack[slot, 0:128, cols] = h
    stack[slot, 128:256, cols] = l
    stack[slot, 256:384, cols] = h


def forward_kernel(
    where,
    img_hbm,
    ty_hbm,
    tx_hbm,
    rho_hbm,
    out,
    keep,
    mine,
    img,
    img_sem,
    ty,
    tx,
    rho_ref,
    table_sem,
    stack,
    spectrum,
):
    def fetch(n):
        return pltpu.make_async_copy(img_hbm.at[n], img.at[n], img_sem.at[n])

    small = [
        pltpu.make_async_copy(source, target, table_sem.at[n])
        for n, (source, target) in enumerate(((ty_hbm, ty), (tx_hbm, tx), (rho_hbm, rho_ref)))
    ]
    fetch(0).start()
    for copy in small:
        copy.start()
    for n in range(1, LOCAL):
        fetch(n).start()
    for copy in small:
        copy.wait()
    mine[...] = rho_ref[where[0]]

    @pl.loop(0, 2)
    def _(pair):
        for i in range(2):
            fetch(2 * pair + i).wait()
        for i in range(2):
            qe = [img[2 * pair + i, c, 0] for c in range(5)]
            qo = [img[2 * pair + i, c, 1] for c in range(5)]
            re = mixed(qe)
            ro = mixed(qo)
            f, _ = local_drive(qe)
            for c, value in enumerate(add_spread(f, ro, 2)):
                push(stack, c, 0, times_right(value, ty[...]))
            f, rolled = local_drive(qo)
            total = [re[1] + along_plane(ro[1], shifts(ro[1], 0), shifts(ro[1], 1))]
            for r, name in ((0, "2"), (2, "5"), (3, "3")):
                total.append(re[r] + along_plane(ro[r], rolled[name, 0], rolled[name, 1]))
            total = (total[1], total[0], total[2], total[3])
            for c, value in enumerate(add_spread(f, total, -1)):
                push(stack, c, 1, times_right(value, ty[...]))
            for r in range(4):
                push(stack, 5 + r // 2, r % 2, times_right(re[r], ty[...]))
            for n in range(7):
                spectrum[i, n] = jnp.dot(tx[i], stack[n], preferred_element_type=F32)
        first = lax.broadcasted_iota(jnp.int32, (16, 8, 128), 1) < 4
        for part in range(2):
            rows = slice(part * 16, part * 16 + 16)
            rho = rho_ref[rows]
            beta = rho + 1.0 / rho
            back = (1.0 / SMOOTH) / beta

            def tile(n, half):
                cols = slice(half * 128, half * 128 + 128)
                a = spectrum[0, n, :, cols].reshape(16, 8, 128)
                b = spectrum[1, n, :, cols].reshape(16, 8, 128)
                return jnp.where(first, a, b) if part == 0 else jnp.where(first, b, a)

            g = [beta * tile(5 + r // 2, r % 2) for r in range(4)]
            ys = [tile(c, 0) for c in range(5)]
            ks = add_spread(ys, g, 1)
            for c in range(5):
                y = ys[c]
                out[rows, 0, pair, c] = beta * tile(c, 1) + y
                out[rows, 1, pair, c] = ks[c]
                keep[pair, c, rows] = back * y


def solve_kernel(f, rho_ref, out, right, work):
    rho = rho_ref[...]
    sigma = rho * rho
    power = sigma
    for _ in range(5):
        power = power * power
    closing = 1.0 / (1.0 - power)
    shape = (2, 5, 8, 128)
    zero = jnp.zeros(shape, F32)
    sb = jnp.broadcast_to(sigma, shape)
    cb = jnp.broadcast_to(closing, shape)

    def ends(s, carry):
        v, u, p = carry
        r = f[s, 0] + f[lax.rem(s + 1, GROUPS), 1]
        right[s] = r
        return r + sb * v, u + p[None, None] * r, p * sigma

    v, u, _ = lax.fori_loop(0, GROUPS, ends, (zero, zero, jnp.ones((8, 128), F32)))
    u_last = u * cb

    def up(s, v):
        v = right[s] + sb * v
        work[s] = v
        return v

    lax.fori_loop(0, GROUPS, up, v * cb)
    gain = jnp.broadcast_to(sigma / (1.0 - sigma * sigma), shape)
    back = jnp.broadcast_to((1.0 / SMOOTH) / (rho + 1.0 / rho), shape)

    def put(s, slot, value):
        out[s, :, :, slot] = value

    def down(n, carry):
        u, after = carry
        s = GROUPS - 1 - n
        value = sb * u
        p = gain * (work[s] + value)
        put(s, 0, p)
        put(s + 1, 1, back * (p + after))
        return right[s] + value, p

    value = sb * u_last
    last = gain * (work[GROUPS - 1] + value)
    put(GROUPS - 1, 0, last)
    _, head = lax.fori_loop(1, GROUPS, down, (right[GROUPS - 1] + value, last))
    put(0, 1, back * (head + last))


def fold(value):
    return jnp.sum((value * value).reshape(16, 8, 128), axis=0)


def inverse_kernel(*refs, chosen):
    spec, keep, img, ty, tx = refs[:5]
    stack = refs[-1]
    if chosen[0] == 0:
        out = [refs[5]]
        start = None
    else:
        start, second, upper, sums = refs[5:9]
        out = [second, upper.at[0], upper.at[1]]
        sums[...] = jnp.zeros_like(sums)
    first = lax.broadcasted_iota(jnp.int32, (16, 8, 128), 1) < 4

    mixes = ((1, 0.5), (0, -0.25), (4, 0.25), (1, -0.5), (2, -0.25))
    for c in range(5):
        source, weight = mixes[c]
        weight = weight / SMOOTH
        if start is not None:
            last = (start[c, 0], start[c, 1])
        for n, image in enumerate(chosen):
            pair, i = image // 2, image % 2
            p_even, p_odd = spec[0:16, pair, c, 0], spec[16:32, pair, c, 0]
            w_even = spec[0:16, pair, c, 1] + keep[pair, c, 0:16]
            w_odd = spec[16:32, pair, c, 1] + keep[pair, c, 16:32]
            if i == 1:
                p_even, p_odd, w_even, w_odd = p_odd, p_even, w_odd, w_even
            slot = (c * len(chosen) + n) % SLOTS
            push(stack, slot, 0, jnp.where(first, w_even, w_odd).reshape(128, 128))
            push(stack, slot, 1, jnp.where(first, p_even, p_odd).reshape(128, 128))
            both = jnp.dot(tx[i], stack[slot], preferred_element_type=F32)
            even = KEEP * img[image, c, 0] + times_right(both[:, :128], ty[...])
            odd = times_right(both[:, 128:], ty[...])
            mix = img[image, source, 1]
            if c == 1:
                mix = mix - img[image, 3, 1]
            odd = KEEP * img[image, c, 1] + odd * (1.0 / SMOOTH) + weight * mix
            out[n][c, 0] = even
            out[n][c, 1] = odd
            if start is not None:
                sums[n] += fold(even - last[0]) + fold(odd - last[1])
                last = (even, odd)


def edge_kernel(sums, upper, above, out):
    edge = jnp.zeros((8, 128), F32)
    for c in range(5):
        for zz in range(2):
            edge = edge + fold(above[c, zz] - upper[1, c, zz])
    rows = [sums[0], sums[1], sums[2], edge]
    index = lax.broadcasted_iota(jnp.int32, (1, 128), 1)
    total = jnp.zeros((1, 128), F32)
    for g, row in enumerate(rows):
        total = jnp.where(index == g, jnp.sum(row), total)
    out[...] = jnp.broadcast_to(total, (128, 1, 128))


def final_kernel(
    centre,
    positions,
    where,
    sums,
    below_hbm,
    s0,
    s1,
    upper,
    a0,
    a1_hbm,
    out_hbm,
    below,
    a1,
    out,
    below_sem,
    a1_sem,
    out_sem,
):
    def fetch_below(c):
        return pltpu.make_async_copy(below_hbm.at[:, c], below.at[c], below_sem.at[c])

    def fetch_a1(c):
        return pltpu.make_async_copy(a1_hbm.at[c], a1.at[c], a1_sem.at[c])

    def store(c):
        return pltpu.make_async_copy(out.at[c], out_hbm.at[:, c], out_sem.at[c])

    for c in range(5):
        fetch_below(c).start()
        fetch_a1(c).start()
    arc = [jnp.zeros((8, 128), F32)]
    lane = lax.broadcasted_iota(jnp.int32, (1, 128), 1)
    for k in range(LOCAL):
        block = jnp.sum(sums[k * GROUPS : (k + 1) * GROUPS], axis=0)
        dist = jnp.sqrt(block * (1.0 / CELLS) + EPS)
        for g in range(4):
            if k * 4 + g < IMAGES - 1:
                value = jnp.sum(jnp.where(lane == g, dist, 0.0), axis=1, keepdims=True)
                arc.append(arc[-1] + jnp.broadcast_to(value, (8, 128)))
    base = where[0] * LOCAL - 2
    weights = {}
    for m in range(LOCAL):
        c = centre[m]
        tau = positions[m] * arc[-1]

        def pick(index):
            value = arc[0]
            for j in range(1, IMAGES):
                value = jnp.where(index == j, arc[j], value)
            return value

        a, b, d = pick(c - 1), pick(c), pick(c + 1)
        w = (
            (tau - b) * (tau - d) / ((a - b) * (a - d)),
            (tau - a) * (tau - d) / ((b - a) * (b - d)),
            (tau - a) * (tau - b) / ((d - a) * (d - b)),
        )
        for r in range(5):
            spot = base + m + r
            value = jnp.zeros((8, 128), F32)
            for n in range(3):
                value = jnp.where(c - 1 + n == spot, w[n], value)
            weights[m, r] = value

    for c in range(5):
        fetch_below(c).wait()
        fetch_a1(c).wait()
        lines = [below.at[c, 0], below.at[c, 1], s0.at[c], s1.at[c]]
        lines += [upper.at[0, c], upper.at[1, c], a0.at[c], a1.at[c]]
        for zz in range(2):
            for n in range(16):
                rows = slice(8 * n, 8 * n + 8)
                pieces = [line[zz, rows] for line in lines]
                for m in range(LOCAL):
                    acc = pieces[m] * weights[m, 0]
                    for r in range(1, 5):
                        acc = acc + pieces[m + r] * weights[m, r]
                    out[c, m, zz, rows] = acc
        store(c).start()
    for c in range(5):
        store(c).wait()


SMEM = pl.BlockSpec(memory_space=pltpu.SMEM)
VMEM = pl.BlockSpec(memory_space=pltpu.VMEM)
HBM = pl.BlockSpec(memory_space=pltpu.HBM)


def plain(mib):
    return pltpu.CompilerParams(vmem_limit_bytes=mib * 1024 * 1024)


def cost(flops, moved):
    return pl.CostEstimate(flops=flops, bytes_accessed=moved, transcendentals=0)


def forward(images, ty, tx, rho):
    where = lax.axis_index("gz").astype(jnp.int32).reshape(1)
    return pl.pallas_call(
        forward_kernel,
        out_shape=(
            pltpu.VMEM((GROUPS, 2, 2, 5, 8, 128), F32),
            pltpu.VMEM((2, 5, GROUPS, 8, 128), F32),
            pltpu.VMEM((8, 128), F32),
        ),
        in_specs=[SMEM, HBM, HBM, HBM, HBM],
        out_specs=(VMEM,) * 3,
        scratch_shapes=[
            pltpu.VMEM((LOCAL, 5, 2, 128, 128), F32),
            pltpu.SemaphoreType.DMA((LOCAL,)),
            pltpu.VMEM((256, 256), BF16),
            pltpu.VMEM((2, 128, 384), BF16),
            pltpu.VMEM((GROUPS, 8, 128), F32),
            pltpu.SemaphoreType.DMA((3,)),
            pltpu.VMEM((7, 384, 256), BF16),
            pltpu.VMEM((2, 7, 128, 256), F32),
        ],
        compiler_params=plain(FORWARD_MIB),
        cost_estimate=cost(3_000_000_000, 9_000_000),
        name="forward",
    )(where, images, ty, tx, rho)


def solve(f, rho):
    return pl.pallas_call(
        solve_kernel,
        out_shape=pltpu.VMEM((GROUPS, 2, 5, 2, 8, 128), F32),
        in_specs=[VMEM, VMEM],
        out_specs=VMEM,
        scratch_shapes=[
            pltpu.VMEM((GROUPS, 2, 5, 8, 128), F32),
            pltpu.VMEM((GROUPS, 2, 5, 8, 128), F32),
        ],
        compiler_params=plain(SOLVE_MIB),
        cost_estimate=cost(20_000_000, 6_000_000),
        name="solve",
    )(f, rho)


def inverse(chosen, spec, keep, images, ty, tx, *start):
    one = pltpu.VMEM((5, 2, 128, 128), F32)
    if start:
        out_shape = (one, pltpu.VMEM((2, 5, 2, 128, 128), F32), pltpu.VMEM((3, 8, 128), F32))
    else:
        out_shape = (one,)
    args = (spec, keep, images, ty, tx, *start)
    count = len(chosen)
    return pl.pallas_call(
        functools.partial(inverse_kernel, chosen=chosen),
        out_shape=out_shape,
        in_specs=[VMEM] * len(args),
        out_specs=(VMEM,) * len(out_shape),
        scratch_shapes=[pltpu.VMEM((SLOTS, 384, 256), BF16)],
        compiler_params=plain(INVERSE_MIB),
        cost_estimate=cost(1_000_000_000 * count, 3_000_000 * count),
        name="inverse",
    )(*args)


def edge(sums, upper, above):
    return pl.pallas_call(
        edge_kernel,
        out_shape=pltpu.VMEM((128, 1, 128), F32),
        in_specs=[VMEM] * 3,
        out_specs=VMEM,
        compiler_params=plain(EDGE_MIB),
        cost_estimate=cost(2_000_000, 1_300_000),
        name="edge",
    )(sums, upper, above)


def final(centre, positions, sums, below, s0, s1, upper, a0, a1):
    where = lax.axis_index("img").astype(jnp.int32).reshape(1)
    return pl.pallas_call(
        final_kernel,
        out_shape=jax.ShapeDtypeStruct((4, 5, 2, 128, 128), F32),
        in_specs=[SMEM, SMEM, SMEM, VMEM, HBM, VMEM, VMEM, VMEM, VMEM, HBM],
        out_specs=HBM,
        scratch_shapes=[
            pltpu.VMEM((5, 2, 2, 128, 128), F32),
            pltpu.VMEM((5, 2, 128, 128), F32),
            pltpu.VMEM((5, 4, 2, 128, 128), F32),
            pltpu.SemaphoreType.DMA((5,)),
            pltpu.SemaphoreType.DMA((5,)),
            pltpu.SemaphoreType.DMA((5,)),
        ],
        compiler_params=plain(FINAL_MIB),
        cost_estimate=cost(30_000_000, 8_000_000),
        name="final",
    )(centre, positions, where, sums, below, s0, s1, upper, a0, a1)


def local(images, centre, positions):
    forward_y, inverse_y, forward_x, inverse_x, rho = (jnp.asarray(t) for t in tables())
    rows = [(i, i + 1) for i in range(LOCAL - 1)]
    rows_back = [(b, a) for a, b in rows]
    f, keep, mine = forward(images, forward_y, forward_x, rho)
    f = lax.all_to_all(f, "gz", 0, 0, tiled=True)
    u = solve(f, mine)
    u = lax.all_to_all(u, "gz", 0, 0, tiled=True)
    (s0,) = inverse((0,), u, keep, images, inverse_y, inverse_x)
    a0 = lax.ppermute(s0, "img", rows_back)
    s1, upper, sums = inverse((1, 2, 3), u, keep, images, inverse_y, inverse_x, s0)
    a1 = lax.ppermute(s1, "img", rows_back)
    below = lax.ppermute(upper, "img", rows)
    part = edge(sums, upper, a0)
    sums = lax.all_to_all(part, ("img", "gz"), 0, 0, tiled=True)
    return final(centre, positions, sums, below, s0, s1, upper, a0, a1)


def solution(mesh):
    in_specs = (P("img", None, "gz", None, None), P("img"), P("img"))
    out_specs = P("img", None, "gz", None, None)
    return jax.shard_map(
        local, mesh=mesh, in_specs=in_specs, out_specs=out_specs, check_vma=False
    )
```

```python
import functools

import jax
import jax.numpy as jnp
import numpy as np
from jax import lax
from jax.experimental import pallas as pl
from jax.experimental.pallas import tpu as pltpu
from jax.sharding import PartitionSpec as P

NX = 128
NY = 128
NZ = 64
GROUPS = 32
IMAGES = 16
LOCAL = 4
CELLS = 5.0 * NZ * NX * NY
SMOOTH = 64.0
EPS = 1e-6
KEEP = 1.0 - 1.0 / SMOOTH
SLOTS = 5
FORWARD_MIB = 56
SOLVE_MIB = 16
INVERSE_MIB = 8
EDGE_MIB = 4
FINAL_MIB = 16
F32 = jnp.float32
BF16 = jnp.bfloat16


def real_basis(length):
    k = np.arange(length)[:, None]
    x = np.arange(length)[None, :]
    angle = 2.0 * np.pi * ((k * x) % length) / length
    table = np.where(k <= length // 2, np.cos(angle), np.sin(angle)) * np.sqrt(2.0 / length)
    table[0] = 1.0 / np.sqrt(length)
    table[length // 2] = np.cos(np.pi * np.arange(length)) / np.sqrt(length)
    return table


def split_np(table):
    import ml_dtypes

    high = table.astype(ml_dtypes.bfloat16)
    low = (table - high.astype(np.float64)).astype(ml_dtypes.bfloat16)
    return high, low


def right_table(table):
    high, low = split_np(table)
    row = np.concatenate([high, low], axis=1)
    return np.concatenate([row, row], axis=0)


def left_table(table):
    high, low = split_np(table)
    return np.concatenate([high, high, low], axis=1)


@functools.cache
def tables():
    basis_x = real_basis(NX)
    basis_y = real_basis(NY)
    swap = np.arange(NX).reshape(-1, 2, 4)[:, ::-1].reshape(-1)
    forward_y = right_table(0.25 * basis_y.T)
    inverse_y = right_table(basis_y)
    forward_x = np.stack([left_table(basis_x), left_table(basis_x[swap])])
    inverse_x = np.stack([left_table(basis_x.T), left_table(basis_x[swap].T)])
    device = np.arange(GROUPS)[:, None]
    row = np.arange(8)[None, :] % 4
    wave_x = 8 * (device % 16) + 4 * (device // 16) + row
    lam_x = 2.0 - 2.0 * np.cos(2.0 * np.pi * wave_x / NX)
    lam_y = 2.0 - 2.0 * np.cos(2.0 * np.pi * np.arange(NY) / NY)
    lam = lam_x[:, :, None] + lam_y[None, None, :]
    excess = 0.5 / SMOOTH + 0.5 * lam
    rho = 1.0 / (1.0 + excess + np.sqrt(excess * (excess + 2.0)))
    return forward_y, inverse_y, forward_x, inverse_x, rho.astype(np.float32)


def split(value):
    high = value.astype(BF16)
    low = (value - high.astype(F32)).astype(BF16)
    return high, low


def times_right(value, table):
    high, low = split(value)
    both = jnp.dot(jnp.concatenate([high, low], axis=1), table, preferred_element_type=F32)
    return both[:, :128] + both[:, 128:]


def shifts(f, axis):
    size = NX if axis == 0 else NY
    return pltpu.roll(f, size - 1, axis), pltpu.roll(f, 1, axis)


def local_drive(q):
    q1, q2, q3, q4, q5 = q
    d1, d2, d3, d4, d5 = (f + f for f in q)
    square = d2 * q2
    s11 = d1 * q1 + (square + d3 * q3)
    s22 = d4 * q4 + (square + d5 * q5)
    trace = (s11 + s22) + (d1 * q4 - square)
    scale = 4.0 * (0.2 + 1.0 / SMOOTH) - 0.4 * trace
    third = trace * (2.0 / 3.0)
    rolled = {}
    for name, f in (("2", q2), ("3", q3), ("5", q5)):
        for axis in range(2):
            rolled[name, axis] = shifts(f, axis)

    def step(name, axis):
        after, before = rolled[name, axis]
        return after - before

    after, before = shifts(d1 + q4, 1)
    step_y = after - before
    after, before = shifts(q1 + d4, 0)
    step_x = after - before
    f1 = scale * q1 + ((s11 - third) - 2.0 * step("3", 1))
    f2 = q2 * (scale + (d1 + d4)) + (d3 * q5 + (step("3", 0) - step("5", 1)))
    f3 = q3 * (scale - d4) + (d2 * q5 + (step_y - step("2", 0)))
    f4 = scale * q4 + ((s22 - third) + 2.0 * step("5", 0))
    f5 = q5 * (scale - d1) + (d2 * q3 + (step("2", 1) - step_x))
    return (f1, f2, f3, f4, f5), rolled


def mixed(q):
    return q[1], q[0] - q[3], q[4], q[2]


def add_spread(f, r, factor):
    whole_part = [value if factor in (1, -1) else abs(factor) * value for value in r]
    twice = (2.0 * abs(factor)) * r[0]
    if factor < 0:
        return (
            f[0] - twice,
            f[1] + whole_part[1],
            f[2] - whole_part[2],
            f[3] + twice,
            f[4] + whole_part[3],
        )
    return (
        f[0] + twice,
        f[1] - whole_part[1],
        f[2] + whole_part[2],
        f[3] - twice,
        f[4] - whole_part[3],
    )


def along_plane(f, x, y):
    return (6.0 + 1.0 / SMOOTH) * f - ((x[0] + x[1]) + (y[0] + y[1]))


def push(stack, slot, half, value):
    h, l = split(value)
    cols = slice(half * 128, half * 128 + 128)
    stack[slot, 0:128, cols] = h
    stack[slot, 128:256, cols] = l
    stack[slot, 256:384, cols] = h


def forward_kernel(
    where,
    img_hbm,
    ty_hbm,
    tx_hbm,
    rho_hbm,
    out,
    keep,
    mine,
    img,
    img_sem,
    ty,
    tx,
    rho_ref,
    table_sem,
    stack,
    spectrum,
):
    def fetch(n):
        return pltpu.make_async_copy(img_hbm.at[n], img.at[n], img_sem.at[n])

    small = [
        pltpu.make_async_copy(source, target, table_sem.at[n])
        for n, (source, target) in enumerate(((ty_hbm, ty), (tx_hbm, tx), (rho_hbm, rho_ref)))
    ]
    fetch(0).start()
    for copy in small:
        copy.start()
    for n in range(1, LOCAL):
        fetch(n).start()
    for copy in small:
        copy.wait()
    mine[...] = rho_ref[where[0]]

    @pl.loop(0, 2)
    def _(pair):
        for i in range(2):
            fetch(2 * pair + i).wait()
        for i in range(2):
            qe = [img[2 * pair + i, c, 0] for c in range(5)]
            qo = [img[2 * pair + i, c, 1] for c in range(5)]
            re = mixed(qe)
            ro = mixed(qo)
            f, _ = local_drive(qe)
            for c, value in enumerate(add_spread(f, ro, 2)):
                push(stack, c, 0, times_right(value, ty[...]))
            f, rolled = local_drive(qo)
            total = [re[1] + along_plane(ro[1], shifts(ro[1], 0), shifts(ro[1], 1))]
            for r, name in ((0, "2"), (2, "5"), (3, "3")):
                total.append(re[r] + along_plane(ro[r], rolled[name, 0], rolled[name, 1]))
            total = (total[1], total[0], total[2], total[3])
            for c, value in enumerate(add_spread(f, total, -1)):
                push(stack, c, 1, times_right(value, ty[...]))
            for r in range(4):
                push(stack, 5 + r // 2, r % 2, times_right(re[r], ty[...]))
            for n in range(7):
                spectrum[i, n] = jnp.dot(tx[i], stack[n], preferred_element_type=F32)
        first = lax.broadcasted_iota(jnp.int32, (16, 8, 128), 1) < 4
        for part in range(2):
            rows = slice(part * 16, part * 16 + 16)
            rho = rho_ref[rows]
            beta = rho + 1.0 / rho
            back = (1.0 / SMOOTH) / beta

            def tile(n, half):
                cols = slice(half * 128, half * 128 + 128)
                a = spectrum[0, n, :, cols].reshape(16, 8, 128)
                b = spectrum[1, n, :, cols].reshape(16, 8, 128)
                return jnp.where(first, a, b) if part == 0 else jnp.where(first, b, a)

            g = [beta * tile(5 + r // 2, r % 2) for r in range(4)]
            ys = [tile(c, 0) for c in range(5)]
            ks = add_spread(ys, g, 1)
            for c in range(5):
                y = ys[c]
                out[rows, 0, pair, c] = beta * tile(c, 1) + y
                out[rows, 1, pair, c] = ks[c]
                keep[pair, c, rows] = back * y


def solve_kernel(f, rho_ref, out, right, work):
    rho = rho_ref[...]
    sigma = rho * rho
    shape = (2, 5, 8, 128)
    sb = jnp.broadcast_to(sigma, shape)
    powers = [sigma]
    for _ in range(GROUPS - 1):
        powers.append(powers[-1] * sigma)
    closing = jnp.broadcast_to(1.0 / (1.0 - powers[-1]), shape)
    v = u = None
    for s in range(GROUPS):
        r = f[s, 0] + f[(s + 1) % GROUPS, 1]
        right[s] = r
        v = r if s == 0 else r + sb * v
        u = r if s == 0 else u + powers[s - 1] * r
        work[s] = v
    v_last = v * closing
    u = u * closing
    gain = jnp.broadcast_to(sigma / (1.0 - sigma * sigma), shape)
    back = jnp.broadcast_to((1.0 / SMOOTH) / (rho + 1.0 / rho), shape)
    after = last = None
    for s in reversed(range(GROUPS)):
        value = sb * u
        p = gain * ((work[s] + powers[s] * v_last) + value)
        out[s, :, :, 0] = p
        if after is None:
            last = p
        else:
            out[s + 1, :, :, 1] = back * (p + after)
        u = right[s] + value
        after = p
    out[0, :, :, 1] = back * (after + last)


def fold(value):
    return jnp.sum((value * value).reshape(16, 8, 128), axis=0)


def inverse_kernel(*refs, chosen):
    spec, keep, img, ty, tx = refs[:5]
    stack = refs[-1]
    if chosen[0] == 0:
        out = [refs[5]]
        start = None
    else:
        start, second, upper, sums = refs[5:9]
        out = [second, upper.at[0], upper.at[1]]
        sums[...] = jnp.zeros_like(sums)
    first = lax.broadcasted_iota(jnp.int32, (16, 8, 128), 1) < 4

    mixes = ((1, 0.5), (0, -0.25), (4, 0.25), (1, -0.5), (2, -0.25))
    for c in range(5):
        source, weight = mixes[c]
        weight = weight / SMOOTH
        if start is not None:
            last = (start[c, 0], start[c, 1])
        for n, image in enumerate(chosen):
            pair, i = image // 2, image % 2
            p_even, p_odd = spec[0:16, pair, c, 0], spec[16:32, pair, c, 0]
            w_even = spec[0:16, pair, c, 1] + keep[pair, c, 0:16]
            w_odd = spec[16:32, pair, c, 1] + keep[pair, c, 16:32]
            if i == 1:
                p_even, p_odd, w_even, w_odd = p_odd, p_even, w_odd, w_even
            slot = (c * len(chosen) + n) % SLOTS
            push(stack, slot, 0, jnp.where(first, w_even, w_odd).reshape(128, 128))
            push(stack, slot, 1, jnp.where(first, p_even, p_odd).reshape(128, 128))
            both = jnp.dot(tx[i], stack[slot], preferred_element_type=F32)
            even = KEEP * img[image, c, 0] + times_right(both[:, :128], ty[...])
            odd = times_right(both[:, 128:], ty[...])
            mix = img[image, source, 1]
            if c == 1:
                mix = mix - img[image, 3, 1]
            odd = KEEP * img[image, c, 1] + odd * (1.0 / SMOOTH) + weight * mix
            out[n][c, 0] = even
            out[n][c, 1] = odd
            if start is not None:
                sums[n] += fold(even - last[0]) + fold(odd - last[1])
                last = (even, odd)


def edge_kernel(sums, upper, above, out):
    edge = jnp.zeros((8, 128), F32)
    for c in range(5):
        for zz in range(2):
            edge = edge + fold(above[c, zz] - upper[1, c, zz])
    rows = [sums[0], sums[1], sums[2], edge]
    index = lax.broadcasted_iota(jnp.int32, (1, 128), 1)
    total = jnp.zeros((1, 128), F32)
    for g, row in enumerate(rows):
        total = jnp.where(index == g, jnp.sum(row), total)
    out[...] = jnp.broadcast_to(total, (128, 1, 128))


def final_kernel(
    centre,
    positions,
    where,
    sums,
    below_hbm,
    s0,
    s1,
    upper,
    a0,
    a1_hbm,
    out_hbm,
    below,
    a1,
    out,
    below_sem,
    a1_sem,
    out_sem,
):
    def fetch_below(c):
        return pltpu.make_async_copy(below_hbm.at[:, c], below.at[c], below_sem.at[c])

    def fetch_a1(c):
        return pltpu.make_async_copy(a1_hbm.at[c], a1.at[c], a1_sem.at[c])

    def store(c):
        return pltpu.make_async_copy(out.at[c], out_hbm.at[:, c], out_sem.at[c])

    for c in range(5):
        fetch_below(c).start()
        fetch_a1(c).start()
    arc = [jnp.zeros((8, 128), F32)]
    lane = lax.broadcasted_iota(jnp.int32, (1, 128), 1)
    for k in range(LOCAL):
        block = jnp.sum(sums[k * GROUPS : (k + 1) * GROUPS], axis=0)
        dist = jnp.sqrt(block * (1.0 / CELLS) + EPS)
        for g in range(4):
            if k * 4 + g < IMAGES - 1:
                value = jnp.sum(jnp.where(lane == g, dist, 0.0), axis=1, keepdims=True)
                arc.append(arc[-1] + jnp.broadcast_to(value, (8, 128)))
    base = where[0] * LOCAL - 2
    weights = {}
    for m in range(LOCAL):
        c = centre[m]
        tau = positions[m] * arc[-1]

        def pick(index):
            value = arc[0]
            for j in range(1, IMAGES):
                value = jnp.where(index == j, arc[j], value)
            return value

        a, b, d = pick(c - 1), pick(c), pick(c + 1)
        w = (
            (tau - b) * (tau - d) / ((a - b) * (a - d)),
            (tau - a) * (tau - d) / ((b - a) * (b - d)),
            (tau - a) * (tau - b) / ((d - a) * (d - b)),
        )
        for r in range(5):
            spot = base + m + r
            value = jnp.zeros((8, 128), F32)
            for n in range(3):
                value = jnp.where(c - 1 + n == spot, w[n], value)
            weights[m, r] = value

    for c in range(5):
        fetch_below(c).wait()
        fetch_a1(c).wait()
        lines = [below.at[c, 0], below.at[c, 1], s0.at[c], s1.at[c]]
        lines += [upper.at[0, c], upper.at[1, c], a0.at[c], a1.at[c]]
        for zz in range(2):
            for n in range(16):
                rows = slice(8 * n, 8 * n + 8)
                pieces = [line[zz, rows] for line in lines]
                for m in range(LOCAL):
                    acc = pieces[m] * weights[m, 0]
                    for r in range(1, 5):
                        acc = acc + pieces[m + r] * weights[m, r]
                    out[c, m, zz, rows] = acc
        store(c).start()
    for c in range(5):
        store(c).wait()


SMEM = pl.BlockSpec(memory_space=pltpu.SMEM)
VMEM = pl.BlockSpec(memory_space=pltpu.VMEM)
HBM = pl.BlockSpec(memory_space=pltpu.HBM)


def plain(mib):
    return pltpu.CompilerParams(vmem_limit_bytes=mib * 1024 * 1024)


def cost(flops, moved):
    return pl.CostEstimate(flops=flops, bytes_accessed=moved, transcendentals=0)


def forward(images, ty, tx, rho):
    where = lax.axis_index("gz").astype(jnp.int32).reshape(1)
    return pl.pallas_call(
        forward_kernel,
        out_shape=(
            pltpu.VMEM((GROUPS, 2, 2, 5, 8, 128), F32),
            pltpu.VMEM((2, 5, GROUPS, 8, 128), F32),
            pltpu.VMEM((8, 128), F32),
        ),
        in_specs=[SMEM, HBM, HBM, HBM, HBM],
        out_specs=(VMEM,) * 3,
        scratch_shapes=[
            pltpu.VMEM((LOCAL, 5, 2, 128, 128), F32),
            pltpu.SemaphoreType.DMA((LOCAL,)),
            pltpu.VMEM((256, 256), BF16),
            pltpu.VMEM((2, 128, 384), BF16),
            pltpu.VMEM((GROUPS, 8, 128), F32),
            pltpu.SemaphoreType.DMA((3,)),
            pltpu.VMEM((7, 384, 256), BF16),
            pltpu.VMEM((2, 7, 128, 256), F32),
        ],
        compiler_params=plain(FORWARD_MIB),
        cost_estimate=cost(3_000_000_000, 9_000_000),
        name="forward",
    )(where, images, ty, tx, rho)


def solve(f, rho):
    return pl.pallas_call(
        solve_kernel,
        out_shape=pltpu.VMEM((GROUPS, 2, 5, 2, 8, 128), F32),
        in_specs=[VMEM, VMEM],
        out_specs=VMEM,
        scratch_shapes=[
            pltpu.VMEM((GROUPS, 2, 5, 8, 128), F32),
            pltpu.VMEM((GROUPS, 2, 5, 8, 128), F32),
        ],
        compiler_params=plain(SOLVE_MIB),
        cost_estimate=cost(20_000_000, 6_000_000),
        name="solve",
    )(f, rho)


def inverse(chosen, spec, keep, images, ty, tx, *start):
    one = pltpu.VMEM((5, 2, 128, 128), F32)
    if start:
        out_shape = (one, pltpu.VMEM((2, 5, 2, 128, 128), F32), pltpu.VMEM((3, 8, 128), F32))
    else:
        out_shape = (one,)
    args = (spec, keep, images, ty, tx, *start)
    count = len(chosen)
    return pl.pallas_call(
        functools.partial(inverse_kernel, chosen=chosen),
        out_shape=out_shape,
        in_specs=[VMEM] * len(args),
        out_specs=(VMEM,) * len(out_shape),
        scratch_shapes=[pltpu.VMEM((SLOTS, 384, 256), BF16)],
        compiler_params=plain(INVERSE_MIB),
        cost_estimate=cost(1_000_000_000 * count, 3_000_000 * count),
        name="inverse",
    )(*args)


def edge(sums, upper, above):
    return pl.pallas_call(
        edge_kernel,
        out_shape=pltpu.VMEM((128, 1, 128), F32),
        in_specs=[VMEM] * 3,
        out_specs=VMEM,
        compiler_params=plain(EDGE_MIB),
        cost_estimate=cost(2_000_000, 1_300_000),
        name="edge",
    )(sums, upper, above)


def final(centre, positions, sums, below, s0, s1, upper, a0, a1):
    where = lax.axis_index("img").astype(jnp.int32).reshape(1)
    return pl.pallas_call(
        final_kernel,
        out_shape=jax.ShapeDtypeStruct((4, 5, 2, 128, 128), F32),
        in_specs=[SMEM, SMEM, SMEM, VMEM, HBM, VMEM, VMEM, VMEM, VMEM, HBM],
        out_specs=HBM,
        scratch_shapes=[
            pltpu.VMEM((5, 2, 2, 128, 128), F32),
            pltpu.VMEM((5, 2, 128, 128), F32),
            pltpu.VMEM((5, 4, 2, 128, 128), F32),
            pltpu.SemaphoreType.DMA((5,)),
            pltpu.SemaphoreType.DMA((5,)),
            pltpu.SemaphoreType.DMA((5,)),
        ],
        compiler_params=plain(FINAL_MIB),
        cost_estimate=cost(30_000_000, 8_000_000),
        name="final",
    )(centre, positions, where, sums, below, s0, s1, upper, a0, a1)


def local(images, centre, positions):
    forward_y, inverse_y, forward_x, inverse_x, rho = (jnp.asarray(t) for t in tables())
    rows = [(i, i + 1) for i in range(LOCAL - 1)]
    rows_back = [(b, a) for a, b in rows]
    f, keep, mine = forward(images, forward_y, forward_x, rho)
    f = lax.all_to_all(f, "gz", 0, 0, tiled=True)
    u = solve(f, mine)
    u = lax.all_to_all(u, "gz", 0, 0, tiled=True)
    (s0,) = inverse((0,), u, keep, images, inverse_y, inverse_x)
    a0 = lax.ppermute(s0, "img", rows_back)
    s1, upper, sums = inverse((1, 2, 3), u, keep, images, inverse_y, inverse_x, s0)
    a1 = lax.ppermute(s1, "img", rows_back)
    below = lax.ppermute(upper, "img", rows)
    part = edge(sums, upper, a0)
    sums = lax.all_to_all(part, ("img", "gz"), 0, 0, tiled=True)
    return final(centre, positions, sums, below, s0, s1, upper, a0, a1)


def solution(mesh):
    in_specs = (P("img", None, "gz", None, None), P("img"), P("img"))
    out_specs = P("img", None, "gz", None, None)
    return jax.shard_map(
        local, mesh=mesh, in_specs=in_specs, out_specs=out_specs, check_vma=False
    )
```

```python
import functools

import jax
import jax.numpy as jnp
import numpy as np
from jax import lax
from jax.experimental import pallas as pl
from jax.experimental.pallas import tpu as pltpu
from jax.sharding import PartitionSpec as P

NX = 128
NY = 128
NZ = 64
GROUPS = 32
IMAGES = 16
LOCAL = 4
CELLS = 5.0 * NZ * NX * NY
SMOOTH = 64.0
EPS = 1e-6
KEEP = 1.0 - 1.0 / SMOOTH
SLOTS = 5
FORWARD_MIB = 56
SOLVE_MIB = 16
INVERSE_MIB = 8
EDGE_MIB = 4
FINAL_MIB = 16
F32 = jnp.float32
BF16 = jnp.bfloat16


def real_basis(length):
    k = np.arange(length)[:, None]
    x = np.arange(length)[None, :]
    angle = 2.0 * np.pi * ((k * x) % length) / length
    table = np.where(k <= length // 2, np.cos(angle), np.sin(angle)) * np.sqrt(2.0 / length)
    table[0] = 1.0 / np.sqrt(length)
    table[length // 2] = np.cos(np.pi * np.arange(length)) / np.sqrt(length)
    return table


def split_np(table):
    import ml_dtypes

    high = table.astype(ml_dtypes.bfloat16)
    low = (table - high.astype(np.float64)).astype(ml_dtypes.bfloat16)
    return high, low


def right_table(table):
    high, low = split_np(table)
    row = np.concatenate([high, low], axis=1)
    return np.concatenate([row, row], axis=0)


def left_table(table):
    high, low = split_np(table)
    return np.concatenate([high, high, low], axis=1)


@functools.cache
def tables():
    basis_x = real_basis(NX)
    basis_y = real_basis(NY)
    swap = np.arange(NX).reshape(-1, 2, 4)[:, ::-1].reshape(-1)
    forward_y = right_table(0.25 * basis_y.T)
    inverse_y = right_table(basis_y)
    forward_x = np.stack([left_table(basis_x), left_table(basis_x[swap])])
    inverse_x = np.stack([left_table(basis_x.T), left_table(basis_x[swap].T)])
    device = np.arange(GROUPS)[:, None]
    row = np.arange(8)[None, :] % 4
    wave_x = 8 * (device % 16) + 4 * (device // 16) + row
    lam_x = 2.0 - 2.0 * np.cos(2.0 * np.pi * wave_x / NX)
    lam_y = 2.0 - 2.0 * np.cos(2.0 * np.pi * np.arange(NY) / NY)
    lam = lam_x[:, :, None] + lam_y[None, None, :]
    excess = 0.5 / SMOOTH + 0.5 * lam
    rho = 1.0 / (1.0 + excess + np.sqrt(excess * (excess + 2.0)))
    return forward_y, inverse_y, forward_x, inverse_x, rho.astype(np.float32)


def split(value):
    high = value.astype(BF16)
    low = (value - high.astype(F32)).astype(BF16)
    return high, low


def times_right(value, table):
    high, low = split(value)
    both = jnp.dot(jnp.concatenate([high, low], axis=1), table, preferred_element_type=F32)
    return both[:, :128] + both[:, 128:]


def shifts(f, axis):
    size = NX if axis == 0 else NY
    return pltpu.roll(f, size - 1, axis), pltpu.roll(f, 1, axis)


def local_drive(q):
    q1, q2, q3, q4, q5 = q
    d1, d2, d3, d4, d5 = (f + f for f in q)
    square = d2 * q2
    s11 = d1 * q1 + (square + d3 * q3)
    s22 = d4 * q4 + (square + d5 * q5)
    trace = (s11 + s22) + (d1 * q4 - square)
    scale = 4.0 * (0.2 + 1.0 / SMOOTH) - 0.4 * trace
    third = trace * (2.0 / 3.0)
    rolled = {}
    for name, f in (("2", q2), ("3", q3), ("5", q5)):
        for axis in range(2):
            rolled[name, axis] = shifts(f, axis)

    def step(name, axis):
        after, before = rolled[name, axis]
        return after - before

    after, before = shifts(d1 + q4, 1)
    step_y = after - before
    after, before = shifts(q1 + d4, 0)
    step_x = after - before
    f1 = scale * q1 + ((s11 - third) - 2.0 * step("3", 1))
    f2 = q2 * (scale + (d1 + d4)) + (d3 * q5 + (step("3", 0) - step("5", 1)))
    f3 = q3 * (scale - d4) + (d2 * q5 + (step_y - step("2", 0)))
    f4 = scale * q4 + ((s22 - third) + 2.0 * step("5", 0))
    f5 = q5 * (scale - d1) + (d2 * q3 + (step("2", 1) - step_x))
    return (f1, f2, f3, f4, f5), rolled


def mixed(q):
    return q[1], q[0] - q[3], q[4], q[2]


def add_spread(f, r, factor):
    whole_part = [value if factor in (1, -1) else abs(factor) * value for value in r]
    twice = (2.0 * abs(factor)) * r[0]
    if factor < 0:
        return (
            f[0] - twice,
            f[1] + whole_part[1],
            f[2] - whole_part[2],
            f[3] + twice,
            f[4] + whole_part[3],
        )
    return (
        f[0] + twice,
        f[1] - whole_part[1],
        f[2] + whole_part[2],
        f[3] - twice,
        f[4] - whole_part[3],
    )


def along_plane(f, x, y):
    return (6.0 + 1.0 / SMOOTH) * f - ((x[0] + x[1]) + (y[0] + y[1]))


def push(stack, slot, half, value):
    h, l = split(value)
    cols = slice(half * 128, half * 128 + 128)
    stack[slot, 0:128, cols] = h
    stack[slot, 128:256, cols] = l
    stack[slot, 256:384, cols] = h


def forward_kernel(
    where,
    img_hbm,
    ty_hbm,
    tx_hbm,
    rho_hbm,
    out,
    keep,
    mine,
    img,
    img_sem,
    ty,
    tx,
    rho_ref,
    table_sem,
    stack,
    spectrum,
):
    def fetch(n):
        return pltpu.make_async_copy(img_hbm.at[n], img.at[n], img_sem.at[n])

    small = [
        pltpu.make_async_copy(source, target, table_sem.at[n])
        for n, (source, target) in enumerate(((ty_hbm, ty), (tx_hbm, tx), (rho_hbm, rho_ref)))
    ]
    fetch(0).start()
    for copy in small:
        copy.start()
    for n in range(1, LOCAL):
        fetch(n).start()
    for copy in small:
        copy.wait()
    mine[...] = rho_ref[where[0]]

    @pl.loop(0, 2)
    def _(pair):
        for i in range(2):
            fetch(2 * pair + i).wait()
        for i in range(2):
            qe = [img[2 * pair + i, c, 0] for c in range(5)]
            qo = [img[2 * pair + i, c, 1] for c in range(5)]
            re = mixed(qe)
            ro = mixed(qo)
            f, _ = local_drive(qe)
            for c, value in enumerate(add_spread(f, ro, 2)):
                push(stack, c, 0, times_right(value, ty[...]))
            f, rolled = local_drive(qo)
            total = [re[1] + along_plane(ro[1], shifts(ro[1], 0), shifts(ro[1], 1))]
            for r, name in ((0, "2"), (2, "5"), (3, "3")):
                total.append(re[r] + along_plane(ro[r], rolled[name, 0], rolled[name, 1]))
            total = (total[1], total[0], total[2], total[3])
            for c, value in enumerate(add_spread(f, total, -1)):
                push(stack, c, 1, times_right(value, ty[...]))
            for r in range(4):
                push(stack, 5 + r // 2, r % 2, times_right(re[r], ty[...]))
            for n in range(7):
                spectrum[i, n] = jnp.dot(tx[i], stack[n], preferred_element_type=F32)
        first = lax.broadcasted_iota(jnp.int32, (16, 8, 128), 1) < 4
        for part in range(2):
            rows = slice(part * 16, part * 16 + 16)
            rho = rho_ref[rows]
            beta = rho + 1.0 / rho
            back = (1.0 / SMOOTH) / beta

            def tile(n, half):
                cols = slice(half * 128, half * 128 + 128)
                a = spectrum[0, n, :, cols].reshape(16, 8, 128)
                b = spectrum[1, n, :, cols].reshape(16, 8, 128)
                return jnp.where(first, a, b) if part == 0 else jnp.where(first, b, a)

            g = [beta * tile(5 + r // 2, r % 2) for r in range(4)]
            ys = [tile(c, 0) for c in range(5)]
            ks = add_spread(ys, g, 1)
            for c in range(5):
                y = ys[c]
                out[rows, 0, pair, c] = beta * tile(c, 1) + y
                out[rows, 1, pair, c] = ks[c]
                keep[pair, c, rows] = back * y


def solve_kernel(f, rho_ref, out, right, work):
    rho = rho_ref[...]
    sigma = rho * rho
    shape = (2, 5, 8, 128)
    sb = jnp.broadcast_to(sigma, shape)
    powers = [sigma]
    for _ in range(GROUPS - 1):
        powers.append(powers[-1] * sigma)
    closing = jnp.broadcast_to(1.0 / (1.0 - powers[-1]), shape)
    v = u = None
    for s in range(GROUPS):
        r = f[s, 0] + f[(s + 1) % GROUPS, 1]
        right[s] = r
        v = r if s == 0 else r + sb * v
        u = r if s == 0 else u + powers[s - 1] * r
        work[s] = v
    v_last = v * closing
    u = u * closing
    gain = jnp.broadcast_to(sigma / (1.0 - sigma * sigma), shape)
    back = jnp.broadcast_to((1.0 / SMOOTH) / (rho + 1.0 / rho), shape)
    after = last = None
    for s in reversed(range(GROUPS)):
        value = sb * u
        p = gain * ((work[s] + powers[s] * v_last) + value)
        out[s, :, :, 0] = p
        if after is None:
            last = p
        else:
            out[s + 1, :, :, 1] = back * (p + after)
        u = right[s] + value
        after = p
    out[0, :, :, 1] = back * (after + last)


def fold(value):
    return jnp.sum((value * value).reshape(16, 8, 128), axis=0)


def inverse_kernel(*refs, chosen):
    spec, keep, img, ty, tx = refs[:5]
    stack = refs[-1]
    if chosen[0] == 0:
        out = [refs[5]]
        start = None
    else:
        start, second, upper, sums = refs[5:9]
        out = [second, upper.at[0], upper.at[1]]
        sums[...] = jnp.zeros_like(sums)
    first = lax.broadcasted_iota(jnp.int32, (16, 8, 128), 1) < 4

    mixes = ((1, 0.5), (0, -0.25), (4, 0.25), (1, -0.5), (2, -0.25))
    for c in range(5):
        source, weight = mixes[c]
        weight = weight / SMOOTH
        if start is not None:
            last = (start[c, 0], start[c, 1])
        for n, image in enumerate(chosen):
            pair, i = image // 2, image % 2
            p_even, p_odd = spec[0:16, pair, c, 0], spec[16:32, pair, c, 0]
            w_even = spec[0:16, pair, c, 1] + keep[pair, c, 0:16]
            w_odd = spec[16:32, pair, c, 1] + keep[pair, c, 16:32]
            if i == 1:
                p_even, p_odd, w_even, w_odd = p_odd, p_even, w_odd, w_even
            slot = (c * len(chosen) + n) % SLOTS
            push(stack, slot, 0, jnp.where(first, w_even, w_odd).reshape(128, 128))
            push(stack, slot, 1, jnp.where(first, p_even, p_odd).reshape(128, 128))
            both = jnp.dot(tx[i], stack[slot], preferred_element_type=F32)
            even = KEEP * img[image, c, 0] + times_right(both[:, :128], ty[...])
            odd = times_right(both[:, 128:], ty[...])
            mix = img[image, source, 1]
            if c == 1:
                mix = mix - img[image, 3, 1]
            odd = KEEP * img[image, c, 1] + odd * (1.0 / SMOOTH) + weight * mix
            out[n][c, 0] = even
            out[n][c, 1] = odd
            if start is not None:
                sums[n] += fold(even - last[0]) + fold(odd - last[1])
                last = (even, odd)


def edge_kernel(sums, upper, above, out):
    edge = jnp.zeros((8, 128), F32)
    for c in range(5):
        for zz in range(2):
            edge = edge + fold(above[c, zz] - upper[1, c, zz])
    rows = [sums[0], sums[1], sums[2], edge]
    index = lax.broadcasted_iota(jnp.int32, (1, 128), 1)
    total = jnp.zeros((1, 128), F32)
    for g, row in enumerate(rows):
        total = jnp.where(index == g, jnp.sum(row), total)
    out[...] = jnp.broadcast_to(total, (128, 1, 128))


def final_kernel(
    centre,
    positions,
    where,
    sums,
    below_hbm,
    s0,
    s1,
    upper,
    a0,
    a1_hbm,
    out_hbm,
    below,
    a1,
    out,
    below_sem,
    a1_sem,
    out_sem,
):
    def fetch_below(c):
        return pltpu.make_async_copy(below_hbm.at[:, c], below.at[c], below_sem.at[c])

    def fetch_a1(c):
        return pltpu.make_async_copy(a1_hbm.at[c], a1.at[c], a1_sem.at[c])

    def store(c, zz):
        return pltpu.make_async_copy(out.at[c, zz], out_hbm.at[:, c, zz], out_sem.at[c, zz])

    for c in range(5):
        fetch_below(c).start()
        fetch_a1(c).start()
    arc = [jnp.zeros((8, 128), F32)]
    lane = lax.broadcasted_iota(jnp.int32, (1, 128), 1)
    for k in range(LOCAL):
        block = jnp.sum(sums[k * GROUPS : (k + 1) * GROUPS], axis=0)
        dist = jnp.sqrt(block * (1.0 / CELLS) + EPS)
        for g in range(4):
            if k * 4 + g < IMAGES - 1:
                value = jnp.sum(jnp.where(lane == g, dist, 0.0), axis=1, keepdims=True)
                arc.append(arc[-1] + jnp.broadcast_to(value, (8, 128)))
    base = where[0] * LOCAL - 2
    weights = {}
    for m in range(LOCAL):
        c = centre[m]
        tau = positions[m] * arc[-1]

        def pick(index):
            value = arc[0]
            for j in range(1, IMAGES):
                value = jnp.where(index == j, arc[j], value)
            return value

        a, b, d = pick(c - 1), pick(c), pick(c + 1)
        w = (
            (tau - b) * (tau - d) / ((a - b) * (a - d)),
            (tau - a) * (tau - d) / ((b - a) * (b - d)),
            (tau - a) * (tau - b) / ((d - a) * (d - b)),
        )
        for r in range(5):
            spot = base + m + r
            value = jnp.zeros((8, 128), F32)
            for n in range(3):
                value = jnp.where(c - 1 + n == spot, w[n], value)
            weights[m, r] = value

    for c in range(5):
        fetch_below(c).wait()
        fetch_a1(c).wait()
    for c in range(5):
        lines = [below.at[c, 0], below.at[c, 1], s0.at[c], s1.at[c]]
        lines += [upper.at[0, c], upper.at[1, c], a0.at[c], a1.at[c]]
        for zz in range(2):
            for n in range(16):
                rows = slice(8 * n, 8 * n + 8)
                pieces = [line[zz, rows] for line in lines]
                for m in range(LOCAL):
                    acc = pieces[m] * weights[m, 0]
                    for r in range(1, 5):
                        acc = acc + pieces[m + r] * weights[m, r]
                    out[c, zz, m, rows] = acc
            store(c, zz).start()
    for c in range(5):
        for zz in range(2):
            store(c, zz).wait()


SMEM = pl.BlockSpec(memory_space=pltpu.SMEM)
VMEM = pl.BlockSpec(memory_space=pltpu.VMEM)
HBM = pl.BlockSpec(memory_space=pltpu.HBM)


def plain(mib):
    return pltpu.CompilerParams(vmem_limit_bytes=mib * 1024 * 1024)


def cost(flops, moved):
    return pl.CostEstimate(flops=flops, bytes_accessed=moved, transcendentals=0)


def forward(images, ty, tx, rho):
    where = lax.axis_index("gz").astype(jnp.int32).reshape(1)
    return pl.pallas_call(
        forward_kernel,
        out_shape=(
            pltpu.VMEM((GROUPS, 2, 2, 5, 8, 128), F32),
            pltpu.VMEM((2, 5, GROUPS, 8, 128), F32),
            pltpu.VMEM((8, 128), F32),
        ),
        in_specs=[SMEM, HBM, HBM, HBM, HBM],
        out_specs=(VMEM,) * 3,
        scratch_shapes=[
            pltpu.VMEM((LOCAL, 5, 2, 128, 128), F32),
            pltpu.SemaphoreType.DMA((LOCAL,)),
            pltpu.VMEM((256, 256), BF16),
            pltpu.VMEM((2, 128, 384), BF16),
            pltpu.VMEM((GROUPS, 8, 128), F32),
            pltpu.SemaphoreType.DMA((3,)),
            pltpu.VMEM((7, 384, 256), BF16),
            pltpu.VMEM((2, 7, 128, 256), F32),
        ],
        compiler_params=plain(FORWARD_MIB),
        cost_estimate=cost(3_000_000_000, 9_000_000),
        name="forward",
    )(where, images, ty, tx, rho)


def solve(f, rho):
    return pl.pallas_call(
        solve_kernel,
        out_shape=pltpu.VMEM((GROUPS, 2, 5, 2, 8, 128), F32),
        in_specs=[VMEM, VMEM],
        out_specs=VMEM,
        scratch_shapes=[
            pltpu.VMEM((GROUPS, 2, 5, 8, 128), F32),
            pltpu.VMEM((GROUPS, 2, 5, 8, 128), F32),
        ],
        compiler_params=plain(SOLVE_MIB),
        cost_estimate=cost(20_000_000, 6_000_000),
        name="solve",
    )(f, rho)


def inverse(chosen, spec, keep, images, ty, tx, *start):
    one = pltpu.VMEM((5, 2, 128, 128), F32)
    if start:
        out_shape = (one, pltpu.VMEM((2, 5, 2, 128, 128), F32), pltpu.VMEM((3, 8, 128), F32))
    else:
        out_shape = (one,)
    args = (spec, keep, images, ty, tx, *start)
    count = len(chosen)
    return pl.pallas_call(
        functools.partial(inverse_kernel, chosen=chosen),
        out_shape=out_shape,
        in_specs=[VMEM] * len(args),
        out_specs=(VMEM,) * len(out_shape),
        scratch_shapes=[pltpu.VMEM((SLOTS, 384, 256), BF16)],
        compiler_params=plain(INVERSE_MIB),
        cost_estimate=cost(1_000_000_000 * count, 3_000_000 * count),
        name="inverse",
    )(*args)


def edge(sums, upper, above):
    return pl.pallas_call(
        edge_kernel,
        out_shape=pltpu.VMEM((128, 1, 128), F32),
        in_specs=[VMEM] * 3,
        out_specs=VMEM,
        compiler_params=plain(EDGE_MIB),
        cost_estimate=cost(2_000_000, 1_300_000),
        name="edge",
    )(sums, upper, above)


def final(centre, positions, sums, below, s0, s1, upper, a0, a1):
    where = lax.axis_index("img").astype(jnp.int32).reshape(1)
    return pl.pallas_call(
        final_kernel,
        out_shape=jax.ShapeDtypeStruct((4, 5, 2, 128, 128), F32),
        in_specs=[SMEM, SMEM, SMEM, VMEM, HBM, VMEM, VMEM, VMEM, VMEM, HBM],
        out_specs=HBM,
        scratch_shapes=[
            pltpu.VMEM((5, 2, 2, 128, 128), F32),
            pltpu.VMEM((5, 2, 128, 128), F32),
            pltpu.VMEM((5, 2, 4, 128, 128), F32),
            pltpu.SemaphoreType.DMA((5,)),
            pltpu.SemaphoreType.DMA((5,)),
            pltpu.SemaphoreType.DMA((5, 2)),
        ],
        compiler_params=plain(FINAL_MIB),
        cost_estimate=cost(30_000_000, 8_000_000),
        name="final",
    )(centre, positions, where, sums, below, s0, s1, upper, a0, a1)


def local(images, centre, positions):
    forward_y, inverse_y, forward_x, inverse_x, rho = (jnp.asarray(t) for t in tables())
    rows = [(i, i + 1) for i in range(LOCAL - 1)]
    rows_back = [(b, a) for a, b in rows]
    f, keep, mine = forward(images, forward_y, forward_x, rho)
    f = lax.all_to_all(f, "gz", 0, 0, tiled=True)
    u = solve(f, mine)
    u = lax.all_to_all(u, "gz", 0, 0, tiled=True)
    (s0,) = inverse((0,), u, keep, images, inverse_y, inverse_x)
    a0 = lax.ppermute(s0, "img", rows_back)
    s1, upper, sums = inverse((1, 2, 3), u, keep, images, inverse_y, inverse_x, s0)
    a1 = lax.ppermute(s1, "img", rows_back)
    below = lax.ppermute(upper, "img", rows)
    part = edge(sums, upper, a0)
    sums = lax.all_to_all(part, ("img", "gz"), 0, 0, tiled=True)
    return final(centre, positions, sums, below, s0, s1, upper, a0, a1)


def solution(mesh):
    in_specs = (P("img", None, "gz", None, None), P("img"), P("img"))
    out_specs = P("img", None, "gz", None, None)
    return jax.shard_map(
        local, mesh=mesh, in_specs=in_specs, out_specs=out_specs, check_vma=False
    )
```
